32 devices in a mesh: rows: 8 (over z, x), grp: 4 (over y, core).
Axes of the slice: x: 2, y: 2, z: 4, core: 2. Of those that a mesh axis runs over, the one named last changes fastest.
Arguments:
- layer_input: bfloat16 [128, 768, 512], P('rows', 'grp'), may hold values from -6 to 6
- segment_ids: int32 [128, 512], P('rows'), may hold values from 0 to 3, never falling along the last dimension, each value on 1 to 256 neighbouring positions
- qkv_weight: bfloat16 [4, 192, 576], P('grp'), may hold values from -0.4375 to 0.4375
- qv_bias: float32 [4, 384], P('grp'), may hold values from -4 to 4
- out_weight: bfloat16 [768, 768], replicated, may hold values from -0.875 to 0.875
- out_bias: float32 [768], replicated, may hold values from -4 to 4
- gain_one: float32 [768], replicated, may hold values from 0.1 to 1.9
- shift_one: float32 [768], replicated, may hold values from -4 to 4
- up_weight: bfloat16 [4, 192, 768], P('grp'), may hold values from -0.4375 to 0.4375
- up_bias: float32 [4, 768], P('grp'), may hold values from -4 to 4
- down_weight: bfloat16 [4, 192, 768], P('grp'), may hold values from -0.21875 to 0.21875
- down_bias: float32 [4, 192], P('grp'), may hold values from -4 to 4
- gain_two: float32 [768], P('grp'), may hold values from 0.1 to 1.9
- shift_two: float32 [768], P('grp'), may hold values from -4 to 4
- out_grad: bfloat16 [128, 768, 512], P('rows', 'grp'), may hold values from -6 to 6
Outputs:
- layer_output: float32 [128, 768, 512], P('rows', 'grp')
- input_grad: float32 [128, 768, 512], P('rows', 'grp')
- qkv_weight_grad: float32 [4, 192, 576], P('grp')
- qv_bias_grad: float32 [4, 384], P('grp')
- out_weight_grad: float32 [768, 768], replicated
- out_bias_grad: float32 [768], replicated
- gain_one_grad: float32 [768], replicated
- shift_one_grad: float32 [768], replicated
- up_weight_grad: float32 [4, 192, 768], P('grp')
- up_bias_grad: float32 [4, 768], P('grp')
- down_weight_grad: float32 [4, 192, 768], P('grp')
- down_bias_grad: float32 [4, 192], P('grp')
- gain_two_grad: float32 [768], P('grp')
- shift_two_grad: float32 [768], P('grp')
The draws below stay inside these ranges and needn't reach their ends.
Inputs may be any that keep to these rules, and one draw needn't show every extreme that they name: `segment_ids`: in each packed sequence the segment numbers never fall, start at 0, and each segment has 1 to 256 tokens; one segment of each sequence has exactly 256.
All inputs are finite; a program needn't handle non-finite values.
Results may differ from the reference program's by a relative error of at most 0.02.
Values may be sent and summed in bfloat16 or wider, within the bound.
A program may use at most 256 MiB of HBM per device.

```python
import math
import jax
import jax.numpy as jnp
import numpy as np
from jax import lax

D = 768
HEADS = 12
HEAD_DIM = 64
FF = 3072
GROUPS = 4
SEQ_LEN = 512
SEQUENCES = 128


def block_levels(rng, dims, shards, smallest, top_value):
    def one(axis_at, parts):
        heights = jax.random.uniform(jax.random.fold_in(jax.random.fold_in(rng, 6), axis_at), (parts,), jnp.float32, smallest / len(shards), top_value / len(shards))
        return jnp.repeat(jnp.exp(heights), dims[axis_at] // parts).reshape((-1,) + (1,) * (len(dims) - axis_at - 1))

    level = one(*shards[0])
    for cut in shards[1:]:
        level = level * one(*cut)
    return level


def split_up(count, total, reach, slope):
    loads = [(1 << 20) // math.isqrt(standing ** slope) + 1 for standing in range(2, count + 1)]
    surplus, given = total - reach - (count - 1), [1] * (count - 1)
    while surplus > 0:
        free = [i for i in range(count - 1) if given[i] < reach]
        pool, budget = sum([loads[i] for i in free]), surplus
        for i in free:
            more = min(reach - given[i], max(1, budget * loads[i] // pool), surplus)
            given[i] = given[i] + more
            surplus = surplus - more
    return np.array([reach] + given)


def ragged(stream_key, count, total, limit, skew):
    if count == 2:
        one = jax.random.randint(stream_key, (), max(1, total - limit), min(limit, total - 1) + 1)
        return jnp.stack([one, total - one])
    tallies = jnp.asarray(split_up(count, total, limit, skew), jnp.int32)
    twos = (count - 1) // 2
    donor, taker = tallies[1:1 + 2 * twos:2], tallies[2:2 + 2 * twos:2]
    room = jnp.minimum(donor - 1, limit - taker)
    passed = jax.random.randint(jax.random.fold_in(stream_key, 1), (twos,), 0, 1 << 20) % (room + 1)
    tallies = tallies.at[1:1 + 2 * twos:2].set(donor - passed).at[2:2 + 2 * twos:2].set(taker + passed)
    return tallies[jax.random.permutation(jax.random.fold_in(stream_key, 2), count)]


def bell_draw(own_key, extent, scale, limit, pieces=(), dtype=jnp.bfloat16):
    level = block_levels(own_key, extent, pieces, -0.22, 0.18) if pieces else 1.0
    drawn = jax.random.normal(own_key, extent, jnp.float32) * scale * level
    return jnp.minimum(jnp.maximum(drawn, -limit), limit).astype(dtype)


def setup_inputs(seed: int = 0) -> dict:
    key_of = jax.random.split(jax.random.key(seed), 16)
    layer_input = bell_draw(key_of[0], (SEQUENCES, D, SEQ_LEN), 1.0, 6.0, ((0, 8), (1, 4)))
    segment_ids = jax.vmap(lambda own: jnp.searchsorted(jnp.cumsum(ragged(own, 4, SEQ_LEN, SEQ_LEN // 2, 0)), jnp.arange(SEQ_LEN), side="right"))(jax.random.split(key_of[1], SEQUENCES)).reshape((SEQUENCES, SEQ_LEN)).astype(jnp.int32)
    qkv_weight = bell_draw(key_of[2], (GROUPS, D // GROUPS, 3 * (D // GROUPS)), (D // GROUPS) ** -0.5, 0.4375, ((0, 4),))
    qv_bias = bell_draw(key_of[3], (GROUPS, 2 * (D // GROUPS)), 0.3, 4.0, ((0, 4),), jnp.float32)
    out_weight = bell_draw(key_of[4], (D, D), (D // 16) ** -0.5, 0.875)
    out_bias = bell_draw(key_of[5], (D,), 0.3, 4.0, (), jnp.float32)
    gain_one = jnp.clip(1.0 + 0.18 * jax.random.normal(key_of[6], (D,), jnp.float32), 0.1, 1.9)
    shift_one = bell_draw(key_of[7], (D,), 0.3, 4.0, (), jnp.float32)
    up_weight = bell_draw(key_of[8], (GROUPS, D // GROUPS, FF // GROUPS), (D // GROUPS) ** -0.5, 0.4375, ((0, 4),))
    up_bias = bell_draw(key_of[9], (GROUPS, FF // GROUPS), 0.3, 4.0, ((0, 4),), jnp.float32)
    down_weight = bell_draw(key_of[10], (GROUPS, D // GROUPS, FF // GROUPS), (FF // GROUPS) ** -0.5, 0.21875, ((0, 4),))
    down_bias = bell_draw(key_of[11], (GROUPS, D // GROUPS), 0.3, 4.0, ((0, 4),), jnp.float32)
    gain_two = jnp.clip(1.0 + 0.18 * jax.random.normal(key_of[12], (D,), jnp.float32), 0.1, 1.9)
    shift_two = bell_draw(key_of[13], (D,), 0.3, 4.0, ((0, 4),), jnp.float32)
    out_grad = bell_draw(key_of[14], (SEQUENCES, D, SEQ_LEN), 1.0, 6.0, ((0, 8), (1, 4)))
    return {"layer_input": layer_input, "segment_ids": segment_ids, "qkv_weight": qkv_weight, "qv_bias": qv_bias, "out_weight": out_weight, "out_bias": out_bias, "gain_one": gain_one, "shift_one": shift_one, "up_weight": up_weight, "up_bias": up_bias, "down_weight": down_weight, "down_bias": down_bias, "gain_two": gain_two, "shift_two": shift_two, "out_grad": out_grad}


@jax.custom_vjp
def low(v):
    return lax.optimization_barrier(v.astype(jnp.bfloat16)).astype(jnp.float32)

@jax.custom_vjp
def low_back(v):
    return v

def low_keep(v):
    return (low(v), None)

def low_pass(kept, grad):
    return (grad,)

def back_keep(v):
    return (v, None)

def back_low(kept, grad):
    return (low(grad),)
low.defvjp(low_keep, low_pass)
low_back.defvjp(back_keep, back_low)
epsilon = 1e-05
masked = -1e+30

def highest(form, left_side, right_side):
    return jnp.einsum(form, left_side, right_side, precision=lax.Precision.HIGHEST)

def normalize(summed, gain, shift):
    center = lax.optimization_barrier(jnp.mean(summed, axis=-1, keepdims=True))
    offsets = summed - center
    spread = lax.optimization_barrier(jnp.mean(offsets * offsets, axis=-1, keepdims=True))
    return offsets * lax.rsqrt(spread + epsilon) * gain + shift

def forward_layer(params, inputs, labels):
    qkv_weight, qv_bias, out_weight, out_bias, gain_one, shift_one, up_weight, up_bias, down_weight, down_bias, gain_two, shift_two = params
    token_count = inputs.shape[0]
    seq_count = labels.shape[0]
    group_width = D // GROUPS
    grouped = inputs.reshape(token_count, GROUPS, group_width)
    projected = highest('ngc,gce->nge', grouped, qkv_weight)
    queries = low_back(low(projected[:, :, :group_width] + qv_bias[None, :, :group_width]))
    keys = low_back(low(projected[:, :, group_width:2 * group_width]))
    values = low_back(low(projected[:, :, 2 * group_width:] + qv_bias[None, :, group_width:]))
    shape_heads = (seq_count, SEQ_LEN, HEADS, HEAD_DIM)
    scores = highest('bqhd,bkhd->bhqk', queries.reshape(shape_heads), keys.reshape(shape_heads)) * HEAD_DIM ** (-0.5)
    scores = low_back(scores)
    same_doc = (labels[:, :, None] == labels[:, None, :])[:, None]
    scores = jnp.where(same_doc, scores, masked)
    largest = lax.optimization_barrier(jnp.max(scores, axis=-1, keepdims=True))
    weights = jnp.exp(scores - largest)
    probability = low(weights / lax.optimization_barrier(jnp.sum(weights, axis=-1, keepdims=True)))
    context = highest('bhqk,bkhd->bqhd', probability, values.reshape(shape_heads)).reshape(token_count, D)
    context = low_back(low(context))
    branch = low(highest('nc,ce->ne', context, out_weight) + out_bias)
    summed = low_back(branch + inputs)
    hidden = low_back(low(normalize(summed, gain_one, shift_one)))
    up_value = highest('ngc,gcf->ngf', hidden.reshape(token_count, GROUPS, group_width), up_weight) + up_bias[None]
    up_value = low_back(up_value)
    activated = low(jax.nn.gelu(up_value, approximate=False))
    down_value = highest('ngf,gcf->ngc', activated, down_weight) + down_bias[None]
    summed_two = low_back(hidden + down_value.reshape(token_count, D))
    return normalize(summed_two, gain_two, shift_two)

def reference(layer_input, segment_ids, qkv_weight, qv_bias, out_weight, out_bias, gain_one, shift_one, up_weight, up_bias, down_weight, down_bias, gain_two, shift_two, out_grad):
    params = tuple((item.astype(jnp.float32) for item in (qkv_weight, qv_bias, out_weight, out_bias, gain_one, shift_one, up_weight, up_bias, down_weight, down_bias, gain_two, shift_two)))
    seq_total = segment_ids.shape[0]
    per_step = math.gcd(seq_total, max(1, 4096 // SEQ_LEN))
    step_count = seq_total // per_step
    inputs = jnp.transpose(layer_input.astype(jnp.float32), (0, 2, 1)).reshape(step_count, per_step * SEQ_LEN, D)
    cotangents = jnp.transpose(out_grad.astype(jnp.float32), (0, 2, 1)).reshape(step_count, per_step * SEQ_LEN, D)
    labels = segment_ids.reshape(step_count, per_step, SEQ_LEN)

    def one_step(totals, block_data):
        block_input, block_labels, block_grad = block_data

        def apply_layer(weights, values):
            return forward_layer(weights, values, block_labels)
        result, pullback = jax.vjp(apply_layer, params, block_input)
        weight_grads, input_part = pullback(block_grad)
        totals = jax.tree.map(lambda first_term, second_term: first_term + second_term, totals, weight_grads)
        return (totals, (result, input_part))
    initial = jax.tree.map(jnp.zeros_like, params)
    totals, (results, input_parts) = lax.scan(one_step, initial, (inputs, labels, cotangents))
    results = jnp.transpose(results.reshape(seq_total, SEQ_LEN, D), (0, 2, 1))
    input_parts = jnp.transpose(input_parts.reshape(seq_total, SEQ_LEN, D), (0, 2, 1))
    return (results, input_parts, totals[0], totals[1], totals[2], totals[3], totals[4], totals[5], totals[6], totals[7], totals[8], totals[9], totals[10], totals[11])
```

```python
import jax
import jax.numpy as jnp
from jax import lax
from jax.experimental import pallas as pl
from jax.experimental.pallas import tpu as pltpu
from jax.sharding import PartitionSpec as P

D = 768
HEAD_DIM = 64
SEQ_LEN = 512
GROUPS = 4
WIDTH = D // GROUPS
HEADS_GROUP = WIDTH // HEAD_DIM
HEADS = D // HEAD_DIM
QKV = 3 * WIDTH
UNITS = 768
PAD = HEAD_DIM + 16
MASKED = -1e30
EPS = 1e-05
UNROLL = 4
SCALE = HEAD_DIM ** (-0.5)

F32 = jnp.float32
BF16 = jnp.bfloat16

Q_BIAS, V_BIAS, UP_BIAS, DOWN_BIAS, GAIN_TWO, SHIFT_TWO = 0, 1, 2, 6, 7, 8
GROUP_COLS = 9
OUT_BIAS, GAIN_ONE, SHIFT_ONE = GROUPS * GROUP_COLS, GROUPS * GROUP_COLS + GROUPS, GROUPS * GROUP_COLS + 2 * GROUPS
COLS = GROUPS * GROUP_COLS + 3 * GROUPS


def nn(a, b):
    return lax.dot_general(a, b, (((1,), (0,)), ((), ())), preferred_element_type=F32)


def nt(a, b):
    return lax.dot_general(a, b, (((1,), (1,)), ((), ())), preferred_element_type=F32)


def tn(a, b):
    return lax.dot_general(a, b, (((0,), (0,)), ((), ())), preferred_element_type=F32)


def lane_part(value):
    total = value[:, 0:128]
    for at in range(128, SEQ_LEN, 128):
        total = total + value[:, at : at + 128]
    return total


def channel_sum(value):
    return jnp.sum(value, axis=0, keepdims=True)


def fold(value):
    return jnp.sum(value.reshape(value.shape[0] // 8, 8, SEQ_LEN), axis=0)


def spread(column):
    return jnp.concatenate([column] * (SEQ_LEN // 128), axis=1)


def gelu_pair(u):
    half_erf = 0.5 * lax.erf(u * 0.7071067811865476) + 0.5
    density = jnp.exp(u * u * -0.5) * 0.3989422804014327
    return u * half_erf, half_erf + u * density


def layer_kernel(
    x, dy, seg, wqkv, wup, wdown, wout, params,
    lo, dx, g_qkv, g_up, g_down, g_out, g_vec,
    wqkv_t, wup_t, wdown_t, wout_t, cols, vec,
    q_s, k_s, v_s, e_s, linv_s, ctx_s, summed_s, hidden_s, act_s, slope_s, summed2_s, grad2_s,
    up_grad_s, hidden_grad_s, summed_grad_s, ctx_grad_s, qkv_grad_s,
):
    step = pl.program_id(0)
    zero = jnp.zeros((8, SEQ_LEN), F32)

    @pl.when(step == 0)
    def _():
        def turn(g, carry):
            wqkv_t[g] = wqkv[g].T
            wup_t[g] = wup[g].T
            wdown_t[g] = wdown[g].T
            return carry

        lax.fori_loop(0, GROUPS, turn, 0)
        wout_t[...] = wout[...].T
        table = params[...].T
        for at in range(COLS):
            cols[at] = jnp.broadcast_to(table[:, at : at + 1], (WIDTH, 128))
        g_qkv[...] = jnp.zeros_like(g_qkv)
        g_up[...] = jnp.zeros_like(g_up)
        g_down[...] = jnp.zeros_like(g_down)
        g_out[...] = jnp.zeros_like(g_out)
        vec[...] = jnp.zeros_like(vec)

    def col(at):
        return spread(cols[at])

    def over_groups(body, init=0):
        return lax.fori_loop(0, GROUPS, body, init)

    def rows_of(g):
        return pl.ds(pl.multiple_of(g * WIDTH, WIDTH), WIDTH)

    label = seg[0:1, :]
    ids = lax.broadcasted_iota(jnp.int32, (16, SEQ_LEN), 0)
    hot = (ids == label).astype(F32)
    hot_k = hot.astype(BF16)
    hot_q = jnp.where(ids < 4, (1.0 - hot) * MASKED, 0.0).astype(BF16)

    def project(g, carry):
        xg = x[g]
        base = g * GROUP_COLS
        q = (nn(wqkv_t[g, 0:WIDTH, :], xg) + col(base + Q_BIAS)).astype(BF16) * jnp.asarray(SCALE, BF16)
        k = nn(wqkv_t[g, WIDTH : 2 * WIDTH, :], xg).astype(BF16)
        v = (nn(wqkv_t[g, 2 * WIDTH :, :], xg) + col(base + V_BIAS)).astype(BF16)
        for h in range(HEADS_GROUP):
            at = g * HEADS_GROUP + h
            q_s[at, 0:HEAD_DIM, :] = q[h * HEAD_DIM : (h + 1) * HEAD_DIM]
            k_s[at, 0:HEAD_DIM, :] = k[h * HEAD_DIM : (h + 1) * HEAD_DIM]
            v_s[at] = v[h * HEAD_DIM : (h + 1) * HEAD_DIM]
            q_s[at, HEAD_DIM:PAD, :] = hot_q
            k_s[at, HEAD_DIM:PAD, :] = hot_k
        return carry

    over_groups(project)

    def attend(h, carry):
        scores = tn(k_s[h], q_s[h])
        largest = jnp.max(scores, axis=0, keepdims=True)
        weights = jnp.exp(scores - largest)
        inverse = 1.0 / channel_sum(weights)
        e = weights.astype(BF16)
        e_s[h] = e
        linv_s[h] = inverse
        ctx_s[h] = (nn(v_s[h], e) * inverse).astype(BF16)
        return carry

    lax.fori_loop(0, HEADS, attend, 0, unroll=UNROLL)

    def mix(g, carry):
        total, square = carry
        ctx = ctx_s[...].reshape(D, SEQ_LEN)
        branch = (nn(wout_t[rows_of(g), :], ctx) + col(OUT_BIAS + g)).astype(BF16)
        summed = branch.astype(F32) + x[g].astype(F32)
        summed_s[g] = summed
        return total + fold(summed), square + fold(summed * summed)

    total, square = over_groups(mix, (zero, zero))
    center1 = channel_sum(total) / D
    inverse1 = lax.rsqrt(channel_sum(square) / D - center1 * center1 + EPS)

    def feed(g, carry):
        total, square = carry
        base = g * GROUP_COLS
        normed = (summed_s[g] - center1) * inverse1
        hidden = (normed * col(GAIN_ONE + g) + col(SHIFT_ONE + g)).astype(BF16)
        hidden_s[g] = hidden
        for part in range(UNITS // WIDTH):
            rows = slice(part * WIDTH, (part + 1) * WIDTH)
            u = nn(wup_t[g, rows, :], hidden) + col(base + UP_BIAS + part)
            act, slope = gelu_pair(u)
            act_s[g, rows, :] = act.astype(BF16)
            slope_s[g, rows, :] = slope.astype(BF16)
        summed2 = hidden.astype(F32) + nn(wdown[g], act_s[g]) + col(base + DOWN_BIAS)
        summed2_s[g] = summed2
        return total + fold(summed2), square + fold(summed2 * summed2)

    total, square = over_groups(feed, (zero, zero))
    center2 = channel_sum(total) / D
    inverse2 = lax.rsqrt(channel_sum(square) / D - center2 * center2 + EPS)

    def finish(g, carry):
        sum_e, sum_en = carry
        base = g * GROUP_COLS
        normed = (summed2_s[g] - center2) * inverse2
        gain = col(base + GAIN_TWO)
        lo[g] = (normed * gain + col(base + SHIFT_TWO)).astype(BF16)
        grad = dy[g].astype(F32)
        product = grad * normed
        vec[base + GAIN_TWO] += lane_part(product)
        vec[base + SHIFT_TWO] += lane_part(grad)
        summed2_s[g] = normed
        return sum_e + fold(grad * gain), sum_en + fold(product * gain)

    sum_e, sum_en = over_groups(finish, (zero, zero))
    mean_e = channel_sum(sum_e) / D
    mean_en = channel_sum(sum_en) / D

    def feed_back(g, carry):
        sum_h, sum_hn = carry
        base = g * GROUP_COLS
        normed2 = summed2_s[g]
        scaled = dy[g].astype(F32) * col(base + GAIN_TWO)
        grad2 = (inverse2 * (scaled - mean_e - normed2 * mean_en)).astype(BF16)
        wide = grad2.astype(F32)
        vec[base + DOWN_BIAS] += lane_part(wide)
        for part in range(UNITS // WIDTH):
            rows = slice(part * WIDTH, (part + 1) * WIDTH)
            up_grad = (nn(wdown_t[g, rows, :], grad2) * slope_s[g, rows, :].astype(F32)).astype(BF16)
            up_grad_s[rows, :] = up_grad
            vec[base + UP_BIAS + part] += lane_part(up_grad.astype(F32))
        g_up[g] += nt(hidden_s[g], up_grad_s[...])
        g_down[g] += nt(grad2, act_s[g])
        hidden_grad = (wide + nn(wup[g], up_grad_s[...])).astype(BF16)
        hidden_grad_s[g] = hidden_grad
        grad1 = hidden_grad.astype(F32)
        normed1 = (summed_s[g] - center1) * inverse1
        product = grad1 * normed1
        gain = col(GAIN_ONE + g)
        vec[GAIN_ONE + g] += lane_part(product)
        vec[SHIFT_ONE + g] += lane_part(grad1)
        return sum_h + fold(grad1 * gain), sum_hn + fold(product * gain)

    sum_h, sum_hn = over_groups(feed_back, (zero, zero))
    mean_h = channel_sum(sum_h) / D
    mean_hn = channel_sum(sum_hn) / D

    def norm_back(g, carry):
        normed1 = (summed_s[g] - center1) * inverse1
        scaled = hidden_grad_s[g].astype(F32) * col(GAIN_ONE + g)
        summed_grad = (inverse1 * (scaled - mean_h - normed1 * mean_hn)).astype(BF16)
        summed_grad_s[rows_of(g), :] = summed_grad
        vec[OUT_BIAS + g] += lane_part(summed_grad.astype(F32))
        return carry

    over_groups(norm_back)

    def mix_back(g, carry):
        summed_grad = summed_grad_s[...]
        ctx = ctx_s[pl.ds(g * HEADS_GROUP, HEADS_GROUP)].reshape(WIDTH, SEQ_LEN)
        g_out[rows_of(g), :] += nt(ctx, summed_grad)
        ctx_grad = nn(wout[rows_of(g), :], summed_grad).astype(BF16)
        for h in range(HEADS_GROUP):
            ctx_grad_s[g * HEADS_GROUP + h] = ctx_grad[h * HEAD_DIM : (h + 1) * HEAD_DIM]
        return carry

    over_groups(mix_back)

    def attend_back(h, carry):
        e = e_s[h]
        grad = (ctx_grad_s[h].astype(F32) * linv_s[h]).astype(BF16)
        middle = channel_sum(grad.astype(F32) * ctx_s[h].astype(F32))
        q = q_s[h, 0:HEAD_DIM, :]
        k = k_s[h, 0:HEAD_DIM, :]
        value_grad = nt(grad, e)
        prob_grad = tn(v_s[h], grad)
        score_grad = (e.astype(F32) * (prob_grad - middle)).astype(BF16)
        qkv_grad_s[0, h] = (nn(k, score_grad) * SCALE).astype(BF16)
        qkv_grad_s[1, h] = nt(q, score_grad).astype(BF16)
        qkv_grad_s[2, h] = value_grad.astype(BF16)
        return carry

    lax.fori_loop(0, HEADS, attend_back, 0, unroll=UNROLL)

    def project_back(g, carry):
        base = g * GROUP_COLS
        xg = x[g]
        into = summed_grad_s[rows_of(g), :].astype(F32)
        for part in range(3):
            grads = qkv_grad_s[part, pl.ds(g * HEADS_GROUP, HEADS_GROUP)].reshape(WIDTH, SEQ_LEN)
            columns = slice(part * WIDTH, (part + 1) * WIDTH)
            g_qkv[g, columns, :] += nt(grads, xg)
            into = into + nn(wqkv[g, :, columns], grads)
            if part != 1:
                vec[base + (Q_BIAS if part == 0 else V_BIAS)] += lane_part(grads.astype(F32))
        dx[g] = into.astype(BF16)
        return carry

    over_groups(project_back)

    @pl.when(step == pl.num_programs(0) - 1)
    def _():
        def close(at, carry):
            g_vec[at] = jnp.sum(vec[at].T, axis=0, keepdims=True)
            return carry

        lax.fori_loop(0, COLS, close, 0)


def layer(x, dy, seg, wqkv, wup, wdown, wout, params):
    count = x.shape[1]
    data = pl.BlockSpec((GROUPS, None, WIDTH, SEQ_LEN), lambda i: (0, i, 0, 0))

    def whole(shape):
        return pl.BlockSpec(shape, lambda i: (0,) * len(shape), pipeline_mode=pl.Buffered(1))

    grads = [
        (GROUPS, QKV, WIDTH),
        (GROUPS, WIDTH, UNITS),
        (GROUPS, WIDTH, UNITS),
        (D, D),
        (COLS, 1, WIDTH),
    ]
    token = (GROUPS, WIDTH, SEQ_LEN)
    return pl.pallas_call(
        layer_kernel,
        grid=(count,),
        out_shape=[jax.ShapeDtypeStruct(x.shape, BF16)] * 2 + [jax.ShapeDtypeStruct(s, F32) for s in grads],
        in_specs=[
            data,
            data,
            pl.BlockSpec((None, 1, SEQ_LEN), lambda i: (i, 0, 0)),
        ]
        + [whole(a.shape) for a in (wqkv, wup, wdown, wout, params)],
        out_specs=[data, data] + [whole(s) for s in grads],
        scratch_shapes=[
            pltpu.VMEM((GROUPS, QKV, WIDTH), BF16),
            pltpu.VMEM((GROUPS, UNITS, WIDTH), BF16),
            pltpu.VMEM((GROUPS, UNITS, WIDTH), BF16),
            pltpu.VMEM((D, D), BF16),
            pltpu.VMEM((COLS, WIDTH, 128), F32),
            pltpu.VMEM((COLS, WIDTH, 128), F32),
            pltpu.VMEM((HEADS, PAD, SEQ_LEN), BF16),
            pltpu.VMEM((HEADS, PAD, SEQ_LEN), BF16),
            pltpu.VMEM((HEADS, HEAD_DIM, SEQ_LEN), BF16),
            pltpu.VMEM((HEADS, SEQ_LEN, SEQ_LEN), BF16),
            pltpu.VMEM((HEADS, 1, SEQ_LEN), F32),
            pltpu.VMEM((HEADS, HEAD_DIM, SEQ_LEN), BF16),
            pltpu.VMEM(token, F32),
            pltpu.VMEM(token, BF16),
            pltpu.VMEM((GROUPS, UNITS, SEQ_LEN), BF16),
            pltpu.VMEM((GROUPS, UNITS, SEQ_LEN), BF16),
            pltpu.VMEM(token, F32),
            pltpu.VMEM(token, BF16),
            pltpu.VMEM((UNITS, SEQ_LEN), BF16),
            pltpu.VMEM(token, BF16),
            pltpu.VMEM((D, SEQ_LEN), BF16),
            pltpu.VMEM((HEADS, HEAD_DIM, SEQ_LEN), BF16),
            pltpu.VMEM((3, HEADS, HEAD_DIM, SEQ_LEN), BF16),
        ],
        compiler_params=pltpu.CompilerParams(vmem_limit_bytes=60 << 20),
    )(x, dy, seg, wqkv, wup, wdown, wout, params)


def local(
    layer_input, segment_ids, qkv_weight, qv_bias, out_weight, out_bias, gain_one, shift_one,
    up_weight, up_bias, down_weight, down_bias, gain_two, shift_two, out_grad,
):
    count = layer_input.shape[0] // GROUPS

    def scatter(a):
        a = a.reshape(GROUPS, count, WIDTH, SEQ_LEN)
        return lax.all_to_all(a, "grp", split_axis=0, concat_axis=0, tiled=True)

    own = jnp.concatenate(
        [
            qv_bias.reshape(2, WIDTH),
            up_bias.reshape(UNITS // WIDTH, WIDTH),
            down_bias.reshape(1, WIDTH),
            gain_two.reshape(1, WIDTH),
            shift_two.reshape(1, WIDTH),
        ]
    )
    params = jnp.concatenate(
        [lax.all_gather(own, "grp", axis=0, tiled=True)]
        + [a.reshape(GROUPS, WIDTH) for a in (out_bias, gain_one, shift_one)]
    )
    gather = lambda a: lax.all_gather(a, "grp", axis=0, tiled=True)
    seg = lax.dynamic_slice_in_dim(segment_ids, lax.axis_index("grp") * count, count, 0)
    lo, dx, g_qkv, g_up, g_down, g_out, g_vec = layer(
        scatter(layer_input),
        scatter(out_grad),
        seg[:, None, :],
        gather(qkv_weight),
        gather(up_weight),
        gather(down_weight),
        out_weight,
        params,
    )
    back = lambda a: scatter(a).reshape(layer_input.shape).astype(F32)

    def total(a):
        a = lax.psum_scatter(a, "grp", scatter_dimension=0, tiled=True)
        return lax.psum(a.astype(BF16), "rows").astype(F32)

    g_vec = g_vec[:, 0, :]
    g_vec = lax.psum(g_vec, ("rows", "grp"))
    shared = g_vec[GROUPS * GROUP_COLS :].reshape(3, D)
    mine = lax.dynamic_slice_in_dim(g_vec, lax.axis_index("grp") * GROUP_COLS, GROUP_COLS, 0)
    g_out = lax.psum(g_out, ("rows", "grp"))
    return (
        back(lo),
        back(dx),
        jnp.swapaxes(total(g_qkv), 1, 2),
        mine[Q_BIAS : V_BIAS + 1].reshape(1, 2 * WIDTH),
        g_out,
        shared[0],
        shared[1],
        shared[2],
        total(g_up),
        mine[UP_BIAS:DOWN_BIAS].reshape(1, UNITS),
        total(g_down),
        mine[DOWN_BIAS].reshape(1, WIDTH),
        mine[GAIN_TWO],
        mine[SHIFT_TWO],
    )


def solution(mesh):
    group = P("grp", None, None)
    data = P("rows", "grp", None)
    in_specs = (
        data, P("rows", None), group, P("grp", None), P(), P(), P(), P(),
        group, P("grp", None), group, P("grp", None), P("grp"), P("grp"), data,
    )
    out_specs = (
        data, data, group, P("grp", None), P(), P(), P(), P(),
        group, P("grp", None), group, P("grp", None), P("grp"), P("grp"),
    )
    return jax.shard_map(local, mesh=mesh, in_specs=in_specs, out_specs=out_specs, check_vma=False)
```

```python
import jax
import jax.numpy as jnp
from jax import lax
from jax.experimental import pallas as pl
from jax.experimental.pallas import tpu as pltpu
from jax.sharding import PartitionSpec as P

D = 768
HEAD_DIM = 64
SEQ_LEN = 512
GROUPS = 4
WIDTH = D // GROUPS
HEADS_GROUP = WIDTH // HEAD_DIM
HEADS = D // HEAD_DIM
QKV = 3 * WIDTH
UNITS = 768
PARTS = UNITS // WIDTH
PAD = HEAD_DIM + 16
MASKED = -1e30
EPS = 1e-05
SCALE = HEAD_DIM ** (-0.5)

F32 = jnp.float32
BF16 = jnp.bfloat16
MESH = pl.DeviceIdType.MESH

Q_BIAS, V_BIAS, UP_BIAS, DOWN_BIAS, GAIN_TWO, SHIFT_TWO, OUT_BIAS, GAIN_ONE, SHIFT_ONE = 0, 1, 2, 6, 7, 8, 9, 10, 11
COLS = 12
TABLE = 16

E_AT = 0
Q_AT = HEADS_GROUP * SEQ_LEN
K_AT = Q_AT + HEADS_GROUP * PAD
V_AT = K_AT + HEADS_GROUP * PAD
FWD_ROWS = V_AT + WIDTH
BWD_ROWS = 2 * WIDTH


def nn(a, b):
    return lax.dot_general(a, b, (((1,), (0,)), ((), ())), preferred_element_type=F32)


def nt(a, b):
    return lax.dot_general(a, b, (((1,), (1,)), ((), ())), preferred_element_type=F32)


def tn(a, b):
    return lax.dot_general(a, b, (((0,), (0,)), ((), ())), preferred_element_type=F32)


def lane_part(value):
    total = value[:, 0:128]
    for at in range(128, SEQ_LEN, 128):
        total = total + value[:, at : at + 128]
    return total


def channel_sum(value):
    return jnp.sum(value, axis=0, keepdims=True)


def fold(value):
    return jnp.sum(value.reshape(value.shape[0] // 8, 8, SEQ_LEN), axis=0)


def spread(column):
    return jnp.concatenate([column] * (SEQ_LEN // 128), axis=1)


def gelu_pair(u):
    half_erf = 0.5 * lax.erf(u * 0.7071067811865476) + 0.5
    density = jnp.exp(u * u * -0.5) * 0.3989422804014327
    return u * half_erf, half_erf + u * density


def flip(me, j):
    return (me + j) % 2 + 2 * ((me // 2 + j // 2) % 2)


def layer_kernel(
    x_in, dy_in, seg, wqkv_in, wup_in, wdown_in, wout, params,
    lo_out, dx_out, fwd_st, bwd_st, g_qkv, g_up, g_down, g_out, g_vec,
    x, dy, wqkv, wup, wdown, table, cols, wqkv_t, wup_t, wdown_t, wout_t, vec,
    fwd, bwd, middle_s, linv_s, ctx_s, summed_s, hidden_s, act_s, slope_s, summed2_s,
    up_grad_s, hidden_grad_s, ctx_grad_s, qkv_grad_s, lo_s,
    s_x, r_x, s_dy, r_dy, s_lo, r_lo, s_dx, r_dx, s_w, r_w, s_fwd, s_bwd,
):
    count = x.shape[0]
    me = lax.axis_index("grp")
    zero = jnp.zeros((8, SEQ_LEN), F32)

    def over(n, body, init=0, unroll=False):
        return lax.fori_loop(0, n, body, init, unroll=unroll)

    def each(n, body):
        def run(at, carry):
            body(at)
            return carry

        lax.fori_loop(0, n, run, 0)

    def remote(src, dst, send, recv, to):
        return pltpu.make_async_remote_copy(
            src_ref=src, dst_ref=dst, send_sem=send, recv_sem=recv, device_id={"grp": to}, device_id_type=MESH
        )

    barrier = pltpu.get_barrier_semaphore()
    for j in range(1, GROUPS):
        pl.semaphore_signal(barrier, inc=1, device_id={"grp": flip(me, j)}, device_id_type=MESH)
    pl.semaphore_wait(barrier, GROUPS - 1)

    def move_in(src, dst, send, recv, i, j):
        to = flip(me, j)
        return remote(src.at[to * count + i], dst.at[i, me], send.at[i, j], recv.at[i, j], to)

    def start_in(src, dst, send, recv, i):
        for j in range(1, GROUPS):
            move_in(src, dst, send, recv, i, j).start()

    def own_in(src, dst, send, i):
        return pltpu.make_async_copy(src.at[me * count + i], dst.at[i, me], send.at[i, 0])

    weights = ((params, table), (wqkv_in.at[0], wqkv), (wup_in.at[0], wup), (wdown_in.at[0], wdown))

    def own_weight(k):
        src, dst = weights[k]
        return pltpu.make_async_copy(src, dst.at[me], s_w.at[k, 0])

    def send_weight(k, j):
        src, dst = weights[k]
        if j < 3:
            return remote(src, dst.at[me], s_w.at[k, j], r_w.at[k, j], flip(me, j))
        got = dst.at[flip(me, 2)]
        return remote(got, got, s_w.at[k, 3], r_w.at[k, 3], flip(me, 1))

    def got_weight(k, j):
        src, dst = weights[k]
        block = dst.at[flip(me, j)]
        remote(block, block, s_w.at[k, j], r_w.at[k, j], flip(me, 1)).wait_recv()

    for k in range(2):
        own_weight(k).start()
        send_weight(k, 2).start()
        send_weight(k, 1).start()
    own_in(x_in, x, s_x, 0).start()
    start_in(x_in, x, s_x, r_x, 0)
    for k in range(2, 4):
        own_weight(k).start()
        send_weight(k, 2).start()
        send_weight(k, 1).start()
    own_in(dy_in, dy, s_dy, 0).start()

    def own_rest(i):
        own_in(x_in, x, s_x, i + 1).start()
        own_in(dy_in, dy, s_dy, i + 1).start()

    each(count - 1, own_rest)

    g_qkv[...] = jnp.zeros_like(g_qkv)
    g_up[...] = jnp.zeros_like(g_up)
    g_down[...] = jnp.zeros_like(g_down)
    g_out[...] = jnp.zeros_like(g_out)
    vec[...] = jnp.zeros_like(vec)
    wout_t[...] = wout[...].T

    own_weight(0).wait()
    got_weight(0, 1)
    got_weight(0, 2)
    send_weight(0, 3).start()
    got_weight(0, 3)
    for g in range(GROUPS):
        cols[g, :, 0:TABLE] = table[g].T

    def col(g, at):
        return cols[g, :, at : at + 1]

    def add_sum(g, at, value):
        vec[g * COLS + at] += lane_part(value)

    def rows_of(g):
        return pl.ds(pl.multiple_of(g * WIDTH, WIDTH), WIDTH)

    def fwd_save(slot, i, g):
        return pltpu.make_async_copy(fwd.at[slot], fwd_st.at[i, g], s_fwd.at[slot])

    def bwd_save(slot, i, g):
        return pltpu.make_async_copy(bwd.at[slot], bwd_st.at[i, g], s_bwd.at[slot])

    def fwd_load(slot, i, g):
        return pltpu.make_async_copy(fwd_st.at[i, g], fwd.at[slot], s_fwd.at[slot])

    def bwd_load(slot, i, g):
        return pltpu.make_async_copy(bwd_st.at[i, g], bwd.at[slot], s_bwd.at[slot])

    def send_lo(i, j):
        to = flip(me, j)
        return remote(lo_s.at[to], lo_out.at[me * count + i], s_lo.at[i, j], r_lo.at[i, j], to)

    def own_lo(i):
        return pltpu.make_async_copy(lo_s.at[me], lo_out.at[me * count + i], s_lo.at[i, 0])

    def sequence(i):
        first = i == 0
        label = seg[pl.ds(me * count + i, 1), :]
        ids = lax.broadcasted_iota(jnp.int32, (16, SEQ_LEN), 0)
        hot = (ids == label).astype(F32)
        hot_k = hot.astype(BF16)
        hot_q = jnp.where(ids < 4, (1.0 - hot) * MASKED, 0.0).astype(BF16)

        def attend(j):
            g = flip(me, j)
            slot = j % 2

            @pl.when(j == 0)
            def _():
                own_in(x_in, x, s_x, i).wait()

            @pl.when(j > 0)
            def _():
                block = x.at[i, g]
                remote(block, block, s_x.at[i, j], r_x.at[i, j], g).wait_recv()

            @pl.when(first & (j == 0))
            def _():
                own_weight(1).wait()

            @pl.when(first & (j == 1))
            def _():
                got_weight(1, 1)

            @pl.when(first & (j == 2))
            def _():
                got_weight(1, 2)
                send_weight(1, 3).start()

            @pl.when(first & (j == 3))
            def _():
                got_weight(1, 3)

            @pl.when(first)
            def _():
                wqkv_t[g] = wqkv[g].T

            @pl.when(i * GROUPS + j >= 2)
            def _():
                fwd_save(slot, 0, 0).wait()

            xg = x[i, g]
            q = (nn(wqkv_t[g, 0:WIDTH, :], xg) + col(g, Q_BIAS)).astype(BF16) * jnp.asarray(SCALE, BF16)
            k = nn(wqkv_t[g, WIDTH : 2 * WIDTH, :], xg).astype(BF16)
            v = (nn(wqkv_t[g, 2 * WIDTH :, :], xg) + col(g, V_BIAS)).astype(BF16)
            fwd[slot, V_AT:FWD_ROWS, :] = v
            for h in range(HEADS_GROUP):
                part = slice(h * HEAD_DIM, (h + 1) * HEAD_DIM)
                qh = jnp.concatenate([q[part], hot_q])
                kh = jnp.concatenate([k[part], hot_k])
                fwd[slot, Q_AT + h * PAD : Q_AT + (h + 1) * PAD, :] = qh
                fwd[slot, K_AT + h * PAD : K_AT + (h + 1) * PAD, :] = kh
                scores = tn(kh, qh)
                largest = jnp.max(scores, axis=0, keepdims=True)
                powers = jnp.exp(scores - largest)
                inverse = 1.0 / channel_sum(powers)
                e = powers.astype(BF16)
                fwd[slot, E_AT + h * SEQ_LEN : E_AT + (h + 1) * SEQ_LEN, :] = e
                linv_s[g * HEADS_GROUP + h] = inverse
                ctx_s[pl.ds(pl.multiple_of(g * WIDTH + h * HEAD_DIM, HEAD_DIM), HEAD_DIM), :] = (
                    nn(v[part], e) * inverse
                ).astype(BF16)
            fwd_save(slot, i, g).start()

        each(GROUPS, attend)

        @pl.when(first)
        def _():
            start_in(dy_in, dy, s_dy, r_dy, 0)
            for k in range(2, 4):
                got_weight(k, 2)
                send_weight(k, 3).start()

        @pl.when(i + 1 < count)
        def _():
            start_in(x_in, x, s_x, r_x, i + 1)

        def mix(g, carry):
            total, square = carry
            branch = (nn(wout_t[rows_of(g), :], ctx_s[...]) + col(g, OUT_BIAS)).astype(BF16)
            summed = branch.astype(F32) + x[i, g].astype(F32)
            summed_s[g] = summed
            return total + fold(summed), square + fold(summed * summed)

        total, square = over(GROUPS, mix, (zero, zero))
        center1 = channel_sum(total) / D
        inverse1 = lax.rsqrt(channel_sum(square) / D - center1 * center1 + EPS)

        @pl.when(first)
        def _():
            for k in range(2, 4):
                own_weight(k).wait()
                got_weight(k, 1)
                got_weight(k, 3)

            def turn(g):
                wup_t[g] = wup[g].T
                wdown_t[g] = wdown[g].T

            each(GROUPS, turn)

        def feed(g, carry):
            total, square = carry
            normed = (summed_s[g] - center1) * inverse1
            hidden = (normed * col(g, GAIN_ONE) + col(g, SHIFT_ONE)).astype(BF16)
            hidden_s[g] = hidden
            for part in range(PARTS):
                rows = slice(part * WIDTH, (part + 1) * WIDTH)
                u = nn(wup_t[g, rows, :], hidden) + col(g, UP_BIAS + part)
                act, slope = gelu_pair(u)
                act_s[g, rows, :] = act.astype(BF16)
                slope_s[g, rows, :] = slope.astype(BF16)
            summed2 = hidden.astype(F32) + nn(wdown[g], act_s[g]) + col(g, DOWN_BIAS)
            summed2_s[g] = summed2
            return total + fold(summed2), square + fold(summed2 * summed2)

        total, square = over(GROUPS, feed, (zero, zero))
        center2 = channel_sum(total) / D
        inverse2 = lax.rsqrt(channel_sum(square) / D - center2 * center2 + EPS)

        @pl.when(i > 0)
        def _():
            own_lo(i - 1).wait()
            for j in range(1, GROUPS):
                send_lo(i - 1, j).wait_send()

        own_in(dy_in, dy, s_dy, i).wait()
        for j in range(1, GROUPS):
            block = dy.at[i, flip(me, j)]
            remote(block, block, s_dy.at[i, j], r_dy.at[i, j], flip(me, j)).wait_recv()

        @pl.when(i + 1 < count)
        def _():
            start_in(dy_in, dy, s_dy, r_dy, i + 1)

        def finish(g, carry):
            sum_e, sum_en = carry
            normed = (summed2_s[g] - center2) * inverse2
            gain = col(g, GAIN_TWO)
            lo_s[g] = (normed * gain + col(g, SHIFT_TWO)).astype(BF16)
            grad = dy[i, g].astype(F32)
            product = grad * normed
            add_sum(g, GAIN_TWO, product)
            add_sum(g, SHIFT_TWO, grad)
            summed2_s[g] = normed
            return sum_e + fold(grad * gain), sum_en + fold(product * gain)

        sum_e, sum_en = over(GROUPS, finish, (zero, zero))
        mean_e = channel_sum(sum_e) / D
        mean_en = channel_sum(sum_en) / D

        own_lo(i).start()
        for j in range(1, GROUPS):
            send_lo(i, j).start()

        def feed_back(g, carry):
            sum_h, sum_hn = carry
            normed2 = summed2_s[g]
            scaled = dy[i, g].astype(F32) * col(g, GAIN_TWO)
            grad2 = (inverse2 * (scaled - mean_e - normed2 * mean_en)).astype(BF16)
            wide = grad2.astype(F32)
            add_sum(g, DOWN_BIAS, wide)
            for part in range(PARTS):
                rows = slice(part * WIDTH, (part + 1) * WIDTH)
                up_grad = (nn(wdown_t[g, rows, :], grad2) * slope_s[g, rows, :].astype(F32)).astype(BF16)
                up_grad_s[rows, :] = up_grad
                add_sum(g, UP_BIAS + part, up_grad.astype(F32))
            g_up[g] += nt(hidden_s[g], up_grad_s[...])
            g_down[g] += nt(grad2, act_s[g])
            hidden_grad = (wide + nn(wup[g], up_grad_s[...])).astype(BF16)
            hidden_grad_s[rows_of(g), :] = hidden_grad
            grad1 = hidden_grad.astype(F32)
            normed1 = (summed_s[g] - center1) * inverse1
            product = grad1 * normed1
            gain = col(g, GAIN_ONE)
            add_sum(g, GAIN_ONE, product)
            add_sum(g, SHIFT_ONE, grad1)
            return sum_h + fold(grad1 * gain), sum_hn + fold(product * gain)

        sum_h, sum_hn = over(GROUPS, feed_back, (zero, zero))
        mean_h = channel_sum(sum_h) / D
        mean_hn = channel_sum(sum_hn) / D

        def norm_back(g):
            normed1 = (summed_s[g] - center1) * inverse1
            scaled = hidden_grad_s[rows_of(g), :].astype(F32) * col(g, GAIN_ONE)
            summed_grad = (inverse1 * (scaled - mean_h - normed1 * mean_hn)).astype(BF16)
            hidden_grad_s[rows_of(g), :] = summed_grad
            add_sum(g, OUT_BIAS, summed_grad.astype(F32))

        each(GROUPS, norm_back)

        def mix_back(g):
            slot = g % 2

            @pl.when(i * GROUPS + g >= 2)
            def _():
                bwd_save(slot, 0, 0).wait()

            ctx = ctx_s[rows_of(g), :]
            g_out[rows_of(g), :] += nt(ctx, hidden_grad_s[...])
            ctx_grad = nn(wout[rows_of(g), :], hidden_grad_s[...]).astype(BF16).astype(F32)
            for h in range(HEADS_GROUP):
                part = slice(h * HEAD_DIM, (h + 1) * HEAD_DIM)
                grad = (ctx_grad[part] * linv_s[g * HEADS_GROUP + h]).astype(BF16)
                bwd[slot, h * HEAD_DIM : (h + 1) * HEAD_DIM, :] = grad
                middle_s[i * HEADS + g * HEADS_GROUP + h] = channel_sum(grad.astype(F32) * ctx[part].astype(F32))
            bwd[slot, WIDTH:BWD_ROWS, :] = hidden_grad_s[rows_of(g), :]
            bwd_save(slot, i, g).start()

        each(GROUPS, mix_back)

    each(count, sequence)
    for slot in range(2):
        fwd_save(slot, 0, 0).wait()
        bwd_save(slot, 0, 0).wait()

    def unit_of(u):
        return u % count, GROUPS - 1 - u // count

    def load(u):
        i, j = unit_of(u)
        g = flip(me, j)
        fwd_load(u % 2, i, g).start()
        bwd_load(u % 2, i, g).start()

    def send_dx(i, j):
        to = flip(me, j)
        return remote(x.at[i, to], dx_out.at[me * count + i], s_dx.at[i, j], r_dx.at[i, j], to)

    def own_dx(i):
        return pltpu.make_async_copy(x.at[i, me], dx_out.at[me * count + i], s_dx.at[i, 0])

    load(0)

    def unit(u):
        i, j = unit_of(u)
        g = flip(me, j)
        slot = u % 2
        fwd_load(slot, i, g).wait()
        bwd_load(slot, i, g).wait()

        @pl.when(u + 1 < count * GROUPS)
        def _():
            load(u + 1)

        for h in range(HEADS_GROUP):
            e = fwd[slot, E_AT + h * SEQ_LEN : E_AT + (h + 1) * SEQ_LEN, :]
            q = fwd[slot, Q_AT + h * PAD : Q_AT + h * PAD + HEAD_DIM, :]
            k = fwd[slot, K_AT + h * PAD : K_AT + h * PAD + HEAD_DIM, :]
            v = fwd[slot, V_AT + h * HEAD_DIM : V_AT + (h + 1) * HEAD_DIM, :]
            grad = bwd[slot, h * HEAD_DIM : (h + 1) * HEAD_DIM, :]
            prob_grad = tn(v, grad)
            score_grad = (e.astype(F32) * (prob_grad - middle_s[i * HEADS + g * HEADS_GROUP + h])).astype(BF16)
            at = h * HEAD_DIM
            qkv_grad_s[2 * WIDTH + at : 2 * WIDTH + at + HEAD_DIM, :] = nt(grad, e).astype(BF16)
            qkv_grad_s[at : at + HEAD_DIM, :] = (nn(k, score_grad) * SCALE).astype(BF16)
            qkv_grad_s[WIDTH + at : WIDTH + at + HEAD_DIM, :] = nt(q, score_grad).astype(BF16)
        g_qkv[g] += nt(qkv_grad_s[...], x[i, g])
        add_sum(g, Q_BIAS, qkv_grad_s[0:WIDTH, :].astype(F32))
        add_sum(g, V_BIAS, qkv_grad_s[2 * WIDTH :, :].astype(F32))
        into = bwd[slot, WIDTH:BWD_ROWS, :].astype(F32) + nn(wqkv[g], qkv_grad_s[...])
        x[i, g] = into.astype(BF16)

        @pl.when(j > 0)
        def _():
            send_dx(i, j).start()

        @pl.when(j == 0)
        def _():
            own_dx(i).start()

    each(count * GROUPS, unit)

    def close(at):
        g_vec[at] = jnp.sum(vec[at].T, axis=0, keepdims=True)

    each(GROUPS * COLS, close)

    for k in range(4):
        for j in (1, 2, 3):
            send_weight(k, j).wait_send()
    own_lo(count - 1).wait()
    for j in range(1, GROUPS):
        send_lo(count - 1, j).wait_send()

    def drain(i):
        own_dx(i).wait()
        for j in range(1, GROUPS):
            move_in(x_in, x, s_x, r_x, i, j).wait_send()
            move_in(dy_in, dy, s_dy, r_dy, i, j).wait_send()
            send_lo(i, j).wait_recv()
            send_dx(i, j).wait_send()
            send_dx(i, j).wait_recv()

    each(count, drain)


def layer(x, dy, seg, wqkv, wup, wdown, wout, params):
    count = x.shape[0] // GROUPS
    here = pl.BlockSpec(memory_space=pl.ANY)
    vmem = pl.BlockSpec(memory_space=pltpu.VMEM)
    grads = [
        (GROUPS, QKV, WIDTH),
        (GROUPS, WIDTH, UNITS),
        (GROUPS, WIDTH, UNITS),
        (D, D),
        (GROUPS * COLS, 1, WIDTH),
    ]
    token = (GROUPS, WIDTH, SEQ_LEN)
    dma = pltpu.SemaphoreType.DMA
    return pl.pallas_call(
        layer_kernel,
        out_shape=[jax.ShapeDtypeStruct(x.shape, BF16)] * 2
        + [
            jax.ShapeDtypeStruct((count, GROUPS, FWD_ROWS, SEQ_LEN), BF16),
            jax.ShapeDtypeStruct((count, GROUPS, BWD_ROWS, SEQ_LEN), BF16),
        ]
        + [jax.ShapeDtypeStruct(s, F32) for s in grads],
        in_specs=[here, here, vmem, here, here, here, vmem, vmem],
        out_specs=[here] * 4 + [vmem] * len(grads),
        scratch_shapes=[
            pltpu.VMEM((count,) + token, BF16),
            pltpu.VMEM((count,) + token, BF16),
            pltpu.VMEM((GROUPS, WIDTH, QKV), BF16),
            pltpu.VMEM((GROUPS, WIDTH, UNITS), BF16),
            pltpu.VMEM((GROUPS, WIDTH, UNITS), BF16),
            pltpu.VMEM((GROUPS, TABLE, WIDTH), F32),
            pltpu.VMEM((GROUPS, WIDTH, 128), F32),
            pltpu.VMEM((GROUPS, QKV, WIDTH), BF16),
            pltpu.VMEM((GROUPS, UNITS, WIDTH), BF16),
            pltpu.VMEM((GROUPS, UNITS, WIDTH), BF16),
            pltpu.VMEM((D, D), BF16),
            pltpu.VMEM((GROUPS * COLS, WIDTH, 128), F32),
            pltpu.VMEM((2, FWD_ROWS, SEQ_LEN), BF16),
            pltpu.VMEM((2, BWD_ROWS, SEQ_LEN), BF16),
            pltpu.VMEM((count * HEADS, 1, SEQ_LEN), F32),
            pltpu.VMEM((HEADS, 1, SEQ_LEN), F32),
            pltpu.VMEM((D, SEQ_LEN), BF16),
            pltpu.VMEM(token, F32),
            pltpu.VMEM(token, BF16),
            pltpu.VMEM((GROUPS, UNITS, SEQ_LEN), BF16),
            pltpu.VMEM((GROUPS, UNITS, SEQ_LEN), BF16),
            pltpu.VMEM(token, F32),
            pltpu.VMEM((UNITS, SEQ_LEN), BF16),
            pltpu.VMEM((D, SEQ_LEN), BF16),
            pltpu.VMEM((D, SEQ_LEN), BF16),
            pltpu.VMEM((QKV, SEQ_LEN), BF16),
            pltpu.VMEM(token, BF16),
        ]
        + [dma((count, GROUPS))] * 8
        + [dma((4, GROUPS))] * 2
        + [dma((2,))] * 2,
        compiler_params=pltpu.CompilerParams(
            vmem_limit_bytes=63 << 20, collective_id=0, has_side_effects=True
        ),
    )(x, dy, seg, wqkv, wup, wdown, wout, params)


def local(
    layer_input, segment_ids, qkv_weight, qv_bias, out_weight, out_bias, gain_one, shift_one,
    up_weight, up_bias, down_weight, down_bias, gain_two, shift_two, out_grad,
):
    me = lax.axis_index("grp")

    def rows(a):
        return a.reshape(-1, WIDTH)

    def mine_of(a):
        return lax.dynamic_slice_in_dim(a, me * WIDTH, WIDTH, 0).reshape(1, WIDTH)

    params = jnp.concatenate(
        [rows(a) for a in (qv_bias, up_bias, down_bias, gain_two, shift_two)]
        + [mine_of(a) for a in (out_bias, gain_one, shift_one)]
        + [jnp.zeros((TABLE - COLS, WIDTH), F32)]
    )
    lo, dx, _, _, g_qkv, g_up, g_down, g_out, g_vec = layer(
        layer_input, out_grad, segment_ids, qkv_weight, up_weight, down_weight, out_weight, params
    )

    def total(a):
        a = lax.psum_scatter(a, "grp", scatter_dimension=0, tiled=True)
        return lax.psum(a.astype(BF16), "rows").astype(F32)

    g_vec = lax.psum(g_vec[:, 0, :], ("rows", "grp")).reshape(GROUPS, COLS, WIDTH)
    mine = lax.dynamic_slice_in_dim(g_vec, me, 1, 0)[0]
    g_out = lax.psum(g_out, ("rows", "grp"))
    return (
        lo.astype(F32),
        dx.astype(F32),
        jnp.swapaxes(total(g_qkv), 1, 2),
        mine[Q_BIAS : V_BIAS + 1].reshape(1, 2 * WIDTH),
        g_out,
        g_vec[:, OUT_BIAS].reshape(D),
        g_vec[:, GAIN_ONE].reshape(D),
        g_vec[:, SHIFT_ONE].reshape(D),
        total(g_up),
        mine[UP_BIAS:DOWN_BIAS].reshape(1, UNITS),
        total(g_down),
        mine[DOWN_BIAS].reshape(1, WIDTH),
        mine[GAIN_TWO],
        mine[SHIFT_TWO],
    )


def solution(mesh):
    group = P("grp", None, None)
    data = P("rows", "grp", None)
    in_specs = (
        data, P("rows", None), group, P("grp", None), P(), P(), P(), P(),
        group, P("grp", None), group, P("grp", None), P("grp"), P("grp"), data,
    )
    out_specs = (
        data, data, group, P("grp", None), P(), P(), P(), P(),
        group, P("grp", None), group, P("grp", None), P("grp"), P("grp"),
    )
    return jax.shard_map(local, mesh=mesh, in_specs=in_specs, out_specs=out_specs, check_vma=False)
```

```python
import functools

import jax
import jax.numpy as jnp
from jax import lax
from jax.experimental import pallas as pl
from jax.experimental.pallas import tpu as pltpu
from jax.sharding import PartitionSpec as P

D = 768
HEAD_DIM = 64
SEQ_LEN = 512
GROUPS = 4
WIDTH = D // GROUPS
HEADS_GROUP = WIDTH // HEAD_DIM
HEADS = D // HEAD_DIM
QKV = 3 * WIDTH
UNITS = 768
PARTS = UNITS // WIDTH
PAD = HEAD_DIM + 16
MASKED = -1e30
EPS = 1e-05
SCALE = HEAD_DIM ** (-0.5)
BLOCKS = 3
HALF = UNITS // 2

F32 = jnp.float32
BF16 = jnp.bfloat16
MESH = pl.DeviceIdType.MESH

Q_BIAS, V_BIAS, UP_BIAS, DOWN_BIAS, GAIN_TWO, SHIFT_TWO, OUT_BIAS, GAIN_ONE, SHIFT_ONE = 0, 1, 2, 6, 7, 8, 9, 10, 11
COLS = 12
TABLE = 16

E_AT = 0
Q_AT = HEADS_GROUP * SEQ_LEN
K_AT = Q_AT + HEADS_GROUP * PAD
V_AT = K_AT + HEADS_GROUP * PAD
FWD_ROWS = V_AT + WIDTH
BWD_ROWS = 2 * WIDTH


def nn(a, b):
    return lax.dot_general(a, b, (((1,), (0,)), ((), ())), preferred_element_type=F32)


def nt(a, b):
    return lax.dot_general(a, b, (((1,), (1,)), ((), ())), preferred_element_type=F32)


def tn(a, b):
    return lax.dot_general(a, b, (((0,), (0,)), ((), ())), preferred_element_type=F32)


def lane_part(value):
    total = value[:, 0:128]
    for at in range(128, SEQ_LEN, 128):
        total = total + value[:, at : at + 128]
    return total


def channel_sum(value):
    return jnp.sum(value, axis=0, keepdims=True)


def fold(value):
    return jnp.sum(value.reshape(value.shape[0] // 8, 8, SEQ_LEN), axis=0)


def spread(column):
    return jnp.concatenate([column] * (SEQ_LEN // 128), axis=1)


def gelu_pair(u):
    half_erf = 0.5 * lax.erf(u * 0.7071067811865476) + 0.5
    density = jnp.exp(u * u * -0.5) * 0.3989422804014327
    return u * half_erf, half_erf + u * density


def flip(me, j):
    return (me + j) % 2 + 2 * ((me // 2 + j // 2) % 2)


def owners_of(rows, parts):
    return max(n for n in range(1, min(rows, parts) + 1) if parts % n == 0)


def layer_kernel(
    size, x_in, dy_in, seg, wqkv_in, wup_in, wdown_in, wout, params,
    lo_out, dx_out, fwd_st, bwd_st, qkv_out, up_out, down_out, mix_l, sums_out, shared_out,
    x, dy, wqkv, wup, wdown, table, cols, wqkv_t, wup_t, wdown_t, wout_t, vec,
    fwd, bwd, middle_s, linv_s, ctx_s, summed_s, hidden_s, act_s, slope_s, summed2_s,
    up_grad_s, hidden_grad_s, qkv_grad_s, lo_s,
    acc, g_qkv, pair_t, pair_l, far_t, far_l, cut_t, cut_l, all_t, all_l,
    qkv_t, qkv_l, qcut_t, qcut_l, qall_t, qall_l, sum_t, sum_l, sum_row_t, sum_row_l, end_t, end_l, end_row_t, end_row_l,
    s_x, r_x, s_dy, r_dy, s_lo, r_lo, s_dx, r_dx, s_w, r_w, s_grp, r_grp, s_row, r_row, s_fwd, s_bwd,
):
    count = x.shape[0]
    me = lax.axis_index("grp")
    row = lax.axis_index("rows")
    zero = jnp.zeros((8, SEQ_LEN), F32)

    def over(n, body, init=0, unroll=False):
        return lax.fori_loop(0, n, body, init, unroll=unroll)

    def each(n, body):
        def run(at, carry):
            body(at)
            return carry

        lax.fori_loop(0, n, run, 0)

    def remote(src, dst, send, recv, to):
        return pltpu.make_async_remote_copy(
            src_ref=src, dst_ref=dst, send_sem=send, recv_sem=recv, device_id={"grp": to}, device_id_type=MESH
        )

    barrier = pltpu.get_barrier_semaphore()
    for j in range(1, GROUPS):
        pl.semaphore_signal(barrier, inc=1, device_id={"grp": flip(me, j)}, device_id_type=MESH)

    def greet(k):
        pl.semaphore_signal(barrier, inc=1, device_id={"rows": (row + k + 1) % size}, device_id_type=MESH)

    each(size - 1, greet)
    pl.semaphore_wait(barrier, GROUPS - 1 + size - 1)

    def move_in(src, dst, send, recv, i, j):
        to = flip(me, j)
        return remote(src.at[to * count + i], dst.at[i, me], send.at[i, j], recv.at[i, j], to)

    def start_in(src, dst, send, recv, i):
        for j in range(1, GROUPS):
            move_in(src, dst, send, recv, i, j).start()

    def own_in(src, dst, send, i):
        return pltpu.make_async_copy(src.at[me * count + i], dst.at[i, me], send.at[i, 0])

    weights = ((params, table), (wqkv_in.at[0], wqkv), (wup_in.at[0], wup), (wdown_in.at[0], wdown))

    def own_weight(k):
        src, dst = weights[k]
        return pltpu.make_async_copy(src, dst.at[me], s_w.at[k, 0])

    def send_weight(k, j):
        src, dst = weights[k]
        if j < 3:
            return remote(src, dst.at[me], s_w.at[k, j], r_w.at[k, j], flip(me, j))
        got = dst.at[flip(me, 2)]
        return remote(got, got, s_w.at[k, 3], r_w.at[k, 3], flip(me, 1))

    def got_weight(k, j):
        src, dst = weights[k]
        block = dst.at[flip(me, j)]
        remote(block, block, s_w.at[k, j], r_w.at[k, j], flip(me, 1)).wait_recv()

    for k in range(2):
        own_weight(k).start()
        send_weight(k, 2).start()
        send_weight(k, 1).start()
    own_in(x_in, x, s_x, 0).start()
    start_in(x_in, x, s_x, r_x, 0)
    for k in range(2, 4):
        own_weight(k).start()
        send_weight(k, 2).start()
        send_weight(k, 1).start()
    own_in(dy_in, dy, s_dy, 0).start()

    def own_rest(i):
        own_in(x_in, x, s_x, i + 1).start()
        own_in(dy_in, dy, s_dy, i + 1).start()

    each(count - 1, own_rest)

    g_qkv[...] = jnp.zeros_like(g_qkv)
    acc[...] = jnp.zeros_like(acc)
    vec[...] = jnp.zeros_like(vec)
    wout_t[...] = wout[...].T

    own_weight(0).wait()
    got_weight(0, 1)
    got_weight(0, 2)
    send_weight(0, 3).start()
    got_weight(0, 3)
    for g in range(GROUPS):
        cols[g, :, 0:TABLE] = table[g].T

    def col(g, at):
        return cols[g, :, at : at + 1]

    def add_sum(g, at, value):
        vec[g * COLS + at] += lane_part(value)

    def rows_of(g):
        return pl.ds(pl.multiple_of(g * WIDTH, WIDTH), WIDTH)

    def fwd_save(slot, i, g):
        return pltpu.make_async_copy(fwd.at[slot], fwd_st.at[i, g], s_fwd.at[slot])

    def bwd_save(slot, i, g):
        return pltpu.make_async_copy(bwd.at[slot], bwd_st.at[i, g], s_bwd.at[slot])

    def fwd_load(slot, i, g):
        return pltpu.make_async_copy(fwd_st.at[i, g], fwd.at[slot], s_fwd.at[slot])

    def bwd_load(slot, i, g):
        return pltpu.make_async_copy(bwd_st.at[i, g], bwd.at[slot], s_bwd.at[slot])

    def send_lo(i, j):
        to = flip(me, j)
        return remote(lo_s.at[to], lo_out.at[me * count + i], s_lo.at[i, j], r_lo.at[i, j], to)

    def own_lo(i):
        return pltpu.make_async_copy(lo_s.at[me], lo_out.at[me * count + i], s_lo.at[i, 0])

    def sequence(i):
        first = i == 0
        label = seg[pl.ds(me * count + i, 1), :]
        ids = lax.broadcasted_iota(jnp.int32, (16, SEQ_LEN), 0)
        hot = (ids == label).astype(F32)
        hot_k = hot.astype(BF16)
        hot_q = jnp.where(ids < 4, (1.0 - hot) * MASKED, 0.0).astype(BF16)

        def attend(j):
            g = flip(me, j)
            slot = j % 2

            @pl.when(j == 0)
            def _():
                own_in(x_in, x, s_x, i).wait()

            @pl.when(j > 0)
            def _():
                block = x.at[i, g]
                remote(block, block, s_x.at[i, j], r_x.at[i, j], g).wait_recv()

            @pl.when(first & (j == 0))
            def _():
                own_weight(1).wait()

            @pl.when(first & (j == 1))
            def _():
                got_weight(1, 1)

            @pl.when(first & (j == 2))
            def _():
                got_weight(1, 2)
                send_weight(1, 3).start()

            @pl.when(first & (j == 3))
            def _():
                got_weight(1, 3)

            @pl.when(first)
            def _():
                wqkv_t[g] = wqkv[g].T

            @pl.when(i * GROUPS + j >= 2)
            def _():
                fwd_save(slot, 0, 0).wait()

            xg = x[i, g]
            q = (nn(wqkv_t[g, 0:WIDTH, :], xg) + col(g, Q_BIAS)).astype(BF16) * jnp.asarray(SCALE, BF16)
            k = nn(wqkv_t[g, WIDTH : 2 * WIDTH, :], xg).astype(BF16)
            v = (nn(wqkv_t[g, 2 * WIDTH :, :], xg) + col(g, V_BIAS)).astype(BF16)
            fwd[slot, V_AT:FWD_ROWS, :] = v
            for h in range(HEADS_GROUP):
                part = slice(h * HEAD_DIM, (h + 1) * HEAD_DIM)
                qh = jnp.concatenate([q[part], hot_q])
                kh = jnp.concatenate([k[part], hot_k])
                fwd[slot, Q_AT + h * PAD : Q_AT + (h + 1) * PAD, :] = qh
                fwd[slot, K_AT + h * PAD : K_AT + (h + 1) * PAD, :] = kh
                scores = tn(kh, qh)
                largest = jnp.max(scores, axis=0, keepdims=True)
                powers = jnp.exp(scores - largest)
                inverse = 1.0 / channel_sum(powers)
                e = powers.astype(BF16)
                fwd[slot, E_AT + h * SEQ_LEN : E_AT + (h + 1) * SEQ_LEN, :] = e
                linv_s[g * HEADS_GROUP + h] = inverse
                ctx_s[pl.ds(pl.multiple_of(g * WIDTH + h * HEAD_DIM, HEAD_DIM), HEAD_DIM), :] = (
                    nn(v[part], e) * inverse
                ).astype(BF16)
            fwd_save(slot, i, g).start()

        each(GROUPS, attend)

        @pl.when(first)
        def _():
            start_in(dy_in, dy, s_dy, r_dy, 0)
            for k in range(2, 4):
                got_weight(k, 2)
                send_weight(k, 3).start()

        @pl.when(i + 1 < count)
        def _():
            start_in(x_in, x, s_x, r_x, i + 1)

        def mix(g, carry):
            total, square = carry
            branch = (nn(wout_t[rows_of(g), :], ctx_s[...]) + col(g, OUT_BIAS)).astype(BF16)
            summed = branch.astype(F32) + x[i, g].astype(F32)
            summed_s[g] = summed
            return total + fold(summed), square + fold(summed * summed)

        total, square = over(GROUPS, mix, (zero, zero))
        center1 = channel_sum(total) / D
        inverse1 = lax.rsqrt(channel_sum(square) / D - center1 * center1 + EPS)

        @pl.when(first)
        def _():
            for k in range(2, 4):
                own_weight(k).wait()
                got_weight(k, 1)
                got_weight(k, 3)

            def turn(g):
                wup_t[g] = wup[g].T
                wdown_t[g] = wdown[g].T

            each(GROUPS, turn)

        def feed(g, carry):
            total, square = carry
            normed = (summed_s[g] - center1) * inverse1
            hidden = (normed * col(g, GAIN_ONE) + col(g, SHIFT_ONE)).astype(BF16)
            hidden_s[g] = hidden
            for part in range(PARTS):
                rows = slice(part * WIDTH, (part + 1) * WIDTH)
                u = nn(wup_t[g, rows, :], hidden) + col(g, UP_BIAS + part)
                act, slope = gelu_pair(u)
                act_s[g, rows, :] = act.astype(BF16)
                slope_s[g, rows, :] = slope.astype(BF16)
            summed2 = hidden.astype(F32) + nn(wdown[g], act_s[g]) + col(g, DOWN_BIAS)
            summed2_s[g] = summed2
            return total + fold(summed2), square + fold(summed2 * summed2)

        total, square = over(GROUPS, feed, (zero, zero))
        center2 = channel_sum(total) / D
        inverse2 = lax.rsqrt(channel_sum(square) / D - center2 * center2 + EPS)

        @pl.when(i > 0)
        def _():
            own_lo(i - 1).wait()
            for j in range(1, GROUPS):
                send_lo(i - 1, j).wait_send()

        own_in(dy_in, dy, s_dy, i).wait()
        for j in range(1, GROUPS):
            block = dy.at[i, flip(me, j)]
            remote(block, block, s_dy.at[i, j], r_dy.at[i, j], flip(me, j)).wait_recv()

        @pl.when(i + 1 < count)
        def _():
            start_in(dy_in, dy, s_dy, r_dy, i + 1)

        def finish(g, carry):
            sum_e, sum_en = carry
            normed = (summed2_s[g] - center2) * inverse2
            gain = col(g, GAIN_TWO)
            lo_s[g] = (normed * gain + col(g, SHIFT_TWO)).astype(BF16)
            grad = dy[i, g].astype(F32)
            product = grad * normed
            add_sum(g, GAIN_TWO, product)
            add_sum(g, SHIFT_TWO, grad)
            summed2_s[g] = normed
            return sum_e + fold(grad * gain), sum_en + fold(product * gain)

        sum_e, sum_en = over(GROUPS, finish, (zero, zero))
        mean_e = channel_sum(sum_e) / D
        mean_en = channel_sum(sum_en) / D

        own_lo(i).start()
        for j in range(1, GROUPS):
            send_lo(i, j).start()

        def feed_back(g, carry):
            sum_h, sum_hn = carry
            normed2 = summed2_s[g]
            scaled = dy[i, g].astype(F32) * col(g, GAIN_TWO)
            grad2 = (inverse2 * (scaled - mean_e - normed2 * mean_en)).astype(BF16)
            wide = grad2.astype(F32)
            add_sum(g, DOWN_BIAS, wide)
            for part in range(PARTS):
                rows = slice(part * WIDTH, (part + 1) * WIDTH)
                up_grad = (nn(wdown_t[g, rows, :], grad2) * slope_s[g, rows, :].astype(F32)).astype(BF16)
                up_grad_s[rows, :] = up_grad
                add_sum(g, UP_BIAS + part, up_grad.astype(F32))
            acc[0, g] += nt(hidden_s[g], up_grad_s[...])
            acc[1, g] += nt(grad2, act_s[g])
            hidden_grad = (wide + nn(wup[g], up_grad_s[...])).astype(BF16)
            hidden_grad_s[rows_of(g), :] = hidden_grad
            grad1 = hidden_grad.astype(F32)
            normed1 = (summed_s[g] - center1) * inverse1
            product = grad1 * normed1
            gain = col(g, GAIN_ONE)
            add_sum(g, GAIN_ONE, product)
            add_sum(g, SHIFT_ONE, grad1)
            return sum_h + fold(grad1 * gain), sum_hn + fold(product * gain)

        sum_h, sum_hn = over(GROUPS, feed_back, (zero, zero))
        mean_h = channel_sum(sum_h) / D
        mean_hn = channel_sum(sum_hn) / D

        def norm_back(g):
            normed1 = (summed_s[g] - center1) * inverse1
            scaled = hidden_grad_s[rows_of(g), :].astype(F32) * col(g, GAIN_ONE)
            summed_grad = (inverse1 * (scaled - mean_h - normed1 * mean_hn)).astype(BF16)
            hidden_grad_s[rows_of(g), :] = summed_grad
            add_sum(g, OUT_BIAS, summed_grad.astype(F32))

        each(GROUPS, norm_back)

        def mix_back(g):
            slot = g % 2

            @pl.when(i * GROUPS + g >= 2)
            def _():
                bwd_save(slot, 0, 0).wait()

            ctx = ctx_s[rows_of(g), :]
            acc[2, g] += nt(ctx, hidden_grad_s[...])
            ctx_grad = nn(wout[rows_of(g), :], hidden_grad_s[...]).astype(BF16).astype(F32)
            for h in range(HEADS_GROUP):
                part = slice(h * HEAD_DIM, (h + 1) * HEAD_DIM)
                grad = (ctx_grad[part] * linv_s[g * HEADS_GROUP + h]).astype(BF16)
                bwd[slot, h * HEAD_DIM : (h + 1) * HEAD_DIM, :] = grad
                middle_s[i * HEADS + g * HEADS_GROUP + h] = channel_sum(grad.astype(F32) * ctx[part].astype(F32))
            bwd[slot, WIDTH:BWD_ROWS, :] = hidden_grad_s[rows_of(g), :]
            bwd_save(slot, i, g).start()

        each(GROUPS, mix_back)

    each(count, sequence)
    for slot in range(2):
        fwd_save(slot, 0, 0).wait()
        bwd_save(slot, 0, 0).wait()

    def unit_of(u):
        return u % count, GROUPS - 1 - u // count

    def load(u):
        i, j = unit_of(u)
        g = flip(me, j)
        fwd_load(u % 2, i, g).start()
        bwd_load(u % 2, i, g).start()

    def send_dx(i, j):
        to = flip(me, j)
        return remote(x.at[i, to], dx_out.at[me * count + i], s_dx.at[i, j], r_dx.at[i, j], to)

    def own_dx(i):
        return pltpu.make_async_copy(x.at[i, me], dx_out.at[me * count + i], s_dx.at[i, 0])

    def across(kind, src, dst, j, to):
        return remote(src, dst, s_grp.at[kind, j], r_grp.at[kind, j], flip(me, to))

    def along(kind, src, dst, k):
        return pltpu.make_async_remote_copy(
            src_ref=src, dst_ref=dst, send_sem=s_row.at[kind, k], recv_sem=r_row.at[kind, k],
            device_id={"rows": (row + k) % size}, device_id_type=MESH,
        )

    def when(condition, body):
        if condition is True:
            body()
        else:
            pl.when(condition)(body)

    def owns(at, owners):
        return True if owners == size else at % size < owners

    def peers(body):
        each(size - 1, lambda k: body(k + 1))

    def scatter(kind, parts, landing, act):
        owners = parts.shape[0]

        def one(k):
            to = (row + k) % size
            piece = parts.at[to if owners == size else jnp.minimum(to, owners - 1)]
            when(owns(to, owners), lambda: act(along(kind, piece, landing.at[k], k)))

        peers(one)

    def scatter_got(kind, parts, landing):
        peers(lambda k: along(kind, parts.at[0], landing.at[k], k).wait_recv())

    def spread_out(kind, piece, landing, act):
        owners = landing.shape[0]
        own = row if owners == size else jnp.minimum(row, owners - 1)
        when(owns(row, owners), lambda: peers(lambda k: act(along(kind, piece, landing.at[own], k))))

    def spread_got(kind, piece, landing):
        owners = landing.shape[0]
        peers(
            lambda k: when(
                owns(row + size - k, owners), lambda: along(kind, piece, landing.at[0], k).wait_recv()
            )
        )

    def start(copy):
        copy.start()

    def sent(copy):
        copy.wait_send()

    owners = all_l.shape[0]
    per_half = owners // 2
    cut = WIDTH // per_half

    def place(o):
        return pl.ds(pl.multiple_of(o % per_half * cut, 16), cut)

    def pair_send():
        for at, bits in enumerate((1, 3)):
            for b in range(BLOCKS):
                pair_t[at, b] = acc[b, flip(me, bits)].astype(BF16)
        across(0, pair_t, pair_l, 1, 1).start()
        for g in range(GROUPS):
            for c in range(COLS):
                sum_t[g, c : c + 1, :] = jnp.sum(vec[g * COLS + c].T, axis=0, keepdims=True)
            sum_t[g, COLS:TABLE, :] = jnp.zeros((TABLE - COLS, WIDTH), F32)
        for j in range(1, GROUPS):
            across(2, sum_t.at[flip(me, j)], sum_l.at[j], j, j).start()

    def far_send():
        across(0, pair_t, pair_l, 1, 1).wait_recv()
        for b in range(BLOCKS):
            far_t[b] = (acc[b, flip(me, 2)] + pair_l[1, b].astype(F32)).astype(BF16)
        across(0, far_t, far_l, 2, 2).start()
        total = sum_t[me]
        for j in range(1, GROUPS):
            across(2, sum_t.at[0], sum_l.at[j], j, j).wait_recv()
            total = total + sum_l[j]
        sum_row_t[...] = total
        peers(lambda k: along(4, sum_row_t, sum_row_l.at[k], k).start())

    def cut_send():
        across(0, far_t, far_l, 2, 2).wait_recv()
        for b in range(BLOCKS):
            total = acc[b, me] + pair_l[0, b].astype(F32) + far_l[b].astype(F32)
            for o in range(owners):
                at = o % per_half * cut
                side = o // per_half * HALF
                cut_t[o, b] = total[at : at + cut, side : side + HALF].astype(BF16)
        scatter(0, cut_t, cut_l, start)
        total = sum_row_t[...]
        peers(lambda k: along(4, sum_row_t, sum_row_l.at[k], k).wait_recv())
        for k in range(1, size):
            total = total + sum_row_l[k]
        sums_out[...] = total
        shared_out[me] = total
        for j in range(1, GROUPS):
            across(5, sums_out, shared_out.at[me], j, j).start()

    def all_send():
        def close():
            scatter_got(0, cut_t, cut_l)
            own = row if owners == size else jnp.minimum(row, owners - 1)
            for b in range(BLOCKS):
                total = cut_t[own, b].astype(F32)
                for k in range(1, size):
                    total = total + cut_l[k, b].astype(F32)
                all_t[b] = total.astype(BF16)
                all_l[own, b] = total.astype(BF16)

        when(owns(row, owners), close)
        spread_out(1, all_t, all_l, start)

    def mix_send():
        spread_got(1, all_t, all_l)
        for o in range(owners):
            rows = slice(o % per_half * cut, o % per_half * cut + cut)
            side = slice(o // per_half * HALF, o // per_half * HALF + HALF)
            mix_l[me, rows, side] = all_l[o, 2]
        across(4, mix_l.at[me], mix_l.at[me], 2, 2).start()
        across(4, mix_l.at[me], mix_l.at[me], 1, 1).start()
        for o in range(owners):
            rows = slice(o % per_half * cut, o % per_half * cut + cut)
            side = slice(o // per_half * HALF, o // per_half * HALF + HALF)
            up_out[rows, side] = all_l[o, 0]
            down_out[rows, side] = all_l[o, 1]

    def mix_forward():
        block = mix_l.at[flip(me, 2)]
        across(4, block, block, 2, 2).wait_recv()
        across(4, block, block, 3, 1).start()

    def mix_close():
        for j in (1, 3):
            block = mix_l.at[flip(me, j)]
            across(4, block, block, j, 1).wait_recv()

    def late_sums(g):
        rows = [jnp.sum(vec[g * COLS + c].T, axis=0, keepdims=True) for c in (Q_BIAS, V_BIAS)]
        return jnp.concatenate(rows + [jnp.zeros((6, WIDTH), F32)])

    qowners = qall_l.shape[0]
    qcut = WIDTH // qowners

    def qkv_cut_send():
        total = g_qkv[me]
        sums = late_sums(me)
        for j in range(1, GROUPS):
            across(1, qkv_t.at[j - 1], qkv_l.at[j - 1], j, j).wait_recv()
            across(3, end_t.at[j], end_l.at[j], j, j).wait_recv()
            total = total + qkv_l[j - 1].astype(F32)
            sums = sums + end_l[j]
        for o in range(qowners):
            qcut_t[o] = total[o * qcut : (o + 1) * qcut].astype(BF16)
        end_row_t[...] = sums
        scatter(2, qcut_t, qcut_l, start)
        peers(lambda k: along(5, end_row_t, end_row_l.at[k], k).start())

    def qkv_all_send():
        def close():
            scatter_got(2, qcut_t, qcut_l)
            own = row if qowners == size else jnp.minimum(row, qowners - 1)
            total = qcut_t[own].astype(F32)
            for k in range(1, size):
                total = total + qcut_l[k].astype(F32)
            qall_t[...] = total.astype(BF16)
            qall_l[own] = total.astype(BF16)

        when(owns(row, qowners), close)
        spread_out(3, qall_t, qall_l, start)

    def qkv_close():
        peers(lambda k: along(5, end_row_t, end_row_l.at[k], k).wait_recv())
        sums = end_row_t[...]
        for k in range(1, size):
            sums = sums + end_row_l[k]
        sums_out[0:2, :] = sums[0:2]
        spread_got(3, qall_t, qall_l)
        for o in range(qowners):
            qkv_out[o * qcut : (o + 1) * qcut, :] = qall_l[o]

    load(0)
    pair_send()

    def unit(u):
        i, j = unit_of(u)
        g = flip(me, j)
        slot = u % 2
        fwd_load(slot, i, g).wait()
        bwd_load(slot, i, g).wait()

        @pl.when(u + 1 < count * GROUPS)
        def _():
            load(u + 1)

        for h in range(HEADS_GROUP):
            e = fwd[slot, E_AT + h * SEQ_LEN : E_AT + (h + 1) * SEQ_LEN, :]
            q = fwd[slot, Q_AT + h * PAD : Q_AT + h * PAD + HEAD_DIM, :]
            k = fwd[slot, K_AT + h * PAD : K_AT + h * PAD + HEAD_DIM, :]
            v = fwd[slot, V_AT + h * HEAD_DIM : V_AT + (h + 1) * HEAD_DIM, :]
            grad = bwd[slot, h * HEAD_DIM : (h + 1) * HEAD_DIM, :]
            prob_grad = tn(v, grad)
            score_grad = (e.astype(F32) * (prob_grad - middle_s[i * HEADS + g * HEADS_GROUP + h])).astype(BF16)
            at = h * HEAD_DIM
            qkv_grad_s[2 * WIDTH + at : 2 * WIDTH + at + HEAD_DIM, :] = nt(grad, e).astype(BF16)
            qkv_grad_s[at : at + HEAD_DIM, :] = (nn(k, score_grad) * SCALE).astype(BF16)
            qkv_grad_s[WIDTH + at : WIDTH + at + HEAD_DIM, :] = nt(q, score_grad).astype(BF16)
        g_qkv[g] += nt(x[i, g], qkv_grad_s[...])
        add_sum(g, Q_BIAS, qkv_grad_s[0:WIDTH, :].astype(F32))
        add_sum(g, V_BIAS, qkv_grad_s[2 * WIDTH :, :].astype(F32))
        into = bwd[slot, WIDTH:BWD_ROWS, :].astype(F32) + nn(wqkv[g], qkv_grad_s[...])
        x[i, g] = into.astype(BF16)

        @pl.when((j > 0) & (i == count - 1))
        def _():
            qkv_t[j - 1] = g_qkv[g].astype(BF16)
            end_t[j] = late_sums(g)
            across(1, qkv_t.at[j - 1], qkv_l.at[j - 1], j, j).start()
            across(3, end_t.at[j], end_l.at[j], j, j).start()

        @pl.when(j > 0)
        def _():
            send_dx(i, j).start()

        @pl.when(j == 0)
        def _():
            own_dx(i).start()

    def units(first, last):
        each(last - first, lambda u: unit(u + first))

    marks = [count * GROUPS * part // 16 for part in (1, 6, 11, 16)]
    units(0, marks[0])
    far_send()
    units(marks[0], marks[1])
    cut_send()
    units(marks[1], marks[2])
    all_send()
    units(marks[2], marks[3])
    for j in range(1, GROUPS):
        across(5, sums_out, shared_out.at[flip(me, j)], j, j).wait_recv()
        across(5, sums_out, shared_out.at[me], j, j).wait_send()
    qkv_cut_send()
    mix_send()
    mix_forward()
    qkv_all_send()
    mix_close()
    qkv_close()

    for k in range(4):
        for j in (1, 2, 3):
            send_weight(k, j).wait_send()
    own_lo(count - 1).wait()
    for j in range(1, GROUPS):
        send_lo(count - 1, j).wait_send()

    def drain(i):
        own_dx(i).wait()
        for j in range(1, GROUPS):
            move_in(x_in, x, s_x, r_x, i, j).wait_send()
            move_in(dy_in, dy, s_dy, r_dy, i, j).wait_send()
            send_lo(i, j).wait_recv()
            send_dx(i, j).wait_send()
            send_dx(i, j).wait_recv()

    each(count, drain)
    across(0, pair_t, pair_l, 1, 1).wait_send()
    across(0, far_t, far_l, 2, 2).wait_send()
    for j in range(1, GROUPS):
        across(1, qkv_t.at[j - 1], qkv_l.at[j - 1], j, j).wait_send()
        across(2, sum_t.at[0], sum_l.at[j], j, j).wait_send()
        across(3, end_t.at[j], end_l.at[j], j, j).wait_send()
        across(4, mix_l.at[me], mix_l.at[me], j, 1).wait_send()
    scatter(0, cut_t, cut_l, sent)
    spread_out(1, all_t, all_l, sent)
    scatter(2, qcut_t, qcut_l, sent)
    spread_out(3, qall_t, qall_l, sent)
    peers(lambda k: along(4, sum_row_t, sum_row_l.at[k], k).wait_send())
    peers(lambda k: along(5, end_row_t, end_row_l.at[k], k).wait_send())


def layer(size, x, dy, seg, wqkv, wup, wdown, wout, params):
    count = x.shape[0] // GROUPS
    here = pl.BlockSpec(memory_space=pl.ANY)
    vmem = pl.BlockSpec(memory_space=pltpu.VMEM)
    grads = [
        ((WIDTH, QKV), BF16),
        ((WIDTH, UNITS), BF16),
        ((WIDTH, UNITS), BF16),
        ((GROUPS, WIDTH, UNITS), BF16),
        ((TABLE, WIDTH), F32),
        ((GROUPS, TABLE, WIDTH), F32),
    ]
    owners = 2 * owners_of(size // 2, WIDTH // 16)
    piece = (BLOCKS, 2 * WIDTH // owners, HALF)
    qowners = owners_of(size, WIDTH // 16)
    qpiece = (WIDTH // qowners, QKV)
    token = (GROUPS, WIDTH, SEQ_LEN)
    dma = pltpu.SemaphoreType.DMA
    return pl.pallas_call(
        functools.partial(layer_kernel, size),
        out_shape=[jax.ShapeDtypeStruct(x.shape, BF16)] * 2
        + [
            jax.ShapeDtypeStruct((count, GROUPS, FWD_ROWS, SEQ_LEN), BF16),
            jax.ShapeDtypeStruct((count, GROUPS, BWD_ROWS, SEQ_LEN), BF16),
        ]
        + [jax.ShapeDtypeStruct(s, t) for s, t in grads],
        in_specs=[here, here, vmem, here, here, here, vmem, vmem],
        out_specs=[here] * 4 + [vmem] * len(grads),
        scratch_shapes=[
            pltpu.VMEM((count,) + token, BF16),
            pltpu.VMEM((count,) + token, BF16),
            pltpu.VMEM((GROUPS, WIDTH, QKV), BF16),
            pltpu.VMEM((GROUPS, WIDTH, UNITS), BF16),
            pltpu.VMEM((GROUPS, WIDTH, UNITS), BF16),
            pltpu.VMEM((GROUPS, TABLE, WIDTH), F32),
            pltpu.VMEM((GROUPS, WIDTH, 128), F32),
            pltpu.VMEM((GROUPS, QKV, WIDTH), BF16),
            pltpu.VMEM((GROUPS, UNITS, WIDTH), BF16),
            pltpu.VMEM((GROUPS, UNITS, WIDTH), BF16),
            pltpu.VMEM((D, D), BF16),
            pltpu.VMEM((GROUPS * COLS, WIDTH, 128), F32),
            pltpu.VMEM((2, FWD_ROWS, SEQ_LEN), BF16),
            pltpu.VMEM((2, BWD_ROWS, SEQ_LEN), BF16),
            pltpu.VMEM((count * HEADS, 1, SEQ_LEN), F32),
            pltpu.VMEM((HEADS, 1, SEQ_LEN), F32),
            pltpu.VMEM((D, SEQ_LEN), BF16),
            pltpu.VMEM(token, F32),
            pltpu.VMEM(token, BF16),
            pltpu.VMEM((GROUPS, UNITS, SEQ_LEN), BF16),
            pltpu.VMEM((GROUPS, UNITS, SEQ_LEN), BF16),
            pltpu.VMEM(token, F32),
            pltpu.VMEM((UNITS, SEQ_LEN), BF16),
            pltpu.VMEM((D, SEQ_LEN), BF16),
            pltpu.VMEM((QKV, SEQ_LEN), BF16),
            pltpu.VMEM(token, BF16),
            pltpu.VMEM((BLOCKS, GROUPS, WIDTH, UNITS), F32),
            pltpu.VMEM((GROUPS, WIDTH, QKV), F32),
            pltpu.VMEM((2, BLOCKS, WIDTH, UNITS), BF16),
            pltpu.VMEM((2, BLOCKS, WIDTH, UNITS), BF16),
            pltpu.VMEM((BLOCKS, WIDTH, UNITS), BF16),
            pltpu.VMEM((BLOCKS, WIDTH, UNITS), BF16),
            pltpu.VMEM((owners,) + piece, BF16),
            pltpu.VMEM((size,) + piece, BF16),
            pltpu.VMEM(piece, BF16),
            pltpu.VMEM((owners,) + piece, BF16),
            pltpu.VMEM((GROUPS - 1, WIDTH, QKV), BF16),
            pltpu.VMEM((GROUPS - 1, WIDTH, QKV), BF16),
            pltpu.VMEM((qowners,) + qpiece, BF16),
            pltpu.VMEM((size,) + qpiece, BF16),
            pltpu.VMEM(qpiece, BF16),
            pltpu.VMEM((qowners,) + qpiece, BF16),
            pltpu.VMEM((GROUPS, TABLE, WIDTH), F32),
            pltpu.VMEM((GROUPS, TABLE, WIDTH), F32),
            pltpu.VMEM((TABLE, WIDTH), F32),
            pltpu.VMEM((size, TABLE, WIDTH), F32),
            pltpu.VMEM((GROUPS, 8, WIDTH), F32),
            pltpu.VMEM((GROUPS, 8, WIDTH), F32),
            pltpu.VMEM((8, WIDTH), F32),
            pltpu.VMEM((size, 8, WIDTH), F32),
        ]
        + [dma((count, GROUPS))] * 8
        + [dma((4, GROUPS))] * 2
        + [dma((6, GROUPS))] * 2
        + [dma((6, size))] * 2
        + [dma((2,))] * 2,
        compiler_params=pltpu.CompilerParams(
            vmem_limit_bytes=63 << 20, collective_id=0, has_side_effects=True
        ),
    )(x, dy, seg, wqkv, wup, wdown, wout, params)


def local(
    size, layer_input, segment_ids, qkv_weight, qv_bias, out_weight, out_bias, gain_one, shift_one,
    up_weight, up_bias, down_weight, down_bias, gain_two, shift_two, out_grad,
):
    me = lax.axis_index("grp")

    def rows(a):
        return a.reshape(-1, WIDTH)

    def mine_of(a):
        return lax.dynamic_slice_in_dim(a, me * WIDTH, WIDTH, 0).reshape(1, WIDTH)

    params = jnp.concatenate(
        [rows(a) for a in (qv_bias, up_bias, down_bias, gain_two, shift_two)]
        + [mine_of(a) for a in (out_bias, gain_one, shift_one)]
        + [jnp.zeros((TABLE - COLS, WIDTH), F32)]
    )
    lo, dx, _, _, g_qkv, g_up, g_down, g_out, sums, shared = layer(
        size, layer_input, out_grad, segment_ids, qkv_weight, up_weight, down_weight, out_weight, params
    )
    return (
        lo.astype(F32),
        dx.astype(F32),
        g_qkv.astype(F32)[None],
        sums[Q_BIAS : V_BIAS + 1].reshape(1, 2 * WIDTH),
        g_out.astype(F32).reshape(D, D),
        shared[:, OUT_BIAS].reshape(D),
        shared[:, GAIN_ONE].reshape(D),
        shared[:, SHIFT_ONE].reshape(D),
        g_up.astype(F32)[None],
        sums[UP_BIAS:DOWN_BIAS].reshape(1, UNITS),
        g_down.astype(F32)[None],
        sums[DOWN_BIAS].reshape(1, WIDTH),
        sums[GAIN_TWO],
        sums[SHIFT_TWO],
    )


def solution(mesh):
    group = P("grp", None, None)
    data = P("rows", "grp", None)
    in_specs = (
        data, P("rows", None), group, P("grp", None), P(), P(), P(), P(),
        group, P("grp", None), group, P("grp", None), P("grp"), P("grp"), data,
    )
    out_specs = (
        data, data, group, P("grp", None), P(), P(), P(), P(),
        group, P("grp", None), group, P("grp", None), P("grp"), P("grp"),
    )
    return jax.shard_map(functools.partial(local, mesh.shape["rows"]), mesh=mesh, in_specs=in_specs, out_specs=out_specs, check_vma=False)
```

```python
import functools

import jax
import jax.numpy as jnp
from jax import lax
from jax.experimental import pallas as pl
from jax.experimental.pallas import tpu as pltpu
from jax.sharding import PartitionSpec as P

D = 768
HEAD_DIM = 64
SEQ_LEN = 512
GROUPS = 4
WIDTH = D // GROUPS
HEADS_GROUP = WIDTH // HEAD_DIM
HEADS = D // HEAD_DIM
QKV = 3 * WIDTH
UNITS = 768
PARTS = UNITS // WIDTH
PAD = HEAD_DIM + 16
MASKED = -1e30
EPS = 1e-05
SCALE = HEAD_DIM ** (-0.5)
BLOCKS = 3
HALF = UNITS // 2

F32 = jnp.float32
BF16 = jnp.bfloat16
MESH = pl.DeviceIdType.MESH

Q_BIAS, V_BIAS, UP_BIAS, DOWN_BIAS, GAIN_TWO, SHIFT_TWO, OUT_BIAS, GAIN_ONE, SHIFT_ONE = 0, 1, 2, 6, 7, 8, 9, 10, 11
COLS = 12
TABLE = 16

E_AT = 0
Q_AT = HEADS_GROUP * SEQ_LEN
K_AT = Q_AT + HEADS_GROUP * PAD
V_AT = K_AT + HEADS_GROUP * PAD
FWD_ROWS = V_AT + WIDTH
BWD_ROWS = 2 * WIDTH


def nn(a, b):
    return lax.dot_general(a, b, (((1,), (0,)), ((), ())), preferred_element_type=F32)


def nt(a, b):
    return lax.dot_general(a, b, (((1,), (1,)), ((), ())), preferred_element_type=F32)


def tn(a, b):
    return lax.dot_general(a, b, (((0,), (0,)), ((), ())), preferred_element_type=F32)


def lane_part(value):
    total = value[:, 0:128]
    for at in range(128, SEQ_LEN, 128):
        total = total + value[:, at : at + 128]
    return total


def channel_sum(value):
    return jnp.sum(value, axis=0, keepdims=True)


def fold(value):
    return jnp.sum(value.reshape(value.shape[0] // 8, 8, SEQ_LEN), axis=0)


def spread(column):
    return jnp.concatenate([column] * (SEQ_LEN // 128), axis=1)


def gelu_pair(u):
    half_erf = 0.5 * lax.erf(u * 0.7071067811865476) + 0.5
    density = jnp.exp(u * u * -0.5) * 0.3989422804014327
    return u * half_erf, half_erf + u * density


def flip(me, j):
    return (me + j) % 2 + 2 * ((me // 2 + j // 2) % 2)


def owners_of(rows, parts):
    return max(n for n in range(1, min(rows, parts) + 1) if parts % n == 0)


def layer_kernel(
    size, x_in, dy_in, seg, wqkv_in, wup_in, wdown_in, wout,
    qv_bias, up_bias, down_bias, gain_two, shift_two, out_bias, gain_one, shift_one,
    lo_out, dx_out, fwd_st, bwd_st, qkv_out, up_out, down_out, mix_out, sums_out, shared_out,
    x, dy, wqkv, wup, wdown, table, cols, wqkv_t, wup_t, wdown_t, wout_t, vec,
    fwd, bwd, middle_s, linv_s, ctx_s, summed_s, hidden_s, act_s, slope_s, summed2_s,
    up_grad_s, hidden_grad_s, qkv_grad_s, lo_s,
    acc, g_qkv, pair_t, pair_l, side_t, side_l, cut_t, cut_l, far_t, far_l, own_s, all_l,
    qpair_t, qpair_l, qfar_t, qfar_l, qpiece_t, qpiece_l, qcut_t, qcut_l, qall_l,
    sum_t, sum_l, sum_row_t, sum_row_l, end_t, end_l, end_row_t, end_row_l,
    s_x, r_x, s_dy, r_dy, s_lo, r_lo, s_dx, r_dx, s_w, r_w, s_one, r_one, s_row, r_row, s_fwd, s_bwd,
):
    count = x.shape[0]
    me = lax.axis_index("grp")
    row = lax.axis_index("rows")
    zero = jnp.zeros((8, SEQ_LEN), F32)

    def over(n, body, init=0, unroll=False):
        return lax.fori_loop(0, n, body, init, unroll=unroll)

    def each(n, body):
        def run(at, carry):
            body(at)
            return carry

        lax.fori_loop(0, n, run, 0)

    def remote(src, dst, send, recv, to):
        return pltpu.make_async_remote_copy(
            src_ref=src, dst_ref=dst, send_sem=send, recv_sem=recv, device_id={"grp": to}, device_id_type=MESH
        )

    half = row % 2
    beside = row + 1 - 2 * half

    def half_rows(at):
        return pl.ds(pl.multiple_of(at * (WIDTH // 2), WIDTH // 2), WIDTH // 2)

    mine_half, other_half = half_rows(half), half_rows(1 - half)

    def across(at, src, dst, j):
        return remote(src, dst, s_one.at[at], r_one.at[at], flip(me, j))

    def aside(at, src, dst):
        return pltpu.make_async_remote_copy(
            src_ref=src, dst_ref=dst, send_sem=s_one.at[at], recv_sem=r_one.at[at],
            device_id={"rows": beside}, device_id_type=MESH,
        )

    barrier = pltpu.get_barrier_semaphore()
    for j in range(1, GROUPS):
        pl.semaphore_signal(barrier, inc=1, device_id={"grp": flip(me, j)}, device_id_type=MESH)

    def greet(k):
        pl.semaphore_signal(barrier, inc=1, device_id={"rows": (row + k + 1) % size}, device_id_type=MESH)

    each(size - 1, greet)
    pl.semaphore_wait(barrier, GROUPS - 1 + size - 1)

    def move_in(src, dst, send, recv, i, j):
        to = flip(me, j)
        return remote(src.at[to * count + i], dst.at[i, me], send.at[i, j], recv.at[i, j], to)

    def start_in(src, dst, send, recv, i):
        for j in range(1, GROUPS):
            move_in(src, dst, send, recv, i, j).start()

    def own_in(src, dst, send, i):
        return pltpu.make_async_copy(src.at[me * count + i], dst.at[i, me], send.at[i, 0])

    weights = (None, (wqkv_in.at[0], wqkv), (wup_in.at[0], wup), (wdown_in.at[0], wdown))

    def own_weight(k):
        src, dst = weights[k]
        return pltpu.make_async_copy(src, dst.at[me], s_w.at[k, 0])

    def send_table(j):
        return remote(table.at[me], table.at[me], s_w.at[0, j], r_w.at[0, j], flip(me, j))

    def send_weight(k, j):
        src, dst = weights[k]
        if j == 1:
            return remote(src, dst.at[me], s_w.at[k, 1], r_w.at[k, 1], flip(me, 1))
        if j == 2 and k == 1:
            return remote(src, dst.at[me], s_w.at[k, 2], r_w.at[k, 2], flip(me, 2))
        if j == 2:
            part = weights[k][0].at[mine_half]
            return remote(part, dst.at[me, mine_half], s_w.at[k, 2], r_w.at[k, 2], flip(me, 2))
        got = dst.at[flip(me, 2)]
        return remote(got, got, s_w.at[k, 3], r_w.at[k, 3], flip(me, 1))

    def pass_weight(k, rows):
        block = weights[k][1].at[flip(me, 2), rows]
        return aside(30 + k, block, block)

    def got_weight(k, j):
        dst = weights[k][1]
        block = dst.at[flip(me, j)] if j != 2 or k == 1 else dst.at[flip(me, j), mine_half]
        remote(block, block, s_w.at[k, j], r_w.at[k, j], flip(me, 1)).wait_recv()

    for c in range(2):
        table[me, c : c + 1, :] = qv_bias[:, c * WIDTH : (c + 1) * WIDTH]
    for c in range(PARTS):
        table[me, UP_BIAS + c : UP_BIAS + c + 1, :] = up_bias[:, c * WIDTH : (c + 1) * WIDTH]
    table[me, DOWN_BIAS : DOWN_BIAS + 1, :] = down_bias[...]
    table[me, GAIN_TWO : GAIN_TWO + 1, :] = gain_two[...].reshape(1, WIDTH)
    table[me, SHIFT_TWO : SHIFT_TWO + 1, :] = shift_two[...].reshape(1, WIDTH)
    table[me, OUT_BIAS:TABLE, :] = jnp.zeros((TABLE - OUT_BIAS, WIDTH), F32)
    for j in (2, 3, 1):
        send_table(j).start()
    own_weight(1).start()
    send_weight(1, 2).start()
    send_weight(1, 1).start()
    own_in(x_in, x, s_x, 0).start()
    start_in(x_in, x, s_x, r_x, 0)
    for k in range(2, 4):
        own_weight(k).start()
        send_weight(k, 1).start()
    own_in(dy_in, dy, s_dy, 0).start()

    def own_rest(i):
        own_in(x_in, x, s_x, i + 1).start()
        own_in(dy_in, dy, s_dy, i + 1).start()

    each(count - 1, own_rest)

    g_qkv[...] = jnp.zeros_like(g_qkv)
    acc[...] = jnp.zeros_like(acc)
    vec[...] = jnp.zeros_like(vec)
    wout_t[...] = wout[...].T

    for j in range(1, GROUPS):
        block = table.at[flip(me, j)]
        remote(block, block, s_w.at[0, j], r_w.at[0, j], flip(me, j)).wait_recv()
    for g in range(GROUPS):
        vectors = [a[...].reshape(1, D)[:, g * WIDTH : (g + 1) * WIDTH] for a in (out_bias, gain_one, shift_one)]
        rows = jnp.concatenate([table[g, 0:OUT_BIAS, :]] + vectors + [jnp.zeros((TABLE - COLS, WIDTH), F32)])
        cols[g, :, 0:TABLE] = rows.T

    def col(g, at):
        return cols[g, :, at : at + 1]

    def add_sum(g, at, value):
        vec[g * COLS + at] += lane_part(value)

    def rows_of(g):
        return pl.ds(pl.multiple_of(g * WIDTH, WIDTH), WIDTH)

    def fwd_save(slot, i, g):
        return pltpu.make_async_copy(fwd.at[slot], fwd_st.at[i, g], s_fwd.at[slot])

    def bwd_save(slot, i, g):
        return pltpu.make_async_copy(bwd.at[slot], bwd_st.at[i, g], s_bwd.at[slot])

    def fwd_load(slot, i, g):
        return pltpu.make_async_copy(fwd_st.at[i, g], fwd.at[slot], s_fwd.at[slot])

    def bwd_load(slot, i, g):
        return pltpu.make_async_copy(bwd_st.at[i, g], bwd.at[slot], s_bwd.at[slot])

    def send_lo(i, j):
        to = flip(me, j)
        return remote(lo_s.at[to], lo_out.at[me * count + i], s_lo.at[i, j], r_lo.at[i, j], to)

    def own_lo(i):
        return pltpu.make_async_copy(lo_s.at[me], lo_out.at[me * count + i], s_lo.at[i, 0])

    def sequence(i):
        first = i == 0
        label = seg[pl.ds(me * count + i, 1), :]
        ids = lax.broadcasted_iota(jnp.int32, (16, SEQ_LEN), 0)
        hot = (ids == label).astype(F32)
        hot_k = hot.astype(BF16)
        hot_q = jnp.where(ids < 4, (1.0 - hot) * MASKED, 0.0).astype(BF16)

        def attend(j):
            g = flip(me, j)
            slot = j % 2

            @pl.when(j == 0)
            def _():
                own_in(x_in, x, s_x, i).wait()

            @pl.when(j > 0)
            def _():
                block = x.at[i, g]
                remote(block, block, s_x.at[i, j], r_x.at[i, j], g).wait_recv()

            @pl.when(first & (j == 0))
            def _():
                own_weight(1).wait()

            @pl.when(first & (j == 1))
            def _():
                got_weight(1, 1)

            @pl.when(first & (j == 2))
            def _():
                got_weight(1, 2)
                send_weight(1, 3).start()
                for k in range(2, 4):
                    send_weight(k, 2).start()

            @pl.when(first & (j == 3))
            def _():
                got_weight(1, 3)

            @pl.when(first)
            def _():
                wqkv_t[g] = wqkv[g].T

            @pl.when(i * GROUPS + j >= 2)
            def _():
                fwd_save(slot, 0, 0).wait()

            xg = x[i, g]
            q = (nn(wqkv_t[g, 0:WIDTH, :], xg) + col(g, Q_BIAS)).astype(BF16) * jnp.asarray(SCALE, BF16)
            k = nn(wqkv_t[g, WIDTH : 2 * WIDTH, :], xg).astype(BF16)
            v = (nn(wqkv_t[g, 2 * WIDTH :, :], xg) + col(g, V_BIAS)).astype(BF16)
            fwd[slot, V_AT:FWD_ROWS, :] = v
            for h in range(HEADS_GROUP):
                part = slice(h * HEAD_DIM, (h + 1) * HEAD_DIM)
                qh = jnp.concatenate([q[part], hot_q])
                kh = jnp.concatenate([k[part], hot_k])
                fwd[slot, Q_AT + h * PAD : Q_AT + (h + 1) * PAD, :] = qh
                fwd[slot, K_AT + h * PAD : K_AT + (h + 1) * PAD, :] = kh
                scores = tn(kh, qh)
                largest = jnp.max(scores, axis=0, keepdims=True)
                powers = jnp.exp(scores - largest)
                inverse = 1.0 / channel_sum(powers)
                e = powers.astype(BF16)
                fwd[slot, E_AT + h * SEQ_LEN : E_AT + (h + 1) * SEQ_LEN, :] = e
                linv_s[g * HEADS_GROUP + h] = inverse
                ctx_s[pl.ds(pl.multiple_of(g * WIDTH + h * HEAD_DIM, HEAD_DIM), HEAD_DIM), :] = (
                    nn(v[part], e) * inverse
                ).astype(BF16)
            fwd_save(slot, i, g).start()

        each(GROUPS, attend)

        @pl.when(first)
        def _():
            start_in(dy_in, dy, s_dy, r_dy, 0)
            for k in range(2, 4):
                got_weight(k, 2)
                pass_weight(k, mine_half).start()

        @pl.when(i + 1 < count)
        def _():
            start_in(x_in, x, s_x, r_x, i + 1)

        def mix(g, carry):
            total, square = carry
            branch = (nn(wout_t[rows_of(g), :], ctx_s[...]) + col(g, OUT_BIAS)).astype(BF16)
            summed = branch.astype(F32) + x[i, g].astype(F32)
            summed_s[g] = summed
            return total + fold(summed), square + fold(summed * summed)

        total, square = over(GROUPS, mix, (zero, zero))
        center1 = channel_sum(total) / D
        inverse1 = lax.rsqrt(channel_sum(square) / D - center1 * center1 + EPS)

        @pl.when(first)
        def _():
            for k in range(2, 4):
                own_weight(k).wait()
                got_weight(k, 1)
                pass_weight(k, other_half).wait_recv()
                send_weight(k, 3).start()
            for k in range(2, 4):
                got_weight(k, 3)

            def turn(g):
                wup_t[g] = wup[g].T
                wdown_t[g] = wdown[g].T

            each(GROUPS, turn)

        def feed(g, carry):
            total, square = carry
            normed = (summed_s[g] - center1) * inverse1
            hidden = (normed * col(g, GAIN_ONE) + col(g, SHIFT_ONE)).astype(BF16)
            hidden_s[g] = hidden
            for part in range(PARTS):
                rows = slice(part * WIDTH, (part + 1) * WIDTH)
                u = nn(wup_t[g, rows, :], hidden) + col(g, UP_BIAS + part)
                act, slope = gelu_pair(u)
                act_s[g, rows, :] = act.astype(BF16)
                slope_s[g, rows, :] = slope.astype(BF16)
            summed2 = hidden.astype(F32) + nn(wdown[g], act_s[g]) + col(g, DOWN_BIAS)
            summed2_s[g] = summed2
            return total + fold(summed2), square + fold(summed2 * summed2)

        total, square = over(GROUPS, feed, (zero, zero))
        center2 = channel_sum(total) / D
        inverse2 = lax.rsqrt(channel_sum(square) / D - center2 * center2 + EPS)

        @pl.when(i > 0)
        def _():
            own_lo(i - 1).wait()
            for j in range(1, GROUPS):
                send_lo(i - 1, j).wait_send()

        own_in(dy_in, dy, s_dy, i).wait()
        for j in range(1, GROUPS):
            block = dy.at[i, flip(me, j)]
            remote(block, block, s_dy.at[i, j], r_dy.at[i, j], flip(me, j)).wait_recv()

        @pl.when(i + 1 < count)
        def _():
            start_in(dy_in, dy, s_dy, r_dy, i + 1)

        def finish(g, carry):
            sum_e, sum_en = carry
            normed = (summed2_s[g] - center2) * inverse2
            gain = col(g, GAIN_TWO)
            lo_s[g] = (normed * gain + col(g, SHIFT_TWO)).astype(BF16)
            grad = dy[i, g].astype(F32)
            product = grad * normed
            add_sum(g, GAIN_TWO, product)
            add_sum(g, SHIFT_TWO, grad)
            summed2_s[g] = normed
            return sum_e + fold(grad * gain), sum_en + fold(product * gain)

        sum_e, sum_en = over(GROUPS, finish, (zero, zero))
        mean_e = channel_sum(sum_e) / D
        mean_en = channel_sum(sum_en) / D

        own_lo(i).start()
        for j in range(1, GROUPS):
            send_lo(i, j).start()

        def feed_back(g, carry):
            sum_h, sum_hn = carry
            normed2 = summed2_s[g]
            scaled = dy[i, g].astype(F32) * col(g, GAIN_TWO)
            grad2 = (inverse2 * (scaled - mean_e - normed2 * mean_en)).astype(BF16)
            wide = grad2.astype(F32)
            add_sum(g, DOWN_BIAS, wide)
            for part in range(PARTS):
                rows = slice(part * WIDTH, (part + 1) * WIDTH)
                up_grad = (nn(wdown_t[g, rows, :], grad2) * slope_s[g, rows, :].astype(F32)).astype(BF16)
                up_grad_s[rows, :] = up_grad
                add_sum(g, UP_BIAS + part, up_grad.astype(F32))
            acc[0, g] += nt(hidden_s[g], up_grad_s[...])
            acc[1, g] += nt(grad2, act_s[g])
            hidden_grad = (wide + nn(wup[g], up_grad_s[...])).astype(BF16)
            hidden_grad_s[rows_of(g), :] = hidden_grad
            grad1 = hidden_grad.astype(F32)
            normed1 = (summed_s[g] - center1) * inverse1
            product = grad1 * normed1
            gain = col(g, GAIN_ONE)
            add_sum(g, GAIN_ONE, product)
            add_sum(g, SHIFT_ONE, grad1)
            return sum_h + fold(grad1 * gain), sum_hn + fold(product * gain)

        sum_h, sum_hn = over(GROUPS, feed_back, (zero, zero))
        mean_h = channel_sum(sum_h) / D
        mean_hn = channel_sum(sum_hn) / D

        def norm_back(g):
            normed1 = (summed_s[g] - center1) * inverse1
            scaled = hidden_grad_s[rows_of(g), :].astype(F32) * col(g, GAIN_ONE)
            summed_grad = (inverse1 * (scaled - mean_h - normed1 * mean_hn)).astype(BF16)
            hidden_grad_s[rows_of(g), :] = summed_grad
            add_sum(g, OUT_BIAS, summed_grad.astype(F32))

        each(GROUPS, norm_back)

        def mix_back(g):
            slot = g % 2

            @pl.when(i * GROUPS + g >= 2)
            def _():
                bwd_save(slot, 0, 0).wait()

            ctx = ctx_s[rows_of(g), :]
            acc[2, g] += nt(ctx, hidden_grad_s[...])
            ctx_grad = nn(wout[rows_of(g), :], hidden_grad_s[...]).astype(BF16).astype(F32)
            for h in range(HEADS_GROUP):
                part = slice(h * HEAD_DIM, (h + 1) * HEAD_DIM)
                grad = (ctx_grad[part] * linv_s[g * HEADS_GROUP + h]).astype(BF16)
                bwd[slot, h * HEAD_DIM : (h + 1) * HEAD_DIM, :] = grad
                middle_s[i * HEADS + g * HEADS_GROUP + h] = channel_sum(grad.astype(F32) * ctx[part].astype(F32))
            bwd[slot, WIDTH:BWD_ROWS, :] = hidden_grad_s[rows_of(g), :]
            bwd_save(slot, i, g).start()

        each(GROUPS, mix_back)

    each(count, sequence)
    for slot in range(2):
        fwd_save(slot, 0, 0).wait()
        bwd_save(slot, 0, 0).wait()

    def unit_of(u):
        return u % count, GROUPS - 1 - u // count

    def load(u):
        i, j = unit_of(u)
        g = flip(me, j)
        fwd_load(u % 2, i, g).start()
        bwd_load(u % 2, i, g).start()

    def send_dx(i, j):
        to = flip(me, j)
        return remote(x.at[i, to], dx_out.at[me * count + i], s_dx.at[i, j], r_dx.at[i, j], to)

    def own_dx(i):
        return pltpu.make_async_copy(x.at[i, me], dx_out.at[me * count + i], s_dx.at[i, 0])

    def when(condition, body):
        if condition is True:
            body()
        else:
            pl.when(condition)(body)

    depth = size // 2
    level = row // 2
    owners = all_l.shape[1]
    per_half = owners // 2
    cut = WIDTH // 2 // per_half
    pair_groups = (flip(me, 1), flip(me, 3))
    kept = (me, flip(me, 2))
    outs = (up_out, down_out, None)

    def peers(n, body):
        def run(k):
            body(k + 1)

        each(n - 1, run)

    def along(kind, src, dst, k, sided):
        to = (level + k) % depth * 2 + half if sided else (row + k) % size
        return pltpu.make_async_remote_copy(
            src_ref=src, dst_ref=dst, send_sem=s_row.at[kind, k], recv_sem=r_row.at[kind, k],
            device_id={"rows": to}, device_id_type=MESH,
        )

    def line(sided):
        return (depth, level) if sided else (size, row)

    def capped(at, n, length):
        return at if n == length else jnp.minimum(at, n - 1)

    def owns(at, n, length):
        return True if n == length else at < n

    def scatter(kind, parts, landing, sided, act):
        n = parts.shape[0]
        length, here = line(sided)

        def one(k):
            to = (here + k) % length
            piece = parts.at[capped(to, n, length)]
            when(owns(to, n, length), lambda: act(along(kind, piece, landing.at[k], k, sided)))

        peers(length, one)

    def scatter_got(kind, parts, landing, sided):
        peers(line(sided)[0], lambda k: along(kind, parts.at[0], landing.at[k], k, sided).wait_recv())

    def spread_out(kind, landing, sided, act):
        n = landing.shape[0]
        length, here = line(sided)
        own = landing.at[capped(here, n, length)]
        when(owns(here, n, length), lambda: peers(length, lambda k: act(along(kind, own, own, k, sided))))

    def spread_got(kind, landing, sided):
        n = landing.shape[0]
        length, here = line(sided)
        peers(
            length,
            lambda k: when(
                owns((here + length - k) % length, n, length),
                lambda: along(kind, landing.at[0], landing.at[0], k, sided).wait_recv(),
            ),
        )

    def start(copy):
        copy.start()

    def sent(copy):
        copy.wait_send()

    def pair_copy(b):
        return across(b, pair_t.at[b], pair_l.at[b], 1)

    def side_copy(b):
        return aside(3 + b, side_t.at[b], side_l.at[b])

    def far_copy(b):
        return across(6 + b, far_t.at[b], far_l.at[b], 2)

    def out_copy(b, rows):
        return aside(9 + b, outs[b].at[rows], outs[b].at[rows])

    def pair_send(b):
        for at in range(2):
            pair_t[b, at] = acc[b, pair_groups[at]].astype(BF16)
        pair_copy(b).start()

    def side_send(b):
        pair_copy(b).wait_recv()
        for at in range(2):
            acc[b, kept[at]] += pair_l[b, at].astype(F32)
            side_t[b, at] = acc[b, kept[at], other_half, :].astype(BF16)
        side_copy(b).start()

    def cut_send(b):
        side_copy(b).wait_recv()
        for at in range(2):
            total = acc[b, kept[at], mine_half, :] + side_l[b, at].astype(F32)
            for o in range(owners):
                rows = o % per_half * cut
                lanes = o // per_half * HALF
                cut_t[b, o, at] = total[rows : rows + cut, lanes : lanes + HALF].astype(BF16)
        scatter(b, cut_t.at[b], cut_l.at[b], True, start)

    def far_send(b):
        def close():
            scatter_got(b, cut_t.at[b], cut_l.at[b], True)
            own = capped(level, owners, depth)
            total = [cut_t[b, own, at].astype(F32) for at in range(2)]
            for k in range(1, depth):
                total = [total[at] + cut_l[b, k, at].astype(F32) for at in range(2)]
            own_s[b] = total[0]
            far_t[b] = total[1].astype(BF16)
            far_copy(b).start()

        when(owns(level, owners, depth), close)

    def all_send(b):
        def close():
            far_copy(b).wait_recv()
            all_l[b, capped(level, owners, depth)] = (own_s[b] + far_l[b].astype(F32)).astype(BF16)

        when(owns(level, owners, depth), close)
        spread_out(3 + b, all_l.at[b], True, start)

    def joined(b):
        spread_got(3 + b, all_l.at[b], True)
        sides = [
            jnp.concatenate([all_l[b, side * per_half + o] for o in range(per_half)]) for side in range(2)
        ]
        return jnp.concatenate(sides, axis=1)

    def out_send(b):
        outs[b][mine_half, :] = joined(b)
        out_copy(b, mine_half).start()

    def mix_part(g, rows):
        return mix_out.at[g, rows]

    def mix_far(g):
        return across(12, mix_part(g, mine_half), mix_part(g, mine_half), 2)

    def mix_beside(at, rows):
        return aside(13 + at, mix_part(kept[at], rows), mix_part(kept[at], rows))

    def mix_core(at, g):
        return across(15 + at, mix_out.at[g], mix_out.at[g], 1)

    def mix_far_send():
        mix_out[me, mine_half, :] = joined(2)
        mix_far(me).start()
        mix_beside(0, mine_half).start()

    def mix_beside_send():
        mix_far(flip(me, 2)).wait_recv()
        mix_beside(1, mine_half).start()

    def mix_core_send():
        for at in range(2):
            mix_beside(at, other_half).wait_recv()
            mix_core(at, kept[at]).start()

    def early_copy(j):
        return across(17 + j, sum_t.at[flip(me, j)], sum_l.at[j], j)

    def shared_copy(j):
        return across(20 + j, shared_out.at[me], shared_out.at[me], j)

    def end_copy(j):
        return across(23 + j, end_t.at[j], end_l.at[j], j)

    def lane_rows(g, columns):
        return [jnp.sum(vec[g * COLS + c].T, axis=0, keepdims=True) for c in columns]

    def early_send():
        for g in range(GROUPS):
            zeros = [jnp.zeros((1, WIDTH), F32)] * 2
            rows = zeros + lane_rows(g, range(UP_BIAS, COLS)) + zeros * ((TABLE - COLS) // 2)
            sum_t[g] = jnp.concatenate(rows)
        for j in range(1, GROUPS):
            early_copy(j).start()

    def early_row_send():
        total = sum_t[me]
        for j in range(1, GROUPS):
            early_copy(j).wait_recv()
            total = total + sum_l[j]
        sum_row_t[...] = total
        peers(size, lambda k: along(8, sum_row_t, sum_row_l.at[k], k, False).start())

    def shared_send():
        total = sum_row_t[...]
        peers(size, lambda k: along(8, sum_row_t, sum_row_l.at[k], k, False).wait_recv())
        for k in range(1, size):
            total = total + sum_row_l[k]
        sums_out[...] = total
        shared_out[me] = total
        for j in range(1, GROUPS):
            shared_copy(j).start()

    qowners = qall_l.shape[0]
    qcut = WIDTH // qowners

    def qpair_copy(at):
        return across(27 + at, qpair_t.at[at], qpair_l.at[at], 1)

    def qpiece_copy():
        return across(29, qpiece_t, qpiece_l, 2)

    def qpair_send(at, j):
        qpair_t[at] = g_qkv[flip(me, j)].astype(BF16)
        qpair_copy(at).start()

    def qpieces(at, g, parts, landing, kind):
        qpair_copy(at).wait_recv()
        for o in range(qowners):
            rows = slice(o * qcut, (o + 1) * qcut)
            parts[o] = (g_qkv[g, rows, :] + qpair_l[at, rows, :].astype(F32)).astype(BF16)
        scatter(kind, parts, landing, False, start)

    def qtotal(parts, landing, kind):
        scatter_got(kind, parts, landing, False)
        total = parts[capped(row, qowners, size)].astype(F32)
        for k in range(1, size):
            total = total + landing[k].astype(F32)
        return total

    def qfar_send():
        qpieces(0, flip(me, 2), qfar_t, qfar_l, 6)

    def qpiece_send():
        def close():
            qpiece_t[...] = qtotal(qfar_t, qfar_l, 6).astype(BF16)
            qpiece_copy().start()

        when(owns(row, qowners, size), close)

    def end_sums(g):
        return jnp.concatenate(lane_rows(g, (Q_BIAS, V_BIAS)) + [jnp.zeros((6, WIDTH), F32)])

    def qcut_send():
        qpieces(1, me, qcut_t, qcut_l, 7)
        sums = end_sums(me)
        for j in range(1, GROUPS):
            end_copy(j).wait_recv()
            sums = sums + end_l[j]
        end_row_t[...] = sums
        peers(size, lambda k: along(9, end_row_t, end_row_l.at[k], k, False).start())

    def qall_send():
        def close():
            total = qtotal(qcut_t, qcut_l, 7)
            qpiece_copy().wait_recv()
            qall_l[capped(row, qowners, size)] = (total + qpiece_l[...].astype(F32)).astype(BF16)

        when(owns(row, qowners, size), close)
        spread_out(10, qall_l, False, start)

    def qclose():
        peers(size, lambda k: along(9, end_row_t, end_row_l.at[k], k, False).wait_recv())
        sums = end_row_t[...]
        for k in range(1, size):
            sums = sums + end_row_l[k]
        sums_out[0:2, :] = sums[0:2]
        spread_got(10, qall_l, False)
        for o in range(qowners):
            qkv_out[o * qcut : (o + 1) * qcut, :] = qall_l[o]

    UP, DOWN, MIX = 0, 1, 2
    plan = {
        1: [lambda: side_send(MIX), early_row_send],
        2: [lambda: side_send(UP)],
        4: [lambda: qpair_send(0, 3), lambda: side_send(DOWN)],
        5: [lambda: cut_send(MIX), shared_send],
        7: [lambda: cut_send(UP)],
        8: [qfar_send],
        9: [lambda: far_send(MIX), lambda: cut_send(DOWN)],
        11: [lambda: all_send(MIX), lambda: far_send(UP)],
        12: [lambda: qpair_send(1, 1), lambda: all_send(UP)],
        13: [qpiece_send, lambda: far_send(DOWN), mix_far_send],
        14: [lambda: out_send(UP), lambda: all_send(DOWN)],
        15: [mix_beside_send],
    }

    def follow(u):
        for at, steps in plan.items():

            @pl.when(u == count * GROUPS * at // 16 - 1)
            def _():
                for step in steps:
                    step()

    load(0)
    for b in (MIX, UP, DOWN):
        pair_send(b)
    early_send()

    def unit(u):
        i, j = unit_of(u)
        g = flip(me, j)
        slot = u % 2
        fwd_load(slot, i, g).wait()
        bwd_load(slot, i, g).wait()

        @pl.when(u + 1 < count * GROUPS)
        def _():
            load(u + 1)

        for h in range(HEADS_GROUP):
            e = fwd[slot, E_AT + h * SEQ_LEN : E_AT + (h + 1) * SEQ_LEN, :]
            q = fwd[slot, Q_AT + h * PAD : Q_AT + h * PAD + HEAD_DIM, :]
            k = fwd[slot, K_AT + h * PAD : K_AT + h * PAD + HEAD_DIM, :]
            v = fwd[slot, V_AT + h * HEAD_DIM : V_AT + (h + 1) * HEAD_DIM, :]
            grad = bwd[slot, h * HEAD_DIM : (h + 1) * HEAD_DIM, :]
            prob_grad = tn(v, grad)
            score_grad = (e.astype(F32) * (prob_grad - middle_s[i * HEADS + g * HEADS_GROUP + h])).astype(BF16)
            at = h * HEAD_DIM
            qkv_grad_s[2 * WIDTH + at : 2 * WIDTH + at + HEAD_DIM, :] = nt(grad, e).astype(BF16)
            qkv_grad_s[at : at + HEAD_DIM, :] = (nn(k, score_grad) * SCALE).astype(BF16)
            qkv_grad_s[WIDTH + at : WIDTH + at + HEAD_DIM, :] = nt(q, score_grad).astype(BF16)
        g_qkv[g] += nt(x[i, g], qkv_grad_s[...])
        add_sum(g, Q_BIAS, qkv_grad_s[0:WIDTH, :].astype(F32))
        add_sum(g, V_BIAS, qkv_grad_s[2 * WIDTH :, :].astype(F32))
        into = bwd[slot, WIDTH:BWD_ROWS, :].astype(F32) + nn(wqkv[g], qkv_grad_s[...])
        x[i, g] = into.astype(BF16)

        @pl.when((j > 0) & (i == count - 1))
        def _():
            end_t[j] = end_sums(g)
            end_copy(j).start()

        @pl.when(j > 0)
        def _():
            send_dx(i, j).start()

        @pl.when(j == 0)
        def _():
            own_dx(i).start()

        follow(u)

    each(count * GROUPS, unit)
    qcut_send()
    out_send(DOWN)
    mix_core_send()
    qall_send()
    for j in range(1, GROUPS):
        block = shared_out.at[flip(me, j)]
        across(20 + j, block, block, j).wait_recv()
    for b in (UP, DOWN):
        out_copy(b, other_half).wait_recv()
    for at, j in enumerate((1, 3)):
        mix_core(at, flip(me, j)).wait_recv()
    qclose()

    for j in range(1, GROUPS):
        send_table(j).wait_send()
        for k in range(1, 4):
            send_weight(k, j).wait_send()
    for k in range(2, 4):
        pass_weight(k, mine_half).wait_send()
    own_lo(count - 1).wait()
    for j in range(1, GROUPS):
        send_lo(count - 1, j).wait_send()

    def drain(i):
        own_dx(i).wait()
        for j in range(1, GROUPS):
            move_in(x_in, x, s_x, r_x, i, j).wait_send()
            move_in(dy_in, dy, s_dy, r_dy, i, j).wait_send()
            send_lo(i, j).wait_recv()
            send_dx(i, j).wait_send()
            send_dx(i, j).wait_recv()

    each(count, drain)
    for b in range(BLOCKS):
        pair_copy(b).wait_send()
        side_copy(b).wait_send()
        scatter(b, cut_t.at[b], cut_l.at[b], True, sent)
        when(owns(level, owners, depth), lambda: far_copy(b).wait_send())
        spread_out(3 + b, all_l.at[b], True, sent)
    for b in (UP, DOWN):
        out_copy(b, mine_half).wait_send()
    mix_far(me).wait_send()
    for at in range(2):
        mix_beside(at, mine_half).wait_send()
        mix_core(at, kept[at]).wait_send()
        qpair_copy(at).wait_send()
    when(owns(row, qowners, size), lambda: qpiece_copy().wait_send())
    for j in range(1, GROUPS):
        early_copy(j).wait_send()
        shared_copy(j).wait_send()
        end_copy(j).wait_send()
    scatter(6, qfar_t, qfar_l, False, sent)
    scatter(7, qcut_t, qcut_l, False, sent)
    spread_out(10, qall_l, False, sent)
    peers(size, lambda k: along(8, sum_row_t, sum_row_l.at[k], k, False).wait_send())
    peers(size, lambda k: along(9, end_row_t, end_row_l.at[k], k, False).wait_send())


def layer(size, x, dy, *rest):
    count = x.shape[0] // GROUPS
    here = pl.BlockSpec(memory_space=pl.ANY)
    vmem = pl.BlockSpec(memory_space=pltpu.VMEM)
    grads = [
        ((WIDTH, QKV), BF16),
        ((WIDTH, UNITS), BF16),
        ((WIDTH, UNITS), BF16),
        ((GROUPS, WIDTH, UNITS), BF16),
        ((TABLE, WIDTH), F32),
        ((GROUPS, TABLE, WIDTH), F32),
    ]
    depth = size // 2
    owners = 2 * owners_of(depth // 2, WIDTH // 32)
    piece = (WIDTH // owners, HALF)
    qowners = owners_of(size, WIDTH // 16)
    qpiece = (WIDTH // qowners, QKV)
    token = (GROUPS, WIDTH, SEQ_LEN)
    dma = pltpu.SemaphoreType.DMA
    return pl.pallas_call(
        functools.partial(layer_kernel, size),
        out_shape=[jax.ShapeDtypeStruct(x.shape, BF16)] * 2
        + [
            jax.ShapeDtypeStruct((count, GROUPS, FWD_ROWS, SEQ_LEN), BF16),
            jax.ShapeDtypeStruct((count, GROUPS, BWD_ROWS, SEQ_LEN), BF16),
        ]
        + [jax.ShapeDtypeStruct(s, t) for s, t in grads],
        in_specs=[here, here, vmem, here, here, here] + [vmem] * 9,
        out_specs=[here] * 4 + [vmem] * len(grads),
        scratch_shapes=[
            pltpu.VMEM((count,) + token, BF16),
            pltpu.VMEM((count,) + token, BF16),
            pltpu.VMEM((GROUPS, WIDTH, QKV), BF16),
            pltpu.VMEM((GROUPS, WIDTH, UNITS), BF16),
            pltpu.VMEM((GROUPS, WIDTH, UNITS), BF16),
            pltpu.VMEM((GROUPS, TABLE, WIDTH), F32),
            pltpu.VMEM((GROUPS, WIDTH, 128), F32),
            pltpu.VMEM((GROUPS, QKV, WIDTH), BF16),
            pltpu.VMEM((GROUPS, UNITS, WIDTH), BF16),
            pltpu.VMEM((GROUPS, UNITS, WIDTH), BF16),
            pltpu.VMEM((D, D), BF16),
            pltpu.VMEM((GROUPS * COLS, WIDTH, 128), F32),
            pltpu.VMEM((2, FWD_ROWS, SEQ_LEN), BF16),
            pltpu.VMEM((2, BWD_ROWS, SEQ_LEN), BF16),
            pltpu.VMEM((count * HEADS, 1, SEQ_LEN), F32),
            pltpu.VMEM((HEADS, 1, SEQ_LEN), F32),
            pltpu.VMEM((D, SEQ_LEN), BF16),
            pltpu.VMEM(token, F32),
            pltpu.VMEM(token, BF16),
            pltpu.VMEM((GROUPS, UNITS, SEQ_LEN), BF16),
            pltpu.VMEM((GROUPS, UNITS, SEQ_LEN), BF16),
            pltpu.VMEM(token, F32),
            pltpu.VMEM((UNITS, SEQ_LEN), BF16),
            pltpu.VMEM((D, SEQ_LEN), BF16),
            pltpu.VMEM((QKV, SEQ_LEN), BF16),
            pltpu.VMEM(token, BF16),
            pltpu.VMEM((BLOCKS, GROUPS, WIDTH, UNITS), F32),
            pltpu.VMEM((GROUPS, WIDTH, QKV), F32),
            pltpu.VMEM((BLOCKS, 2, WIDTH, UNITS), BF16),
            pltpu.VMEM((BLOCKS, 2, WIDTH, UNITS), BF16),
            pltpu.VMEM((BLOCKS, 2, WIDTH // 2, UNITS), BF16),
            pltpu.VMEM((BLOCKS, 2, WIDTH // 2, UNITS), BF16),
            pltpu.VMEM((BLOCKS, owners, 2) + piece, BF16),
            pltpu.VMEM((BLOCKS, depth, 2) + piece, BF16),
            pltpu.VMEM((BLOCKS,) + piece, BF16),
            pltpu.VMEM((BLOCKS,) + piece, BF16),
            pltpu.VMEM((BLOCKS,) + piece, F32),
            pltpu.VMEM((BLOCKS, owners) + piece, BF16),
            pltpu.VMEM((2, WIDTH, QKV), BF16),
            pltpu.VMEM((2, WIDTH, QKV), BF16),
            pltpu.VMEM((qowners,) + qpiece, BF16),
            pltpu.VMEM((size,) + qpiece, BF16),
            pltpu.VMEM(qpiece, BF16),
            pltpu.VMEM(qpiece, BF16),
            pltpu.VMEM((qowners,) + qpiece, BF16),
            pltpu.VMEM((size,) + qpiece, BF16),
            pltpu.VMEM((qowners,) + qpiece, BF16),
            pltpu.VMEM((GROUPS, TABLE, WIDTH), F32),
            pltpu.VMEM((GROUPS, TABLE, WIDTH), F32),
            pltpu.VMEM((TABLE, WIDTH), F32),
            pltpu.VMEM((size, TABLE, WIDTH), F32),
            pltpu.VMEM((GROUPS, 8, WIDTH), F32),
            pltpu.VMEM((GROUPS, 8, WIDTH), F32),
            pltpu.VMEM((8, WIDTH), F32),
            pltpu.VMEM((size, 8, WIDTH), F32),
        ]
        + [dma((count, GROUPS))] * 8
        + [dma((4, GROUPS))] * 2
        + [dma((34,))] * 2
        + [dma((11, size))] * 2
        + [dma((2,))] * 2,
        compiler_params=pltpu.CompilerParams(
            vmem_limit_bytes=63 << 20, collective_id=0, has_side_effects=True
        ),
    )(x, dy, *rest)


def local(
    size, layer_input, segment_ids, qkv_weight, qv_bias, out_weight, out_bias, gain_one, shift_one,
    up_weight, up_bias, down_weight, down_bias, gain_two, shift_two, out_grad,
):
    lo, dx, _, _, *grads = layer(
        size, layer_input, out_grad, segment_ids, qkv_weight, up_weight, down_weight, out_weight,
        qv_bias, up_bias, down_bias, gain_two, shift_two, out_bias, gain_one, shift_one,
    )
    lo, dx, g_qkv, g_up, g_down, g_out, qv, out_b, gain1, shift1, up_b, down_b, gain2, shift2 = widen(lo, dx, *grads)
    return lo, dx, g_qkv, qv, g_out, out_b, gain1, shift1, g_up, up_b, g_down, down_b, gain2, shift2


def widen_kernel(
    lo, dx, qkv, up, down, mix, sums, shared,
    lo_o, dx_o, qkv_o, up_o, down_o, mix_o, qv_o, out_o, gain1_o, shift1_o, up_b_o, down_b_o, gain2_o, shift2_o,
):
    for src, out in ((lo, lo_o), (dx, dx_o), (qkv, qkv_o), (up, up_o), (down, down_o), (mix, mix_o)):
        out[...] = src[...].astype(F32).reshape(out.shape)

    @pl.when(pl.program_id(0) == 0)
    def _():
        def own(first, n):
            return jnp.concatenate([sums[first + c : first + c + 1, :] for c in range(n)], axis=1)

        def joint(at):
            return jnp.concatenate([shared[g, at : at + 1, :] for g in range(GROUPS)], axis=1)

        qv_o[...] = own(Q_BIAS, 2)
        up_b_o[...] = own(UP_BIAS, PARTS)
        down_b_o[...] = own(DOWN_BIAS, 1)
        gain2_o[...] = own(GAIN_TWO, 1).reshape(WIDTH)
        shift2_o[...] = own(SHIFT_TWO, 1).reshape(WIDTH)
        for out, at in ((out_o, OUT_BIAS), (gain1_o, GAIN_ONE), (shift1_o, SHIFT_ONE)):
            out[...] = joint(at).reshape(D)


def widen(lo, dx, *grads):
    steps = 8
    part = WIDTH // steps
    data = pl.BlockSpec((lo.shape[0] // steps, WIDTH, SEQ_LEN), lambda i: (i, 0, 0))

    def slab(columns):
        return pl.BlockSpec((part, columns), lambda i: (i, 0)), pl.BlockSpec((1, part, columns), lambda i: (0, i, 0))

    def whole(shape):
        return pl.BlockSpec(shape, lambda i: (0,) * len(shape), pipeline_mode=pl.Buffered(1))

    qkv_in, qkv_out = slab(QKV)
    unit_in, unit_out = slab(UNITS)
    mix_in = pl.BlockSpec((1, WIDTH // 2, D), lambda i: (i // 2, i % 2, 0))
    mix_out = pl.BlockSpec((WIDTH // 2, D), lambda i: (i, 0))
    wide = [(1, WIDTH, QKV), (1, WIDTH, UNITS), (1, WIDTH, UNITS), (D, D)]
    vectors = [(1, 2 * WIDTH), (D,), (D,), (D,), (1, UNITS), (1, WIDTH), (WIDTH,), (WIDTH,)]
    return pl.pallas_call(
        widen_kernel,
        grid=(steps,),
        out_shape=[jax.ShapeDtypeStruct(s, F32) for s in [lo.shape, dx.shape] + wide + vectors],
        in_specs=[data, data, qkv_in, unit_in, unit_in, mix_in] + [whole(a.shape) for a in grads[4:]],
        out_specs=[data, data, qkv_out, unit_out, unit_out, mix_out] + [whole(s) for s in vectors],
        compiler_params=pltpu.CompilerParams(vmem_limit_bytes=62 << 20),
    )(lo, dx, *grads)


def solution(mesh):
    group = P("grp", None, None)
    data = P("rows", "grp", None)
    in_specs = (
        data, P("rows", None), group, P("grp", None), P(), P(), P(), P(),
        group, P("grp", None), group, P("grp", None), P("grp"), P("grp"), data,
    )
    out_specs = (
        data, data, group, P("grp", None), P(), P(), P(), P(),
        group, P("grp", None), group, P("grp", None), P("grp"), P("grp"),
    )
    return jax.shard_map(functools.partial(local, mesh.shape["rows"]), mesh=mesh, in_specs=in_specs, out_specs=out_specs, check_vma=False)
```

```python
import functools

import jax
import jax.numpy as jnp
from jax import lax
from jax.experimental import pallas as pl
from jax.experimental.pallas import tpu as pltpu
from jax.sharding import PartitionSpec as P

D = 768
HEAD_DIM = 64
SEQ_LEN = 512
GROUPS = 4
WIDTH = D // GROUPS
HEADS_GROUP = WIDTH // HEAD_DIM
HEADS = D // HEAD_DIM
QKV = 3 * WIDTH
UNITS = 768
PARTS = UNITS // WIDTH
PAD = HEAD_DIM + 16
MASKED = -1e30
EPS = 1e-05
SCALE = HEAD_DIM ** (-0.5)
BLOCKS = 3
EARLY = 2
HALF = UNITS // 2

F32 = jnp.float32
BF16 = jnp.bfloat16
MESH = pl.DeviceIdType.MESH

Q_BIAS, V_BIAS, UP_BIAS, DOWN_BIAS, GAIN_TWO, SHIFT_TWO, OUT_BIAS, GAIN_ONE, SHIFT_ONE = 0, 1, 2, 6, 7, 8, 9, 10, 11
COLS = 12
LANE_COLS = COLS - PARTS
TABLE = 16

E_AT = 0
Q_AT = HEADS_GROUP * SEQ_LEN
K_AT = Q_AT + HEADS_GROUP * PAD
V_AT = K_AT + HEADS_GROUP * PAD
FWD_ROWS = V_AT + WIDTH
BWD_ROWS = 2 * WIDTH


def nn(a, b):
    return lax.dot_general(a, b, (((1,), (0,)), ((), ())), preferred_element_type=F32)


def nt(a, b):
    return lax.dot_general(a, b, (((1,), (1,)), ((), ())), preferred_element_type=F32)


def tn(a, b):
    return lax.dot_general(a, b, (((0,), (0,)), ((), ())), preferred_element_type=F32)


def lane_part(value):
    total = value[:, 0:128]
    for at in range(128, SEQ_LEN, 128):
        total = total + value[:, at : at + 128]
    return total


def channel_sum(value):
    return jnp.sum(value, axis=0, keepdims=True)


def fold(value):
    return jnp.sum(value.reshape(value.shape[0] // 8, 8, SEQ_LEN), axis=0)


def spread(column):
    return jnp.concatenate([column] * (SEQ_LEN // 128), axis=1)


def gelu_pair(u):
    half_erf = 0.5 * lax.erf(u * 0.7071067811865476) + 0.5
    density = jnp.exp(u * u * -0.5) * 0.3989422804014327
    return u * half_erf, half_erf + u * density


def flip(me, j):
    return (me + j) % 2 + 2 * ((me // 2 + j // 2) % 2)


def owners_of(rows, parts):
    return max(n for n in range(1, min(rows, parts) + 1) if parts % n == 0)


def layer_kernel(
    size, x_in, dy_in, seg, wqkv_in, wup_in, wdown_in, wout,
    qv_bias, up_bias, down_bias, gain_two, shift_two, out_bias, gain_one, shift_one,
    lo_out, dx_out, fwd_st, bwd_st, qkv_out, up_out, down_out, mix_out, sums_out, shared_out,
    x, dy, wqkv, wup, wdown, table, cols, wqkv_t, wup_t, wdown_t, wout_t, vec, up_sum,
    fwd, bwd, middle_s, linv_s, ctx_s, summed_s, hidden_s, act_s, slope_s, summed2_s,
    up_grad_s, hidden_grad_s, lo_s,
    acc, g_qkv, pair_t, pair_l, side_t, side_l, cut_t, cut_l, far_t, far_l, all_l,
    qpair_t, qpair_l, qfar_t, qfar_l, qpiece_t, qpiece_l, qcut_t, qcut_l, qall_l,
    sum_t, sum_l, sum_row_t, sum_row_l, end_t, end_l, end_row_t, end_row_l,
    s_x, r_x, s_dy, r_dy, s_lo, r_lo, s_dx, r_dx, s_w, r_w, s_one, r_one, s_row, r_row, s_fwd, s_bwd,
):
    count = x.shape[0]
    early = ctx_s.shape[0]
    me = lax.axis_index("grp")
    row = lax.axis_index("rows")
    zero = jnp.zeros((8, SEQ_LEN), F32)

    def over(n, body, init=0, unroll=False):
        return lax.fori_loop(0, n, body, init, unroll=unroll)

    def each(n, body):
        def run(at, carry):
            body(at)
            return carry

        lax.fori_loop(0, n, run, 0)

    def remote(src, dst, send, recv, to):
        return pltpu.make_async_remote_copy(
            src_ref=src, dst_ref=dst, send_sem=send, recv_sem=recv, device_id={"grp": to}, device_id_type=MESH
        )

    half = row % 2
    beside = row + 1 - 2 * half

    def half_rows(at):
        return pl.ds(pl.multiple_of(at * (WIDTH // 2), WIDTH // 2), WIDTH // 2)

    mine_half, other_half = half_rows(half), half_rows(1 - half)

    def across(at, src, dst, j):
        return remote(src, dst, s_one.at[at], r_one.at[at], flip(me, j))

    def aside(at, src, dst):
        return pltpu.make_async_remote_copy(
            src_ref=src, dst_ref=dst, send_sem=s_one.at[at], recv_sem=r_one.at[at],
            device_id={"rows": beside}, device_id_type=MESH,
        )

    barrier = pltpu.get_barrier_semaphore()
    for j in range(1, GROUPS):
        pl.semaphore_signal(barrier, inc=1, device_id={"grp": flip(me, j)}, device_id_type=MESH)

    def greet(k):
        pl.semaphore_signal(barrier, inc=1, device_id={"rows": (row + k + 1) % size}, device_id_type=MESH)

    each(size - 1, greet)
    pl.semaphore_wait(barrier, GROUPS - 1 + size - 1)

    def move_in(src, dst, send, recv, i, j):
        to = flip(me, j)
        return remote(src.at[to * count + i], dst.at[i, me], send.at[i, j], recv.at[i, j], to)

    def start_in(src, dst, send, recv, i):
        for j in (2, 3):
            move_in(src, dst, send, recv, i, j).start()

    def own_in(src, dst, send, i):
        return pltpu.make_async_copy(src.at[me * count + i], dst.at[i, me], send.at[i, 0])

    weights = (None, (wqkv_in.at[0], wqkv), (wup_in.at[0], wup), (wdown_in.at[0], wdown))

    def own_weight(k):
        src, dst = weights[k]
        return pltpu.make_async_copy(src, dst.at[me], s_w.at[k, 0])

    def send_table(j):
        return remote(table.at[me], table.at[me], s_w.at[0, j], r_w.at[0, j], flip(me, j))

    def send_weight(k, j):
        src, dst = weights[k]
        if j == 1:
            return remote(src, dst.at[me], s_w.at[k, 1], r_w.at[k, 1], flip(me, 1))
        if j == 2 and k == 1:
            return remote(src, dst.at[me], s_w.at[k, 2], r_w.at[k, 2], flip(me, 2))
        if j == 2:
            part = weights[k][0].at[mine_half]
            return remote(part, dst.at[me, mine_half], s_w.at[k, 2], r_w.at[k, 2], flip(me, 2))
        got = dst.at[flip(me, 2)]
        return remote(got, got, s_w.at[k, 3], r_w.at[k, 3], flip(me, 1))

    def pass_weight(k, rows):
        block = weights[k][1].at[flip(me, 2), rows]
        return aside(30 + k, block, block)

    def got_weight(k, j):
        dst = weights[k][1]
        block = dst.at[flip(me, j)] if j != 2 or k == 1 else dst.at[flip(me, j), mine_half]
        remote(block, block, s_w.at[k, j], r_w.at[k, j], flip(me, 1)).wait_recv()

    for c in range(2):
        table[me, c : c + 1, :] = qv_bias[:, c * WIDTH : (c + 1) * WIDTH]
    for c in range(PARTS):
        table[me, UP_BIAS + c : UP_BIAS + c + 1, :] = up_bias[:, c * WIDTH : (c + 1) * WIDTH]
    table[me, DOWN_BIAS : DOWN_BIAS + 1, :] = down_bias[...]
    table[me, GAIN_TWO : GAIN_TWO + 1, :] = gain_two[...].reshape(1, WIDTH)
    table[me, SHIFT_TWO : SHIFT_TWO + 1, :] = shift_two[...].reshape(1, WIDTH)
    table[me, OUT_BIAS:TABLE, :] = jnp.zeros((TABLE - OUT_BIAS, WIDTH), F32)
    for j in (2, 3, 1):
        send_table(j).start()
    own_weight(1).start()
    send_weight(1, 2).start()
    send_weight(1, 1).start()
    for k in range(2, 4):
        own_weight(k).start()
        send_weight(k, 2).start()

    def near_x(i):
        own_in(x_in, x, s_x, i).start()
        move_in(x_in, x, s_x, r_x, i, 1).start()

    def near_dy(i):
        own_in(dy_in, dy, s_dy, i).start()
        move_in(dy_in, dy, s_dy, r_dy, i, 1).start()

    each(count, near_x)
    for k in range(2, 4):
        send_weight(k, 1).start()
    each(count, near_dy)

    g_qkv[...] = jnp.zeros_like(g_qkv)
    acc[...] = jnp.zeros_like(acc)
    vec[...] = jnp.zeros_like(vec)
    up_sum[...] = jnp.zeros_like(up_sum)
    for g in range(GROUPS):
        hidden_s[g, WIDTH:, :] = jnp.ones((16, SEQ_LEN), BF16)
    wout_t[...] = wout[...].T

    for j in range(1, GROUPS):
        block = table.at[flip(me, j)]
        remote(block, block, s_w.at[0, j], r_w.at[0, j], flip(me, j)).wait_recv()
    for g in range(GROUPS):
        vectors = [a[...].reshape(1, D)[:, g * WIDTH : (g + 1) * WIDTH] for a in (out_bias, gain_one, shift_one)]
        rows = jnp.concatenate([table[g, 0:OUT_BIAS, :]] + vectors + [jnp.zeros((TABLE - COLS, WIDTH), F32)])
        cols[g, :, 0:TABLE] = rows.T

    def col(g, at):
        return cols[g, :, at : at + 1]

    def lane_col(g, at):
        return g * LANE_COLS + (at if at < UP_BIAS else at - PARTS)

    def add_sum(g, at, value):
        vec[lane_col(g, at)] += lane_part(value)

    def rows_of(g):
        return pl.ds(pl.multiple_of(g * WIDTH, WIDTH), WIDTH)

    def fwd_save(slot, i, g):
        return pltpu.make_async_copy(fwd.at[slot], fwd_st.at[i, g], s_fwd.at[slot])

    def bwd_save(slot, i, g):
        return pltpu.make_async_copy(bwd.at[slot], bwd_st.at[i, g], s_bwd.at[slot])

    def fwd_load(slot, i, g):
        return pltpu.make_async_copy(fwd_st.at[i, g], fwd.at[slot], s_fwd.at[slot])

    def bwd_load(slot, i, g):
        return pltpu.make_async_copy(bwd_st.at[i, g], bwd.at[slot], s_bwd.at[slot])

    def send_lo(i, j):
        to = flip(me, j)
        return remote(lo_s.at[to], lo_out.at[me * count + i], s_lo.at[i, j], r_lo.at[i, j], to)

    def own_lo(i):
        return pltpu.make_async_copy(lo_s.at[me], lo_out.at[me * count + i], s_lo.at[i, 0])

    def attend(i, j):
        first = i == 0
        label = seg[pl.ds(me * count + i, 1), :]
        ids = lax.broadcasted_iota(jnp.int32, (16, SEQ_LEN), 0)
        hot = (ids == label).astype(F32)
        hot_k = hot.astype(BF16)
        hot_q = jnp.where(ids < 4, (1.0 - hot) * MASKED, 0.0).astype(BF16)

        g = flip(me, j)
        slot = j % 2

        @pl.when(j == 0)
        def _():
            own_in(x_in, x, s_x, i).wait()

        @pl.when(j > 0)
        def _():
            block = x.at[i, g]
            remote(block, block, s_x.at[i, j], r_x.at[i, j], g).wait_recv()

        @pl.when(first & (j == 0))
        def _():
            own_weight(1).wait()

        @pl.when(first & (j == 1))
        def _():
            got_weight(1, 1)

        @pl.when(first & (j == 3))
        def _():
            got_weight(1, 3)

        @pl.when(first)
        def _():
            wqkv_t[g] = wqkv[g].T

        @pl.when(i * GROUPS + j >= 2)
        def _():
            fwd_save(slot, 0, 0).wait()

        xg = x[i, g]
        q = (nn(wqkv_t[g, 0:WIDTH, :], xg) + col(g, Q_BIAS)).astype(BF16) * jnp.asarray(SCALE, BF16)
        k = nn(wqkv_t[g, WIDTH : 2 * WIDTH, :], xg).astype(BF16)
        v = (nn(wqkv_t[g, 2 * WIDTH :, :], xg) + col(g, V_BIAS)).astype(BF16)
        fwd[slot, V_AT:FWD_ROWS, :] = v
        for h in range(HEADS_GROUP):
            part = slice(h * HEAD_DIM, (h + 1) * HEAD_DIM)
            qh = jnp.concatenate([q[part], hot_q])
            kh = jnp.concatenate([k[part], hot_k])
            fwd[slot, Q_AT + h * PAD : Q_AT + (h + 1) * PAD, :] = qh
            fwd[slot, K_AT + h * PAD : K_AT + (h + 1) * PAD, :] = kh
            scores = tn(kh, qh)
            largest = jnp.max(scores, axis=0, keepdims=True)
            powers = jnp.exp(scores - largest)
            inverse = 1.0 / channel_sum(powers)
            e = powers.astype(BF16)
            fwd[slot, E_AT + h * SEQ_LEN : E_AT + (h + 1) * SEQ_LEN, :] = e
            linv_s[i % early * HEADS + g * HEADS_GROUP + h] = inverse
            ctx_s[i % early, pl.ds(pl.multiple_of(g * WIDTH + h * HEAD_DIM, HEAD_DIM), HEAD_DIM), :] = (
                nn(v[part], e) * inverse
            ).astype(BF16)
        fwd_save(slot, i, g).start()

    def prepare(n):
        attend(n // 2, n % 2)

        @pl.when(n == 0)
        def _():
            start_in(x_in, x, s_x, r_x, 0)

        @pl.when(n == early)
        def _():
            got_weight(1, 2)
            send_weight(1, 3).start()
            for k in range(2, 4):
                got_weight(k, 2)
                pass_weight(k, mine_half).start()
            start_in(dy_in, dy, s_dy, r_dy, 0)

        @pl.when(n == 2 * early - 2)
        def _():
            for k in range(2, 4):
                pass_weight(k, other_half).wait_recv()
                send_weight(k, 3).start()

    def sequence(i):
        first = i == 0

        @pl.when(i + 1 < count)
        def _():
            start_in(x_in, x, s_x, r_x, i + 1)

        def attend_from(j, carry):
            attend(i, j)
            return carry

        lax.fori_loop(2 if early == count else jnp.where(i < early, 2, 0), GROUPS, attend_from, 0)

        @pl.when(i + 1 < count)
        def _():
            start_in(dy_in, dy, s_dy, r_dy, i + 1)

        def mix(g, carry):
            total, square = carry
            branch = (nn(wout_t[rows_of(g), :], ctx_s[i % early]) + col(g, OUT_BIAS)).astype(BF16)
            summed = branch.astype(F32) + x[i, g].astype(F32)
            summed_s[g] = summed
            return total + fold(summed), square + fold(summed * summed)

        total, square = over(GROUPS, mix, (zero, zero), 4)
        center1 = channel_sum(total) / D
        inverse1 = lax.rsqrt(channel_sum(square) / D - center1 * center1 + EPS)

        @pl.when(first)
        def _():
            for k in range(2, 4):
                own_weight(k).wait()
                got_weight(k, 1)
                got_weight(k, 3)

            def turn(g):
                wup_t[g] = wup[g].T
                wdown_t[g] = wdown[g].T

            each(GROUPS, turn)

        def feed(g, carry):
            total, square = carry
            normed = (summed_s[g] - center1) * inverse1
            hidden = (normed * col(g, GAIN_ONE) + col(g, SHIFT_ONE)).astype(BF16)
            hidden_s[g, 0:WIDTH, :] = hidden
            for part in range(PARTS):
                rows = slice(part * WIDTH, (part + 1) * WIDTH)
                u = nn(wup_t[g, rows, :], hidden) + col(g, UP_BIAS + part)
                act, slope = gelu_pair(u)
                act_s[g, rows, :] = act.astype(BF16)
                slope_s[g, rows, :] = slope.astype(BF16)
            summed2 = hidden.astype(F32) + nn(wdown[g], act_s[g]) + col(g, DOWN_BIAS)
            summed2_s[g] = summed2
            return total + fold(summed2), square + fold(summed2 * summed2)

        total, square = over(GROUPS, feed, (zero, zero), 4)
        center2 = channel_sum(total) / D
        inverse2 = lax.rsqrt(channel_sum(square) / D - center2 * center2 + EPS)

        @pl.when(i > 0)
        def _():
            own_lo(i - 1).wait()
            for j in range(1, GROUPS):
                send_lo(i - 1, j).wait_send()

        own_in(dy_in, dy, s_dy, i).wait()
        for j in range(1, GROUPS):
            block = dy.at[i, flip(me, j)]
            remote(block, block, s_dy.at[i, j], r_dy.at[i, j], flip(me, j)).wait_recv()

        def finish(g, carry):
            sum_e, sum_en = carry
            normed = (summed2_s[g] - center2) * inverse2
            gain = col(g, GAIN_TWO)
            lo_s[g] = (normed * gain + col(g, SHIFT_TWO)).astype(BF16)
            grad = dy[i, g].astype(F32)
            product = grad * normed
            add_sum(g, GAIN_TWO, product)
            add_sum(g, SHIFT_TWO, grad)
            summed2_s[g] = normed
            return sum_e + fold(grad * gain), sum_en + fold(product * gain)

        sum_e, sum_en = over(GROUPS, finish, (zero, zero), 4)
        mean_e = channel_sum(sum_e) / D
        mean_en = channel_sum(sum_en) / D

        own_lo(i).start()
        for j in range(1, GROUPS):
            send_lo(i, j).start()

        def feed_back(g, carry):
            sum_h, sum_hn = carry
            normed2 = summed2_s[g]
            scaled = dy[i, g].astype(F32) * col(g, GAIN_TWO)
            grad2 = (inverse2 * (scaled - mean_e - normed2 * mean_en)).astype(BF16)
            wide = grad2.astype(F32)
            add_sum(g, DOWN_BIAS, wide)
            for part in range(PARTS):
                rows = slice(part * WIDTH, (part + 1) * WIDTH)
                up_grad = (nn(wdown_t[g, rows, :], grad2) * slope_s[g, rows, :].astype(F32)).astype(BF16)
                up_grad_s[rows, :] = up_grad
            both = nt(hidden_s[g], up_grad_s[...])
            acc[0, g] += both[0:WIDTH]
            up_sum[g] += both[WIDTH : WIDTH + 8]
            acc[1, g] += nt(grad2, act_s[g])
            hidden_grad = (wide + nn(wup[g], up_grad_s[...])).astype(BF16)
            hidden_grad_s[rows_of(g), :] = hidden_grad
            grad1 = hidden_grad.astype(F32)
            normed1 = (summed_s[g] - center1) * inverse1
            product = grad1 * normed1
            gain = col(g, GAIN_ONE)
            add_sum(g, GAIN_ONE, product)
            add_sum(g, SHIFT_ONE, grad1)
            return sum_h + fold(grad1 * gain), sum_hn + fold(product * gain)

        sum_h, sum_hn = over(GROUPS, feed_back, (zero, zero), 4)
        mean_h = channel_sum(sum_h) / D
        mean_hn = channel_sum(sum_hn) / D

        def norm_back(g):
            normed1 = (summed_s[g] - center1) * inverse1
            scaled = hidden_grad_s[rows_of(g), :].astype(F32) * col(g, GAIN_ONE)
            summed_grad = (inverse1 * (scaled - mean_h - normed1 * mean_hn)).astype(BF16)
            hidden_grad_s[rows_of(g), :] = summed_grad
            add_sum(g, OUT_BIAS, summed_grad.astype(F32))

        for g in range(GROUPS):
            norm_back(g)

        def mix_back(g):
            slot = g
            ctx = ctx_s[i % early, rows_of(g), :]
            acc[2, g] += nt(ctx, hidden_grad_s[...])
            ctx_grad = nn(wout[rows_of(g), :], hidden_grad_s[...]).astype(BF16).astype(F32)
            for h in range(HEADS_GROUP):
                part = slice(h * HEAD_DIM, (h + 1) * HEAD_DIM)
                grad = (ctx_grad[part] * linv_s[i % early * HEADS + g * HEADS_GROUP + h]).astype(BF16)
                bwd[slot, h * HEAD_DIM : (h + 1) * HEAD_DIM, :] = grad
                middle_s[i * HEADS + g * HEADS_GROUP + h] = channel_sum(grad.astype(F32) * ctx[part].astype(F32))
            bwd[slot, WIDTH:BWD_ROWS, :] = hidden_grad_s[rows_of(g), :]
            bwd_save(slot, i, g).start()

        @pl.when(i > 0)
        def _():
            for g in range(GROUPS):
                bwd_save(g, 0, 0).wait()

        for g in range(GROUPS):
            mix_back(g)

    each(2 * early, prepare)
    each(count, sequence)
    for slot in range(2):
        fwd_save(slot, 0, 0).wait()
    for slot in range(GROUPS):
        bwd_save(slot, 0, 0).wait()

    def unit_of(u):
        return u % count, GROUPS - 1 - u // count

    def load(u):
        i, j = unit_of(u)
        g = flip(me, j)
        fwd_load(u % 2, i, g).start()
        bwd_load(u % 2, i, g).start()

    def send_dx(i, j):
        to = flip(me, j)
        return remote(x.at[i, to], dx_out.at[me * count + i], s_dx.at[i, j], r_dx.at[i, j], to)

    def own_dx(i):
        return pltpu.make_async_copy(x.at[i, me], dx_out.at[me * count + i], s_dx.at[i, 0])

    def when(condition, body):
        if condition is True:
            body()
        else:
            pl.when(condition)(body)

    depth = size // 2
    level = row // 2
    owners = all_l.shape[1]
    per_half = owners // 2
    cut = WIDTH // 2 // per_half
    pair_groups = (flip(me, 1), flip(me, 3))
    kept = (me, flip(me, 2))
    outs = (up_out, down_out, None)

    def peers(n, body):
        def run(k):
            body(k + 1)

        each(n - 1, run)

    def along(kind, src, dst, k, sided):
        to = (level + k) % depth * 2 + half if sided else (row + k) % size
        return pltpu.make_async_remote_copy(
            src_ref=src, dst_ref=dst, send_sem=s_row.at[kind, k], recv_sem=r_row.at[kind, k],
            device_id={"rows": to}, device_id_type=MESH,
        )

    def line(sided):
        return (depth, level) if sided else (size, row)

    def capped(at, n, length):
        return at if n == length else jnp.minimum(at, n - 1)

    def owns(at, n, length):
        return True if n == length else at < n

    def scatter(kind, parts, landing, sided, act):
        n = parts.shape[0]
        length, here = line(sided)

        def one(k):
            to = (here + k) % length
            piece = parts.at[capped(to, n, length)]
            when(owns(to, n, length), lambda: act(along(kind, piece, landing.at[k], k, sided)))

        peers(length, one)

    def scatter_got(kind, parts, landing, sided):
        peers(line(sided)[0], lambda k: along(kind, parts.at[0], landing.at[k], k, sided).wait_recv())

    def spread_out(kind, landing, sided, act):
        n = landing.shape[0]
        length, here = line(sided)
        own = landing.at[capped(here, n, length)]
        when(owns(here, n, length), lambda: peers(length, lambda k: act(along(kind, own, own, k, sided))))

    def spread_got(kind, landing, sided):
        n = landing.shape[0]
        length, here = line(sided)
        peers(
            length,
            lambda k: when(
                owns((here + length - k) % length, n, length),
                lambda: along(kind, landing.at[0], landing.at[0], k, sided).wait_recv(),
            ),
        )

    def start(copy):
        copy.start()

    def sent(copy):
        copy.wait_send()

    def pair_copy(b):
        return across(b, pair_t.at[b], pair_l.at[b], 1)

    def side_copy(b):
        return aside(3 + b, side_t.at[b], side_l.at[b])

    def far_copy(b):
        return across(6 + b, far_t.at[b], far_l.at[b], 2)

    def out_copy(b, rows):
        return aside(9 + b, outs[b].at[rows], outs[b].at[rows])

    def pair_send(b):
        for at in range(2):
            pair_t[b, at] = acc[b, pair_groups[at]].astype(BF16)
        pair_copy(b).start()

    def side_send(b):
        pair_copy(b).wait_recv()
        for at in range(2):
            acc[b, kept[at]] += pair_l[b, at].astype(F32)
            side_t[b, at] = acc[b, kept[at], other_half, :].astype(BF16)
        side_copy(b).start()

    def far_send(b):
        side_copy(b).wait_recv()
        acc[b, me, mine_half, :] += side_l[b, 0].astype(F32)
        far_t[b] = (acc[b, kept[1], mine_half, :] + side_l[b, 1].astype(F32)).astype(BF16)
        far_copy(b).start()

    def cut_send(b):
        far_copy(b).wait_recv()
        total = acc[b, me, mine_half, :] + far_l[b].astype(F32)
        for o in range(owners):
            rows = o % per_half * cut
            lanes = o // per_half * HALF
            cut_t[b, o] = total[rows : rows + cut, lanes : lanes + HALF].astype(BF16)
        scatter(b, cut_t.at[b], cut_l.at[b], True, start)

    def all_send(b):
        def close():
            scatter_got(b, cut_t.at[b], cut_l.at[b], True)
            own = capped(level, owners, depth)
            total = cut_t[b, own].astype(F32)
            for k in range(1, depth):
                total = total + cut_l[b, k].astype(F32)
            all_l[b, own] = total.astype(BF16)

        when(owns(level, owners, depth), close)
        spread_out(3 + b, all_l.at[b], True, start)

    def joined(b):
        spread_got(3 + b, all_l.at[b], True)
        sides = [
            jnp.concatenate([all_l[b, side * per_half + o] for o in range(per_half)]) for side in range(2)
        ]
        return jnp.concatenate(sides, axis=1)

    def out_send(b):
        outs[b][mine_half, :] = joined(b)
        out_copy(b, mine_half).start()

    def mix_part(g, rows):
        return mix_out.at[g, rows]

    def mix_far(g):
        return across(12, mix_part(g, mine_half), mix_part(g, mine_half), 2)

    def mix_beside(at, rows):
        return aside(13 + at, mix_part(kept[at], rows), mix_part(kept[at], rows))

    def mix_core(at, g):
        return across(15 + at, mix_out.at[g], mix_out.at[g], 1)

    def mix_far_send():
        mix_out[me, mine_half, :] = joined(2)
        mix_far(me).start()
        mix_beside(0, mine_half).start()

    def mix_beside_send():
        mix_far(flip(me, 2)).wait_recv()
        mix_beside(1, mine_half).start()

    def mix_core_send():
        for at in range(2):
            mix_beside(at, other_half).wait_recv()
            mix_core(at, kept[at]).start()

    def early_copy(j):
        return across(17 + j, sum_t.at[flip(me, j)], sum_l.at[j], j)

    def shared_copy(j):
        return across(20 + j, shared_out.at[me], shared_out.at[me], j)

    def end_copy(j):
        return across(23 + j, end_t.at[j], end_l.at[j], j)

    def lane_rows(g, columns):
        return [jnp.sum(vec[lane_col(g, c)].T, axis=0, keepdims=True) for c in columns]

    def early_send():
        for g in range(GROUPS):
            zeros = [jnp.zeros((1, WIDTH), F32)] * 2
            up = [up_sum[g, 0:1, c * WIDTH : (c + 1) * WIDTH] for c in range(PARTS)]
            rows = zeros + up + lane_rows(g, range(DOWN_BIAS, COLS)) + zeros * ((TABLE - COLS) // 2)
            sum_t[g] = jnp.concatenate(rows)
        for j in range(1, GROUPS):
            early_copy(j).start()

    def early_row_send():
        total = sum_t[me]
        for j in range(1, GROUPS):
            early_copy(j).wait_recv()
            total = total + sum_l[j]
        sum_row_t[...] = total
        peers(size, lambda k: along(8, sum_row_t, sum_row_l.at[k], k, False).start())

    def shared_send():
        total = sum_row_t[...]
        peers(size, lambda k: along(8, sum_row_t, sum_row_l.at[k], k, False).wait_recv())
        for k in range(1, size):
            total = total + sum_row_l[k]
        sums_out[...] = total
        shared_out[me] = total
        for j in range(1, GROUPS):
            shared_copy(j).start()

    qowners = qall_l.shape[0]
    qcut = WIDTH // qowners

    def qpair_copy(at):
        return across(27 + at, qpair_t.at[at], qpair_l.at[at], 1)

    def qpiece_copy():
        return across(29, qpiece_t, qpiece_l, 2)

    def qpair_send(at, j):
        qpair_t[at] = g_qkv[flip(me, j)].astype(BF16)
        qpair_copy(at).start()

    def qpieces(at, g, parts, landing, kind):
        qpair_copy(at).wait_recv()
        for o in range(qowners):
            rows = slice(o * qcut, (o + 1) * qcut)
            parts[o] = (g_qkv[g, rows, :] + qpair_l[at, rows, :].astype(F32)).astype(BF16)
        scatter(kind, parts, landing, False, start)

    def qtotal(parts, landing, kind):
        scatter_got(kind, parts, landing, False)
        total = parts[capped(row, qowners, size)].astype(F32)
        for k in range(1, size):
            total = total + landing[k].astype(F32)
        return total

    def qfar_send():
        qpieces(0, flip(me, 2), qfar_t, qfar_l, 6)

    def qpiece_send():
        def close():
            qpiece_t[...] = qtotal(qfar_t, qfar_l, 6).astype(BF16)
            qpiece_copy().start()

        when(owns(row, qowners, size), close)

    def end_sums(g):
        return jnp.concatenate(lane_rows(g, (Q_BIAS, V_BIAS)) + [jnp.zeros((6, WIDTH), F32)])

    def qcut_send():
        qpieces(1, me, qcut_t, qcut_l, 7)
        sums = end_sums(me)
        for j in range(1, GROUPS):
            end_copy(j).wait_recv()
            sums = sums + end_l[j]
        end_row_t[...] = sums
        peers(size, lambda k: along(9, end_row_t, end_row_l.at[k], k, False).start())

    def qall_send():
        def close():
            total = qtotal(qcut_t, qcut_l, 7)
            qpiece_copy().wait_recv()
            qall_l[capped(row, qowners, size)] = (total + qpiece_l[...].astype(F32)).astype(BF16)

        when(owns(row, qowners, size), close)
        spread_out(10, qall_l, False, start)

    def qclose():
        peers(size, lambda k: along(9, end_row_t, end_row_l.at[k], k, False).wait_recv())
        sums = end_row_t[...]
        for k in range(1, size):
            sums = sums + end_row_l[k]
        sums_out[0:2, :] = sums[0:2]
        spread_got(10, qall_l, False)
        for o in range(qowners):
            qkv_out[o * qcut : (o + 1) * qcut, :] = qall_l[o]

    UP, DOWN, MIX = 0, 1, 2
    plan = {
        1: [lambda: side_send(MIX), early_row_send],
        2: [lambda: side_send(UP)],
        4: [lambda: qpair_send(0, 3), lambda: side_send(DOWN)],
        5: [lambda: far_send(MIX), shared_send],
        7: [lambda: far_send(UP)],
        8: [qfar_send, lambda: cut_send(MIX)],
        9: [lambda: far_send(DOWN)],
        10: [lambda: cut_send(UP)],
        11: [lambda: all_send(MIX)],
        12: [lambda: qpair_send(1, 1), lambda: cut_send(DOWN)],
        13: [qpiece_send, lambda: all_send(UP)],
        14: [mix_far_send],
        15: [lambda: all_send(DOWN), lambda: out_send(UP)],
    }

    def follow(u):
        for at, steps in plan.items():

            @pl.when(u == count * GROUPS * at // 16 - 1)
            def _():
                for step in steps:
                    step()

    load(0)
    for b in (MIX, UP, DOWN):
        pair_send(b)
    early_send()

    def unit(u):
        i, j = unit_of(u)
        g = flip(me, j)
        slot = u % 2
        fwd_load(slot, i, g).wait()
        bwd_load(slot, i, g).wait()

        @pl.when(u + 1 < count * GROUPS)
        def _():
            load(u + 1)

        for h in range(HEADS_GROUP):
            e = fwd[slot, E_AT + h * SEQ_LEN : E_AT + (h + 1) * SEQ_LEN, :]
            q = fwd[slot, Q_AT + h * PAD : Q_AT + h * PAD + HEAD_DIM, :]
            k = fwd[slot, K_AT + h * PAD : K_AT + h * PAD + HEAD_DIM, :]
            v = fwd[slot, V_AT + h * HEAD_DIM : V_AT + (h + 1) * HEAD_DIM, :]
            grad = bwd[slot, h * HEAD_DIM : (h + 1) * HEAD_DIM, :]
            prob_grad = tn(v, grad)
            score_grad = (e.astype(F32) * (prob_grad - middle_s[i * HEADS + g * HEADS_GROUP + h])).astype(BF16)
            at = h * HEAD_DIM
            act_s[0, 2 * WIDTH + at : 2 * WIDTH + at + HEAD_DIM, :] = nt(grad, e).astype(BF16)
            act_s[0, at : at + HEAD_DIM, :] = (nn(k, score_grad) * SCALE).astype(BF16)
            act_s[0, WIDTH + at : WIDTH + at + HEAD_DIM, :] = nt(q, score_grad).astype(BF16)
        g_qkv[g] += nt(x[i, g], act_s[0, 0:QKV, :])
        add_sum(g, Q_BIAS, act_s[0, 0:WIDTH, :].astype(F32))
        add_sum(g, V_BIAS, act_s[0, 2 * WIDTH : QKV, :].astype(F32))
        into = bwd[slot, WIDTH:BWD_ROWS, :].astype(F32) + nn(wqkv[g], act_s[0, 0:QKV, :])
        x[i, g] = into.astype(BF16)

        @pl.when((j > 0) & (i == count - 1))
        def _():
            end_t[j] = end_sums(g)
            end_copy(j).start()

        @pl.when(j == 1)
        def _():
            send_dx(i, 1).start()

        @pl.when(u % 2 == 1)
        def _():
            late_i, late_j = unit_of(u // 2)
            send_dx(late_i, late_j).start()

        @pl.when(j == 0)
        def _():
            own_dx(i).start()

        follow(u)

    each(count * GROUPS, unit)
    qcut_send()
    qall_send()
    mix_beside_send()
    out_send(DOWN)
    mix_core_send()
    for j in range(1, GROUPS):
        block = shared_out.at[flip(me, j)]
        across(20 + j, block, block, j).wait_recv()
    for b in (UP, DOWN):
        out_copy(b, other_half).wait_recv()
    for at, j in enumerate((1, 3)):
        mix_core(at, flip(me, j)).wait_recv()
    qclose()

    for j in range(1, GROUPS):
        send_table(j).wait_send()
        for k in range(1, 4):
            send_weight(k, j).wait_send()
    for k in range(2, 4):
        pass_weight(k, mine_half).wait_send()
    own_lo(count - 1).wait()
    for j in range(1, GROUPS):
        send_lo(count - 1, j).wait_send()

    def drain(i):
        own_dx(i).wait()
        for j in range(1, GROUPS):
            move_in(x_in, x, s_x, r_x, i, j).wait_send()
            move_in(dy_in, dy, s_dy, r_dy, i, j).wait_send()
            send_lo(i, j).wait_recv()
            send_dx(i, j).wait_send()
            send_dx(i, j).wait_recv()

    each(count, drain)
    for b in range(BLOCKS):
        pair_copy(b).wait_send()
        side_copy(b).wait_send()
        scatter(b, cut_t.at[b], cut_l.at[b], True, sent)
        far_copy(b).wait_send()
        spread_out(3 + b, all_l.at[b], True, sent)
    for b in (UP, DOWN):
        out_copy(b, mine_half).wait_send()
    mix_far(me).wait_send()
    for at in range(2):
        mix_beside(at, mine_half).wait_send()
        mix_core(at, kept[at]).wait_send()
        qpair_copy(at).wait_send()
    when(owns(row, qowners, size), lambda: qpiece_copy().wait_send())
    for j in range(1, GROUPS):
        early_copy(j).wait_send()
        shared_copy(j).wait_send()
        end_copy(j).wait_send()
    scatter(6, qfar_t, qfar_l, False, sent)
    scatter(7, qcut_t, qcut_l, False, sent)
    spread_out(10, qall_l, False, sent)
    peers(size, lambda k: along(8, sum_row_t, sum_row_l.at[k], k, False).wait_send())
    peers(size, lambda k: along(9, end_row_t, end_row_l.at[k], k, False).wait_send())


def layer(size, x, dy, *rest):
    count = x.shape[0] // GROUPS
    here = pl.BlockSpec(memory_space=pl.ANY)
    vmem = pl.BlockSpec(memory_space=pltpu.VMEM)
    grads = [
        ((WIDTH, QKV), BF16),
        ((WIDTH, UNITS), BF16),
        ((WIDTH, UNITS), BF16),
        ((GROUPS, WIDTH, UNITS), BF16),
        ((TABLE, WIDTH), F32),
        ((GROUPS, TABLE, WIDTH), F32),
    ]
    early = min(count, EARLY)
    depth = size // 2
    owners = 2 * owners_of(depth // 2, WIDTH // 32)
    piece = (WIDTH // owners, HALF)
    qowners = owners_of(size, WIDTH // 16)
    qpiece = (WIDTH // qowners, QKV)
    token = (GROUPS, WIDTH, SEQ_LEN)
    dma = pltpu.SemaphoreType.DMA
    return pl.pallas_call(
        functools.partial(layer_kernel, size),
        out_shape=[jax.ShapeDtypeStruct(x.shape, BF16)] * 2
        + [
            jax.ShapeDtypeStruct((count, GROUPS, FWD_ROWS, SEQ_LEN), BF16),
            jax.ShapeDtypeStruct((count, GROUPS, BWD_ROWS, SEQ_LEN), BF16),
        ]
        + [jax.ShapeDtypeStruct(s, t) for s, t in grads],
        in_specs=[here, here, vmem, here, here, here] + [vmem] * 9,
        out_specs=[here] * 4 + [vmem] * len(grads),
        scratch_shapes=[
            pltpu.VMEM((count,) + token, BF16),
            pltpu.VMEM((count,) + token, BF16),
            pltpu.VMEM((GROUPS, WIDTH, QKV), BF16),
            pltpu.VMEM((GROUPS, WIDTH, UNITS), BF16),
            pltpu.VMEM((GROUPS, WIDTH, UNITS), BF16),
            pltpu.VMEM((GROUPS, TABLE, WIDTH), F32),
            pltpu.VMEM((GROUPS, WIDTH, 128), F32),
            pltpu.VMEM((GROUPS, QKV, WIDTH), BF16),
            pltpu.VMEM((GROUPS, UNITS, WIDTH), BF16),
            pltpu.VMEM((GROUPS, UNITS, WIDTH), BF16),
            pltpu.VMEM((D, D), BF16),
            pltpu.VMEM((GROUPS * LANE_COLS, WIDTH, 128), F32),
            pltpu.VMEM((GROUPS, 8, UNITS), F32),
            pltpu.VMEM((2, FWD_ROWS, SEQ_LEN), BF16),
            pltpu.VMEM((GROUPS, BWD_ROWS, SEQ_LEN), BF16),
            pltpu.VMEM((count * HEADS, 1, SEQ_LEN), F32),
            pltpu.VMEM((early * HEADS, 1, SEQ_LEN), F32),
            pltpu.VMEM((early, D, SEQ_LEN), BF16),
            pltpu.VMEM(token, F32),
            pltpu.VMEM((GROUPS, WIDTH + 16, SEQ_LEN), BF16),
            pltpu.VMEM((GROUPS, UNITS, SEQ_LEN), BF16),
            pltpu.VMEM((GROUPS, UNITS, SEQ_LEN), BF16),
            pltpu.VMEM(token, F32),
            pltpu.VMEM((UNITS, SEQ_LEN), BF16),
            pltpu.VMEM((D, SEQ_LEN), BF16),
            pltpu.VMEM(token, BF16),
            pltpu.VMEM((BLOCKS, GROUPS, WIDTH, UNITS), F32),
            pltpu.VMEM((GROUPS, WIDTH, QKV), F32),
            pltpu.VMEM((BLOCKS, 2, WIDTH, UNITS), BF16),
            pltpu.VMEM((BLOCKS, 2, WIDTH, UNITS), BF16),
            pltpu.VMEM((BLOCKS, 2, WIDTH // 2, UNITS), BF16),
            pltpu.VMEM((BLOCKS, 2, WIDTH // 2, UNITS), BF16),
            pltpu.VMEM((BLOCKS, owners) + piece, BF16),
            pltpu.VMEM((BLOCKS, depth) + piece, BF16),
            pltpu.VMEM((BLOCKS, WIDTH // 2, UNITS), BF16),
            pltpu.VMEM((BLOCKS, WIDTH // 2, UNITS), BF16),
            pltpu.VMEM((BLOCKS, owners) + piece, BF16),
            pltpu.VMEM((2, WIDTH, QKV), BF16),
            pltpu.VMEM((2, WIDTH, QKV), BF16),
            pltpu.VMEM((qowners,) + qpiece, BF16),
            pltpu.VMEM((size,) + qpiece, BF16),
            pltpu.VMEM(qpiece, BF16),
            pltpu.VMEM(qpiece, BF16),
            pltpu.VMEM((qowners,) + qpiece, BF16),
            pltpu.VMEM((size,) + qpiece, BF16),
            pltpu.VMEM((qowners,) + qpiece, BF16),
            pltpu.VMEM((GROUPS, TABLE, WIDTH), F32),
            pltpu.VMEM((GROUPS, TABLE, WIDTH), F32),
            pltpu.VMEM((TABLE, WIDTH), F32),
            pltpu.VMEM((size, TABLE, WIDTH), F32),
            pltpu.VMEM((GROUPS, 8, WIDTH), F32),
            pltpu.VMEM((GROUPS, 8, WIDTH), F32),
            pltpu.VMEM((8, WIDTH), F32),
            pltpu.VMEM((size, 8, WIDTH), F32),
        ]
        + [dma((count, GROUPS))] * 8
        + [dma((4, GROUPS))] * 2
        + [dma((34,))] * 2
        + [dma((11, size))] * 2
        + [dma((2,)), dma((GROUPS,))],
        compiler_params=pltpu.CompilerParams(
            vmem_limit_bytes=(64 << 20) - (1 << 17), collective_id=0, has_side_effects=True
        ),
    )(x, dy, *rest)


def local(
    size, layer_input, segment_ids, qkv_weight, qv_bias, out_weight, out_bias, gain_one, shift_one,
    up_weight, up_bias, down_weight, down_bias, gain_two, shift_two, out_grad,
):
    lo, dx, _, _, *grads = layer(
        size, layer_input, out_grad, segment_ids, qkv_weight, up_weight, down_weight, out_weight,
        qv_bias, up_bias, down_bias, gain_two, shift_two, out_bias, gain_one, shift_one,
    )
    lo, dx, g_qkv, g_up, g_down, g_out, qv, out_b, gain1, shift1, up_b, down_b, gain2, shift2 = widen(lo, dx, *grads)
    return lo, dx, g_qkv, qv, g_out, out_b, gain1, shift1, g_up, up_b, g_down, down_b, gain2, shift2


def widen_kernel(
    lo, dx, qkv, up, down, mix, sums, shared,
    lo_o, dx_o, qkv_o, up_o, down_o, mix_o, qv_o, out_o, gain1_o, shift1_o, up_b_o, down_b_o, gain2_o, shift2_o,
):
    for src, out in ((lo, lo_o), (dx, dx_o), (qkv, qkv_o), (up, up_o), (down, down_o), (mix, mix_o)):
        out[...] = src[...].astype(F32).reshape(out.shape)

    @pl.when(pl.program_id(0) == 0)
    def _():
        def own(first, n):
            return jnp.concatenate([sums[first + c : first + c + 1, :] for c in range(n)], axis=1)

        def joint(at):
            return jnp.concatenate([shared[g, at : at + 1, :] for g in range(GROUPS)], axis=1)

        qv_o[...] = own(Q_BIAS, 2)
        up_b_o[...] = own(UP_BIAS, PARTS)
        down_b_o[...] = own(DOWN_BIAS, 1)
        gain2_o[...] = own(GAIN_TWO, 1).reshape(WIDTH)
        shift2_o[...] = own(SHIFT_TWO, 1).reshape(WIDTH)
        for out, at in ((out_o, OUT_BIAS), (gain1_o, GAIN_ONE), (shift1_o, SHIFT_ONE)):
            out[...] = joint(at).reshape(D)


def widen(lo, dx, *grads):
    steps = 8
    part = WIDTH // steps
    data = pl.BlockSpec((lo.shape[0] // steps, WIDTH, SEQ_LEN), lambda i: (i, 0, 0))

    def slab(columns):
        return pl.BlockSpec((part, columns), lambda i: (i, 0)), pl.BlockSpec((1, part, columns), lambda i: (0, i, 0))

    def whole(shape):
        return pl.BlockSpec(shape, lambda i: (0,) * len(shape), pipeline_mode=pl.Buffered(1))

    qkv_in, qkv_out = slab(QKV)
    unit_in, unit_out = slab(UNITS)
    mix_in = pl.BlockSpec((1, WIDTH // 2, D), lambda i: (i // 2, i % 2, 0))
    mix_out = pl.BlockSpec((WIDTH // 2, D), lambda i: (i, 0))
    wide = [(1, WIDTH, QKV), (1, WIDTH, UNITS), (1, WIDTH, UNITS), (D, D)]
    vectors = [(1, 2 * WIDTH), (D,), (D,), (D,), (1, UNITS), (1, WIDTH), (WIDTH,), (WIDTH,)]
    return pl.pallas_call(
        widen_kernel,
        grid=(steps,),
        out_shape=[jax.ShapeDtypeStruct(s, F32) for s in [lo.shape, dx.shape] + wide + vectors],
        in_specs=[data, data, qkv_in, unit_in, unit_in, mix_in] + [whole(a.shape) for a in grads[4:]],
        out_specs=[data, data, qkv_out, unit_out, unit_out, mix_out] + [whole(s) for s in vectors],
        compiler_params=pltpu.CompilerParams(vmem_limit_bytes=62 << 20),
    )(lo, dx, *grads)


def solution(mesh):
    group = P("grp", None, None)
    data = P("rows", "grp", None)
    in_specs = (
        data, P("rows", None), group, P("grp", None), P(), P(), P(), P(),
        group, P("grp", None), group, P("grp", None), P("grp"), P("grp"), data,
    )
    out_specs = (
        data, data, group, P("grp", None), P(), P(), P(), P(),
        group, P("grp", None), group, P("grp", None), P("grp"), P("grp"),
    )
    return jax.shard_map(functools.partial(local, mesh.shape["rows"]), mesh=mesh, in_specs=in_specs, out_specs=out_specs, check_vma=False)
```

```python
import functools

import jax
import jax.numpy as jnp
from jax import lax
from jax.experimental import pallas as pl
from jax.experimental.pallas import tpu as pltpu
from jax.sharding import PartitionSpec as P

D = 768
HEAD_DIM = 64
SEQ_LEN = 512
GROUPS = 4
WIDTH = D // GROUPS
HEADS_GROUP = WIDTH // HEAD_DIM
HEADS = D // HEAD_DIM
QKV = 3 * WIDTH
UNITS = 768
PARTS = UNITS // WIDTH
PAD = HEAD_DIM + 16
MASKED = -1e30
EPS = 1e-05
SCALE = HEAD_DIM ** (-0.5)
BLOCKS = 3
EARLY = 2
HALF = UNITS // 2

F32 = jnp.float32
BF16 = jnp.bfloat16
MESH = pl.DeviceIdType.MESH

Q_BIAS, V_BIAS, UP_BIAS, DOWN_BIAS, GAIN_TWO, SHIFT_TWO, OUT_BIAS, GAIN_ONE, SHIFT_ONE = 0, 1, 2, 6, 7, 8, 9, 10, 11
COLS = 12
LANE_COLS = COLS - PARTS
TABLE = 16

E_AT = 0
Q_AT = HEADS_GROUP * SEQ_LEN
K_AT = Q_AT + HEADS_GROUP * PAD
V_AT = K_AT + HEADS_GROUP * PAD
FWD_ROWS = V_AT + WIDTH
BWD_ROWS = 2 * WIDTH


def nn(a, b):
    return lax.dot_general(a, b, (((1,), (0,)), ((), ())), preferred_element_type=F32)


def nt(a, b):
    return lax.dot_general(a, b, (((1,), (1,)), ((), ())), preferred_element_type=F32)


def tn(a, b):
    return lax.dot_general(a, b, (((0,), (0,)), ((), ())), preferred_element_type=F32)


def lane_part(value):
    total = value[:, 0:128]
    for at in range(128, SEQ_LEN, 128):
        total = total + value[:, at : at + 128]
    return total


def channel_sum(value):
    return jnp.sum(value, axis=0, keepdims=True)


def fold(value):
    return jnp.sum(value.reshape(value.shape[0] // 8, 8, SEQ_LEN), axis=0)


def spread(column):
    return jnp.concatenate([column] * (SEQ_LEN // 128), axis=1)


def gelu_pair(u):
    half_erf = 0.5 * lax.erf(u * 0.7071067811865476) + 0.5
    density = jnp.exp(u * u * -0.5) * 0.3989422804014327
    return u * half_erf, half_erf + u * density


def flip(me, j):
    return (me + j) % 2 + 2 * ((me // 2 + j // 2) % 2)


def owners_of(rows, parts):
    return max(n for n in range(1, min(rows, parts) + 1) if parts % n == 0)


def layer_kernel(
    size, x_in, dy_in, seg, wqkv_in, wup_in, wdown_in, wout,
    qv_bias, up_bias, down_bias, gain_two, shift_two, out_bias, gain_one, shift_one,
    lo_out, dx_out, fwd_st, bwd_st, qkv_out, up_out, down_out, mix_out, sums_out, shared_out,
    x, dy, wqkv, wup, wdown, table, cols, wqkv_t, wup_t, wdown_t, wout_t, vec, up_sum,
    fwd, bwd, middle_s, linv_s, ctx_s, summed_s, hidden_s, act_s, slope_s, summed2_s,
    up_grad_s, hidden_grad_s, lo_s,
    acc, g_qkv, pair_t, pair_l, side_t, side_l, cut_t, cut_l, far_t, far_l, all_l,
    qpair_t, qpair_l, qfar_t, qfar_l, qpiece_t, qpiece_l, qcut_t, qcut_l, qall_l,
    sum_t, sum_l, sum_row_t, sum_row_l, end_t, end_l, end_row_t, end_row_l,
    s_x, r_x, s_dy, r_dy, s_lo, r_lo, s_dx, r_dx, s_w, r_w, s_one, r_one, s_row, r_row, s_fwd, s_bwd,
):
    count = x.shape[0]
    early = ctx_s.shape[0]
    me = lax.axis_index("grp")
    row = lax.axis_index("rows")
    zero = jnp.zeros((8, SEQ_LEN), F32)

    def over(n, body, init=0, unroll=False):
        return lax.fori_loop(0, n, body, init, unroll=unroll)

    def each(n, body):
        def run(at, carry):
            body(at)
            return carry

        lax.fori_loop(0, n, run, 0)

    def remote(src, dst, send, recv, to):
        return pltpu.make_async_remote_copy(
            src_ref=src, dst_ref=dst, send_sem=send, recv_sem=recv, device_id={"grp": to}, device_id_type=MESH
        )

    half = row % 2
    beside = row + 1 - 2 * half

    def half_rows(at):
        return pl.ds(pl.multiple_of(at * (WIDTH // 2), WIDTH // 2), WIDTH // 2)

    mine_half, other_half = half_rows(half), half_rows(1 - half)

    def across(at, src, dst, j):
        return remote(src, dst, s_one.at[at], r_one.at[at], flip(me, j))

    def aside(at, src, dst):
        return pltpu.make_async_remote_copy(
            src_ref=src, dst_ref=dst, send_sem=s_one.at[at], recv_sem=r_one.at[at],
            device_id={"rows": beside}, device_id_type=MESH,
        )

    barrier = pltpu.get_barrier_semaphore()
    for j in range(1, GROUPS):
        pl.semaphore_signal(barrier, inc=1, device_id={"grp": flip(me, j)}, device_id_type=MESH)

    def greet(k):
        pl.semaphore_signal(barrier, inc=1, device_id={"rows": (row + k + 1) % size}, device_id_type=MESH)

    each(size - 1, greet)
    pl.semaphore_wait(barrier, GROUPS - 1 + size - 1)

    def move_in(src, dst, send, recv, i, j):
        to = flip(me, j)
        return remote(src.at[to * count + i], dst.at[i, me], send.at[i, j], recv.at[i, j], to)

    def start_in(src, dst, send, recv, i):
        for j in (2, 3):
            move_in(src, dst, send, recv, i, j).start()

    def own_in(src, dst, send, i):
        return pltpu.make_async_copy(src.at[me * count + i], dst.at[i, me], send.at[i, 0])

    weights = (None, (wqkv_in.at[0], wqkv), (wup_in.at[0], wup), (wdown_in.at[0], wdown))

    def own_weight(k):
        src, dst = weights[k]
        return pltpu.make_async_copy(src, dst.at[me], s_w.at[k, 0])

    def send_table(j):
        return remote(table.at[me], table.at[me], s_w.at[0, j], r_w.at[0, j], flip(me, j))

    def send_weight(k, j):
        src, dst = weights[k]
        if j == 1:
            return remote(src, dst.at[me], s_w.at[k, 1], r_w.at[k, 1], flip(me, 1))
        if j == 2 and k == 1:
            return remote(src, dst.at[me], s_w.at[k, 2], r_w.at[k, 2], flip(me, 2))
        if j == 2:
            part = weights[k][0].at[mine_half]
            return remote(part, dst.at[me, mine_half], s_w.at[k, 2], r_w.at[k, 2], flip(me, 2))
        got = dst.at[flip(me, 2)]
        return remote(got, got, s_w.at[k, 3], r_w.at[k, 3], flip(me, 1))

    def pass_weight(k, rows):
        block = weights[k][1].at[flip(me, 2), rows]
        return aside(30 + k, block, block)

    def got_weight(k, j):
        dst = weights[k][1]
        block = dst.at[flip(me, j)] if j != 2 or k == 1 else dst.at[flip(me, j), mine_half]
        remote(block, block, s_w.at[k, j], r_w.at[k, j], flip(me, 1)).wait_recv()

    for c in range(2):
        table[me, c : c + 1, :] = qv_bias[:, c * WIDTH : (c + 1) * WIDTH]
    for c in range(PARTS):
        table[me, UP_BIAS + c : UP_BIAS + c + 1, :] = up_bias[:, c * WIDTH : (c + 1) * WIDTH]
    table[me, DOWN_BIAS : DOWN_BIAS + 1, :] = down_bias[...]
    table[me, GAIN_TWO : GAIN_TWO + 1, :] = gain_two[...].reshape(1, WIDTH)
    table[me, SHIFT_TWO : SHIFT_TWO + 1, :] = shift_two[...].reshape(1, WIDTH)
    table[me, OUT_BIAS:TABLE, :] = jnp.zeros((TABLE - OUT_BIAS, WIDTH), F32)
    for j in (2, 3, 1):
        send_table(j).start()
    own_weight(1).start()
    send_weight(1, 2).start()
    send_weight(1, 1).start()
    for k in range(2, 4):
        own_weight(k).start()
        send_weight(k, 2).start()

    def near_x(i):
        own_in(x_in, x, s_x, i).start()
        move_in(x_in, x, s_x, r_x, i, 1).start()

    def near_dy(i):
        own_in(dy_in, dy, s_dy, i).start()
        move_in(dy_in, dy, s_dy, r_dy, i, 1).start()

    each(count, near_x)
    for k in range(2, 4):
        send_weight(k, 1).start()
    each(count, near_dy)

    g_qkv[...] = jnp.zeros_like(g_qkv)
    acc[...] = jnp.zeros_like(acc)
    vec[...] = jnp.zeros_like(vec)
    up_sum[...] = jnp.zeros_like(up_sum)
    for g in range(GROUPS):
        hidden_s[g, WIDTH:, :] = jnp.ones((16, SEQ_LEN), BF16)
    wout_t[...] = wout[...].T

    for j in range(1, GROUPS):
        block = table.at[flip(me, j)]
        remote(block, block, s_w.at[0, j], r_w.at[0, j], flip(me, j)).wait_recv()
    for g in range(GROUPS):
        vectors = [a[...].reshape(1, D)[:, g * WIDTH : (g + 1) * WIDTH] for a in (out_bias, gain_one, shift_one)]
        rows = jnp.concatenate([table[g, 0:OUT_BIAS, :]] + vectors + [jnp.zeros((TABLE - COLS, WIDTH), F32)])
        cols[g, :, 0:TABLE] = rows.T

    def col(g, at):
        return cols[g, :, at : at + 1]

    def lane_col(g, at):
        return g * LANE_COLS + (at if at < UP_BIAS else at - PARTS)

    def add_sum(g, at, value):
        vec[lane_col(g, at)] += lane_part(value)

    def rows_of(g):
        return pl.ds(pl.multiple_of(g * WIDTH, WIDTH), WIDTH)

    def fwd_save(slot, i, g):
        return pltpu.make_async_copy(fwd.at[slot], fwd_st.at[i, g], s_fwd.at[slot])

    def bwd_save(slot, i, g):
        return pltpu.make_async_copy(bwd.at[slot], bwd_st.at[i, g], s_bwd.at[slot])

    def fwd_load(slot, i, g):
        return pltpu.make_async_copy(fwd_st.at[i, g], fwd.at[slot], s_fwd.at[slot])

    def bwd_load(slot, i, g):
        return pltpu.make_async_copy(bwd_st.at[i, g], bwd.at[slot], s_bwd.at[slot])

    def send_lo(i, j):
        to = flip(me, j)
        return remote(lo_s.at[to], lo_out.at[me * count + i], s_lo.at[i, j], r_lo.at[i, j], to)

    def own_lo(i):
        return pltpu.make_async_copy(lo_s.at[me], lo_out.at[me * count + i], s_lo.at[i, 0])

    def attend(i, j):
        first = i == 0
        label = seg[pl.ds(me * count + i, 1), :]
        ids = lax.broadcasted_iota(jnp.int32, (16, SEQ_LEN), 0)
        hot = (ids == label).astype(F32)
        hot_k = hot.astype(BF16)
        hot_q = jnp.where(ids < 4, (1.0 - hot) * MASKED, 0.0).astype(BF16)

        g = flip(me, j)
        slot = j % 2

        @pl.when(j == 0)
        def _():
            own_in(x_in, x, s_x, i).wait()

        @pl.when(j > 0)
        def _():
            block = x.at[i, g]
            remote(block, block, s_x.at[i, j], r_x.at[i, j], g).wait_recv()

        @pl.when(first & (j == 0))
        def _():
            own_weight(1).wait()

        @pl.when(first & (j == 1))
        def _():
            got_weight(1, 1)

        @pl.when(first & (j == 3))
        def _():
            got_weight(1, 3)

        @pl.when(first)
        def _():
            wqkv_t[g] = wqkv[g].T

        @pl.when(i * GROUPS + j >= 2)
        def _():
            fwd_save(slot, 0, 0).wait()

        xg = x[i, g]
        q = (nn(wqkv_t[g, 0:WIDTH, :], xg) + col(g, Q_BIAS)).astype(BF16) * jnp.asarray(SCALE, BF16)
        k = nn(wqkv_t[g, WIDTH : 2 * WIDTH, :], xg).astype(BF16)
        v = (nn(wqkv_t[g, 2 * WIDTH :, :], xg) + col(g, V_BIAS)).astype(BF16)
        fwd[slot, V_AT:FWD_ROWS, :] = v
        for h in range(HEADS_GROUP):
            part = slice(h * HEAD_DIM, (h + 1) * HEAD_DIM)
            qh = jnp.concatenate([q[part], hot_q])
            kh = jnp.concatenate([k[part], hot_k])
            fwd[slot, Q_AT + h * PAD : Q_AT + (h + 1) * PAD, :] = qh
            fwd[slot, K_AT + h * PAD : K_AT + (h + 1) * PAD, :] = kh
            scores = tn(kh, qh)
            largest = jnp.max(scores, axis=0, keepdims=True)
            powers = jnp.exp(scores - largest)
            inverse = 1.0 / channel_sum(powers)
            e = powers.astype(BF16)
            fwd[slot, E_AT + h * SEQ_LEN : E_AT + (h + 1) * SEQ_LEN, :] = e
            linv_s[i % early * HEADS + g * HEADS_GROUP + h] = inverse
            ctx_s[i % early, pl.ds(pl.multiple_of(g * WIDTH + h * HEAD_DIM, HEAD_DIM), HEAD_DIM), :] = (
                nn(v[part], e) * inverse
            ).astype(BF16)
        fwd_save(slot, i, g).start()

    def prepare(n):
        attend(n // 2, n % 2)

        @pl.when(n == 0)
        def _():
            start_in(x_in, x, s_x, r_x, 0)

        @pl.when(n == early)
        def _():
            got_weight(1, 2)
            send_weight(1, 3).start()
            for k in range(2, 4):
                got_weight(k, 2)
                pass_weight(k, mine_half).start()
            start_in(dy_in, dy, s_dy, r_dy, 0)

        @pl.when(n == 2 * early - 2)
        def _():
            for k in range(2, 4):
                pass_weight(k, other_half).wait_recv()
                send_weight(k, 3).start()

    def sequence(i):
        first = i == 0

        @pl.when(i + 1 < count)
        def _():
            start_in(x_in, x, s_x, r_x, i + 1)

        def attend_from(j, carry):
            attend(i, j)
            return carry

        lax.fori_loop(2 if early == count else jnp.where(i < early, 2, 0), GROUPS, attend_from, 0)

        @pl.when(i + 1 < count)
        def _():
            start_in(dy_in, dy, s_dy, r_dy, i + 1)

        def mix(g, carry):
            total, square = carry
            branch = (nn(wout_t[rows_of(g), :], ctx_s[i % early]) + col(g, OUT_BIAS)).astype(BF16)
            summed = branch.astype(F32) + x[i, g].astype(F32)
            summed_s[g] = summed
            return total + fold(summed), square + fold(summed * summed)

        total, square = over(GROUPS, mix, (zero, zero), 4)
        center1 = channel_sum(total) / D
        inverse1 = lax.rsqrt(channel_sum(square) / D - center1 * center1 + EPS)

        @pl.when(first)
        def _():
            for k in range(2, 4):
                own_weight(k).wait()
                got_weight(k, 1)
                got_weight(k, 3)

            def turn(g):
                wup_t[g] = wup[g].T
                wdown_t[g] = wdown[g].T

            each(GROUPS, turn)

        def feed(g, carry):
            total, square = carry
            normed = (summed_s[g] - center1) * inverse1
            hidden = (normed * col(g, GAIN_ONE) + col(g, SHIFT_ONE)).astype(BF16)
            hidden_s[g, 0:WIDTH, :] = hidden
            for part in range(PARTS):
                rows = slice(part * WIDTH, (part + 1) * WIDTH)
                u = nn(wup_t[g, rows, :], hidden) + col(g, UP_BIAS + part)
                act, slope = gelu_pair(u)
                act_s[g, rows, :] = act.astype(BF16)
                slope_s[g, rows, :] = slope.astype(BF16)
            summed2 = hidden.astype(F32) + nn(wdown[g], act_s[g]) + col(g, DOWN_BIAS)
            summed2_s[g] = summed2
            return total + fold(summed2), square + fold(summed2 * summed2)

        total, square = over(GROUPS, feed, (zero, zero), 4)
        center2 = channel_sum(total) / D
        inverse2 = lax.rsqrt(channel_sum(square) / D - center2 * center2 + EPS)

        @pl.when(i > 0)
        def _():
            own_lo(i - 1).wait()
            for j in range(1, GROUPS):
                send_lo(i - 1, j).wait_send()

        own_in(dy_in, dy, s_dy, i).wait()
        for j in range(1, GROUPS):
            block = dy.at[i, flip(me, j)]
            remote(block, block, s_dy.at[i, j], r_dy.at[i, j], flip(me, j)).wait_recv()

        def finish(g, carry):
            sum_e, sum_en = carry
            normed = (summed2_s[g] - center2) * inverse2
            gain = col(g, GAIN_TWO)
            lo_s[g] = (normed * gain + col(g, SHIFT_TWO)).astype(BF16)
            grad = dy[i, g].astype(F32)
            product = grad * normed
            add_sum(g, GAIN_TWO, product)
            add_sum(g, SHIFT_TWO, grad)
            summed2_s[g] = normed
            return sum_e + fold(grad * gain), sum_en + fold(product * gain)

        sum_e, sum_en = over(GROUPS, finish, (zero, zero), 4)
        mean_e = channel_sum(sum_e) / D
        mean_en = channel_sum(sum_en) / D

        own_lo(i).start()
        for j in range(1, GROUPS):
            send_lo(i, j).start()

        def feed_back(g, carry):
            sum_h, sum_hn = carry
            normed2 = summed2_s[g]
            scaled = dy[i, g].astype(F32) * col(g, GAIN_TWO)
            grad2 = (inverse2 * (scaled - mean_e - normed2 * mean_en)).astype(BF16)
            wide = grad2.astype(F32)
            add_sum(g, DOWN_BIAS, wide)
            for part in range(PARTS):
                rows = slice(part * WIDTH, (part + 1) * WIDTH)
                up_grad = (nn(wdown_t[g, rows, :], grad2) * slope_s[g, rows, :].astype(F32)).astype(BF16)
                up_grad_s[rows, :] = up_grad
            both = nt(hidden_s[g], up_grad_s[...])
            acc[0, g] += both[0:WIDTH]
            up_sum[g] += both[WIDTH : WIDTH + 8]
            acc[1, g] += nt(grad2, act_s[g])
            hidden_grad = (wide + nn(wup[g], up_grad_s[...])).astype(BF16)
            hidden_grad_s[rows_of(g), :] = hidden_grad
            grad1 = hidden_grad.astype(F32)
            normed1 = (summed_s[g] - center1) * inverse1
            product = grad1 * normed1
            gain = col(g, GAIN_ONE)
            add_sum(g, GAIN_ONE, product)
            add_sum(g, SHIFT_ONE, grad1)
            return sum_h + fold(grad1 * gain), sum_hn + fold(product * gain)

        sum_h, sum_hn = over(GROUPS, feed_back, (zero, zero), 4)
        mean_h = channel_sum(sum_h) / D
        mean_hn = channel_sum(sum_hn) / D

        def norm_back(g):
            normed1 = (summed_s[g] - center1) * inverse1
            scaled = hidden_grad_s[rows_of(g), :].astype(F32) * col(g, GAIN_ONE)
            summed_grad = (inverse1 * (scaled - mean_h - normed1 * mean_hn)).astype(BF16)
            hidden_grad_s[rows_of(g), :] = summed_grad
            add_sum(g, OUT_BIAS, summed_grad.astype(F32))

        for g in range(GROUPS):
            norm_back(g)

        def mix_back(g):
            slot = g
            ctx = ctx_s[i % early, rows_of(g), :]
            acc[2, g] += nt(ctx, hidden_grad_s[...])
            ctx_grad = nn(wout[rows_of(g), :], hidden_grad_s[...]).astype(BF16).astype(F32)
            for h in range(HEADS_GROUP):
                part = slice(h * HEAD_DIM, (h + 1) * HEAD_DIM)
                grad = (ctx_grad[part] * linv_s[i % early * HEADS + g * HEADS_GROUP + h]).astype(BF16)
                bwd[slot, h * HEAD_DIM : (h + 1) * HEAD_DIM, :] = grad
                middle_s[i * HEADS + g * HEADS_GROUP + h] = channel_sum(grad.astype(F32) * ctx[part].astype(F32))
            bwd[slot, WIDTH:BWD_ROWS, :] = hidden_grad_s[rows_of(g), :]
            bwd_save(slot, i, g).start()

        @pl.when(i > 0)
        def _():
            for g in range(GROUPS):
                bwd_save(g, 0, 0).wait()

        for g in range(GROUPS):
            mix_back(g)

    each(2 * early, prepare)
    each(count, sequence)
    for slot in range(2):
        fwd_save(slot, 0, 0).wait()
    for slot in range(GROUPS):
        bwd_save(slot, 0, 0).wait()

    def unit_of(u):
        return u % count, GROUPS - 1 - u // count

    def load(u):
        i, j = unit_of(u)
        g = flip(me, j)
        fwd_load(u % 2, i, g).start()
        bwd_load(u % 2, i, g).start()

    def send_dx(i, j):
        to = flip(me, j)
        return remote(x.at[i, to], dx_out.at[me * count + i], s_dx.at[i, j], r_dx.at[i, j], to)

    def own_dx(i):
        return pltpu.make_async_copy(x.at[i, me], dx_out.at[me * count + i], s_dx.at[i, 0])

    def when(condition, body):
        if condition is True:
            body()
        else:
            pl.when(condition)(body)

    depth = size // 2
    level = row // 2
    owners = all_l.shape[1]
    per_half = owners // 2
    cut = WIDTH // 2 // per_half
    pair_groups = (flip(me, 1), flip(me, 3))
    kept = (me, flip(me, 2))
    outs = (up_out, down_out, None)

    def peers(n, body):
        def run(k):
            body(k + 1)

        each(n - 1, run)

    def along(kind, src, dst, k, sided):
        to = (level + k) % depth * 2 + half if sided else (row + k) % size
        return pltpu.make_async_remote_copy(
            src_ref=src, dst_ref=dst, send_sem=s_row.at[kind, k], recv_sem=r_row.at[kind, k],
            device_id={"rows": to}, device_id_type=MESH,
        )

    def line(sided):
        return (depth, level) if sided else (size, row)

    def capped(at, n, length):
        return at if n == length else jnp.clip(at - (length - n) // 2, 0, n - 1)

    def owns(at, n, length):
        first = (length - n) // 2
        return True if n == length else (at >= first) & (at < first + n)

    def scatter(kind, parts, landing, sided, act):
        n = parts.shape[0]
        length, here = line(sided)

        def one(k):
            to = (here + k) % length
            piece = parts.at[capped(to, n, length)]
            when(owns(to, n, length), lambda: act(along(kind, piece, landing.at[k], k, sided)))

        peers(length, one)

    def scatter_got(kind, parts, landing, sided):
        peers(line(sided)[0], lambda k: along(kind, parts.at[0], landing.at[k], k, sided).wait_recv())

    def spread_out(kind, landing, sided, act):
        n = landing.shape[0]
        length, here = line(sided)
        own = landing.at[capped(here, n, length)]
        when(owns(here, n, length), lambda: peers(length, lambda k: act(along(kind, own, own, k, sided))))

    def spread_got(kind, landing, sided):
        n = landing.shape[0]
        length, here = line(sided)
        peers(
            length,
            lambda k: when(
                owns((here + length - k) % length, n, length),
                lambda: along(kind, landing.at[0], landing.at[0], k, sided).wait_recv(),
            ),
        )

    def start(copy):
        copy.start()

    def sent(copy):
        copy.wait_send()

    def pair_copy(b):
        return across(b, pair_t.at[b], pair_l.at[b], 1)

    def side_copy(b):
        return aside(3 + b, side_t.at[b], side_l.at[b])

    def far_copy(b):
        return across(6 + b, far_t.at[b], far_l.at[b], 2)

    def out_copy(b, rows):
        return aside(9 + b, outs[b].at[rows], outs[b].at[rows])

    def pair_send(b):
        for at in range(2):
            pair_t[b, at] = acc[b, pair_groups[at]].astype(BF16)
        pair_copy(b).start()

    def side_send(b):
        pair_copy(b).wait_recv()
        for at in range(2):
            acc[b, kept[at]] += pair_l[b, at].astype(F32)
            side_t[b, at] = acc[b, kept[at], other_half, :].astype(BF16)
        side_copy(b).start()

    def far_send(b):
        side_copy(b).wait_recv()
        acc[b, me, mine_half, :] += side_l[b, 0].astype(F32)
        far_t[b] = (acc[b, kept[1], mine_half, :] + side_l[b, 1].astype(F32)).astype(BF16)
        far_copy(b).start()

    def cut_send(b):
        far_copy(b).wait_recv()
        total = acc[b, me, mine_half, :] + far_l[b].astype(F32)
        for o in range(owners):
            rows = o % per_half * cut
            lanes = o // per_half * HALF
            cut_t[b, o] = total[rows : rows + cut, lanes : lanes + HALF].astype(BF16)
        scatter(b, cut_t.at[b], cut_l.at[b], True, start)

    def all_send(b):
        def close():
            scatter_got(b, cut_t.at[b], cut_l.at[b], True)
            own = capped(level, owners, depth)
            total = cut_t[b, own].astype(F32)
            for k in range(1, depth):
                total = total + cut_l[b, k].astype(F32)
            all_l[b, own] = total.astype(BF16)

        when(owns(level, owners, depth), close)
        spread_out(3 + b, all_l.at[b], True, start)

    def joined(b):
        spread_got(3 + b, all_l.at[b], True)
        sides = [
            jnp.concatenate([all_l[b, side * per_half + o] for o in range(per_half)]) for side in range(2)
        ]
        return jnp.concatenate(sides, axis=1)

    def out_send(b):
        outs[b][mine_half, :] = joined(b)
        out_copy(b, mine_half).start()

    def mix_part(g, rows):
        return mix_out.at[g, rows]

    def mix_far(g):
        return across(12, mix_part(g, mine_half), mix_part(g, mine_half), 2)

    def mix_beside(at, rows):
        return aside(13 + at, mix_part(kept[at], rows), mix_part(kept[at], rows))

    def mix_core(at, g):
        return across(15 + at, mix_out.at[g], mix_out.at[g], 1)

    def mix_far_send():
        mix_out[me, mine_half, :] = joined(2)
        mix_far(me).start()
        mix_beside(0, mine_half).start()

    def mix_beside_send():
        mix_far(flip(me, 2)).wait_recv()
        mix_beside(1, mine_half).start()

    def mix_core_send():
        for at in range(2):
            mix_beside(at, other_half).wait_recv()
            mix_core(at, kept[at]).start()

    def early_copy(j):
        return across(17 + j, sum_t.at[flip(me, j)], sum_l.at[j], j)

    def shared_copy(j):
        return across(20 + j, shared_out.at[me], shared_out.at[me], j)

    def end_copy(j):
        return across(23 + j, end_t.at[j], end_l.at[j], j)

    def lane_rows(g, columns):
        return [jnp.sum(vec[lane_col(g, c)].T, axis=0, keepdims=True) for c in columns]

    def early_send():
        for g in range(GROUPS):
            zeros = [jnp.zeros((1, WIDTH), F32)] * 2
            up = [up_sum[g, 0:1, c * WIDTH : (c + 1) * WIDTH] for c in range(PARTS)]
            rows = zeros + up + lane_rows(g, range(DOWN_BIAS, COLS)) + zeros * ((TABLE - COLS) // 2)
            sum_t[g] = jnp.concatenate(rows)
        for j in range(1, GROUPS):
            early_copy(j).start()

    def early_row_send():
        total = sum_t[me]
        for j in range(1, GROUPS):
            early_copy(j).wait_recv()
            total = total + sum_l[j]
        sum_row_t[...] = total
        peers(size, lambda k: along(8, sum_row_t, sum_row_l.at[k], k, False).start())

    def shared_send():
        total = sum_row_t[...]
        peers(size, lambda k: along(8, sum_row_t, sum_row_l.at[k], k, False).wait_recv())
        for k in range(1, size):
            total = total + sum_row_l[k]
        sums_out[...] = total
        shared_out[me] = total
        for j in range(1, GROUPS):
            shared_copy(j).start()

    qowners = qall_l.shape[0]
    qcut = WIDTH // qowners

    def qpair_copy(at):
        return across(27 + at, qpair_t.at[at], qpair_l.at[at], 1)

    def qpiece_copy():
        return across(29, qpiece_t, qpiece_l, 2)

    def qpair_send(at, j):
        qpair_t[at] = g_qkv[flip(me, j)].astype(BF16)
        qpair_copy(at).start()

    def qpieces(at, g, parts, landing, kind):
        qpair_copy(at).wait_recv()
        for o in range(qowners):
            rows = slice(o * qcut, (o + 1) * qcut)
            parts[o] = (g_qkv[g, rows, :] + qpair_l[at, rows, :].astype(F32)).astype(BF16)
        scatter(kind, parts, landing, False, start)

    def qtotal(parts, landing, kind):
        scatter_got(kind, parts, landing, False)
        total = parts[capped(row, qowners, size)].astype(F32)
        for k in range(1, size):
            total = total + landing[k].astype(F32)
        return total

    def qfar_send():
        qpieces(0, flip(me, 2), qfar_t, qfar_l, 6)

    def qpiece_send():
        def close():
            qpiece_t[...] = qtotal(qfar_t, qfar_l, 6).astype(BF16)
            qpiece_copy().start()

        when(owns(row, qowners, size), close)

    def end_sums(g):
        return jnp.concatenate(lane_rows(g, (Q_BIAS, V_BIAS)) + [jnp.zeros((6, WIDTH), F32)])

    def qcut_send():
        qpieces(1, me, qcut_t, qcut_l, 7)
        sums = end_sums(me)
        for j in range(1, GROUPS):
            end_copy(j).wait_recv()
            sums = sums + end_l[j]
        end_row_t[...] = sums
        peers(size, lambda k: along(9, end_row_t, end_row_l.at[k], k, False).start())

    def qall_send():
        def close():
            total = qtotal(qcut_t, qcut_l, 7)
            qpiece_copy().wait_recv()
            qall_l[capped(row, qowners, size)] = (total + qpiece_l[...].astype(F32)).astype(BF16)

        when(owns(row, qowners, size), close)
        spread_out(10, qall_l, False, start)

    def qclose():
        peers(size, lambda k: along(9, end_row_t, end_row_l.at[k], k, False).wait_recv())
        sums = end_row_t[...]
        for k in range(1, size):
            sums = sums + end_row_l[k]
        sums_out[0:2, :] = sums[0:2]
        spread_got(10, qall_l, False)
        for o in range(qowners):
            qkv_out[o * qcut : (o + 1) * qcut, :] = qall_l[o]

    UP, DOWN, MIX = 0, 1, 2
    plan = {
        1: [lambda: side_send(MIX), early_row_send],
        2: [lambda: side_send(UP)],
        4: [lambda: qpair_send(0, 3), lambda: side_send(DOWN)],
        5: [lambda: far_send(MIX), shared_send],
        6: [lambda: far_send(UP)],
        7: [lambda: cut_send(MIX)],
        8: [qfar_send],
        9: [lambda: cut_send(UP), lambda: far_send(DOWN)],
        10: [lambda: all_send(MIX)],
        12: [lambda: qpair_send(1, 1), lambda: cut_send(DOWN), lambda: all_send(UP)],
        13: [mix_far_send, qpiece_send],
        15: [lambda: all_send(DOWN), lambda: out_send(UP)],
    }

    def follow(u):
        for at, steps in plan.items():

            @pl.when(u == count * GROUPS * at // 16 - 1)
            def _():
                for step in steps:
                    step()

    load(0)
    for b in (MIX, UP, DOWN):
        pair_send(b)
    early_send()

    def unit(u):
        i, j = unit_of(u)
        g = flip(me, j)
        slot = u % 2
        fwd_load(slot, i, g).wait()
        bwd_load(slot, i, g).wait()

        @pl.when(u + 1 < count * GROUPS)
        def _():
            load(u + 1)

        for h in range(HEADS_GROUP):
            e = fwd[slot, E_AT + h * SEQ_LEN : E_AT + (h + 1) * SEQ_LEN, :]
            q = fwd[slot, Q_AT + h * PAD : Q_AT + h * PAD + HEAD_DIM, :]
            k = fwd[slot, K_AT + h * PAD : K_AT + h * PAD + HEAD_DIM, :]
            v = fwd[slot, V_AT + h * HEAD_DIM : V_AT + (h + 1) * HEAD_DIM, :]
            grad = bwd[slot, h * HEAD_DIM : (h + 1) * HEAD_DIM, :]
            prob_grad = tn(v, grad)
            score_grad = (e.astype(F32) * (prob_grad - middle_s[i * HEADS + g * HEADS_GROUP + h])).astype(BF16)
            at = h * HEAD_DIM
            act_s[0, 2 * WIDTH + at : 2 * WIDTH + at + HEAD_DIM, :] = nt(grad, e).astype(BF16)
            act_s[0, at : at + HEAD_DIM, :] = (nn(k, score_grad) * SCALE).astype(BF16)
            act_s[0, WIDTH + at : WIDTH + at + HEAD_DIM, :] = nt(q, score_grad).astype(BF16)
        g_qkv[g] += nt(x[i, g], act_s[0, 0:QKV, :])
        add_sum(g, Q_BIAS, act_s[0, 0:WIDTH, :].astype(F32))
        add_sum(g, V_BIAS, act_s[0, 2 * WIDTH : QKV, :].astype(F32))
        into = bwd[slot, WIDTH:BWD_ROWS, :].astype(F32) + nn(wqkv[g], act_s[0, 0:QKV, :])
        x[i, g] = into.astype(BF16)

        @pl.when((j > 0) & (i == count - 1))
        def _():
            end_t[j] = end_sums(g)
            end_copy(j).start()

        @pl.when(j == 1)
        def _():
            send_dx(i, 1).start()

        @pl.when(u % 2 == 1)
        def _():
            late_i, late_j = unit_of(u // 2)
            send_dx(late_i, late_j).start()

        @pl.when(j == 0)
        def _():
            own_dx(i).start()

        follow(u)

    each(count * GROUPS, unit)
    qcut_send()
    mix_beside_send()
    qall_send()
    out_send(DOWN)
    mix_core_send()
    for j in range(1, GROUPS):
        block = shared_out.at[flip(me, j)]
        across(20 + j, block, block, j).wait_recv()
    for b in (UP, DOWN):
        out_copy(b, other_half).wait_recv()
    for at, j in enumerate((1, 3)):
        mix_core(at, flip(me, j)).wait_recv()
    qclose()

    for j in range(1, GROUPS):
        send_table(j).wait_send()
        for k in range(1, 4):
            send_weight(k, j).wait_send()
    for k in range(2, 4):
        pass_weight(k, mine_half).wait_send()
    own_lo(count - 1).wait()
    for j in range(1, GROUPS):
        send_lo(count - 1, j).wait_send()

    def drain(i):
        own_dx(i).wait()
        for j in range(1, GROUPS):
            move_in(x_in, x, s_x, r_x, i, j).wait_send()
            move_in(dy_in, dy, s_dy, r_dy, i, j).wait_send()
            send_lo(i, j).wait_recv()
            send_dx(i, j).wait_send()
            send_dx(i, j).wait_recv()

    each(count, drain)
    for b in range(BLOCKS):
        pair_copy(b).wait_send()
        side_copy(b).wait_send()
        scatter(b, cut_t.at[b], cut_l.at[b], True, sent)
        far_copy(b).wait_send()
        spread_out(3 + b, all_l.at[b], True, sent)
    for b in (UP, DOWN):
        out_copy(b, mine_half).wait_send()
    mix_far(me).wait_send()
    for at in range(2):
        mix_beside(at, mine_half).wait_send()
        mix_core(at, kept[at]).wait_send()
        qpair_copy(at).wait_send()
    when(owns(row, qowners, size), lambda: qpiece_copy().wait_send())
    for j in range(1, GROUPS):
        early_copy(j).wait_send()
        shared_copy(j).wait_send()
        end_copy(j).wait_send()
    scatter(6, qfar_t, qfar_l, False, sent)
    scatter(7, qcut_t, qcut_l, False, sent)
    spread_out(10, qall_l, False, sent)
    peers(size, lambda k: along(8, sum_row_t, sum_row_l.at[k], k, False).wait_send())
    peers(size, lambda k: along(9, end_row_t, end_row_l.at[k], k, False).wait_send())


def layer(size, x, dy, *rest):
    count = x.shape[0] // GROUPS
    here = pl.BlockSpec(memory_space=pl.ANY)
    vmem = pl.BlockSpec(memory_space=pltpu.VMEM)
    grads = [
        ((WIDTH, QKV), BF16),
        ((WIDTH, UNITS), BF16),
        ((WIDTH, UNITS), BF16),
        ((GROUPS, WIDTH, UNITS), BF16),
        ((TABLE, WIDTH), F32),
        ((GROUPS, TABLE, WIDTH), F32),
    ]
    early = min(count, EARLY)
    depth = size // 2
    owners = 2 * owners_of(depth // 2, WIDTH // 32)
    piece = (WIDTH // owners, HALF)
    qowners = owners_of(size, WIDTH // 16)
    qpiece = (WIDTH // qowners, QKV)
    token = (GROUPS, WIDTH, SEQ_LEN)
    dma = pltpu.SemaphoreType.DMA
    return pl.pallas_call(
        functools.partial(layer_kernel, size),
        out_shape=[jax.ShapeDtypeStruct(x.shape, BF16)] * 2
        + [
            jax.ShapeDtypeStruct((count, GROUPS, FWD_ROWS, SEQ_LEN), BF16),
            jax.ShapeDtypeStruct((count, GROUPS, BWD_ROWS, SEQ_LEN), BF16),
        ]
        + [jax.ShapeDtypeStruct(s, t) for s, t in grads],
        in_specs=[here, here, vmem, here, here, here] + [vmem] * 9,
        out_specs=[here] * 4 + [vmem] * len(grads),
        scratch_shapes=[
            pltpu.VMEM((count,) + token, BF16),
            pltpu.VMEM((count,) + token, BF16),
            pltpu.VMEM((GROUPS, WIDTH, QKV), BF16),
            pltpu.VMEM((GROUPS, WIDTH, UNITS), BF16),
            pltpu.VMEM((GROUPS, WIDTH, UNITS), BF16),
            pltpu.VMEM((GROUPS, TABLE, WIDTH), F32),
            pltpu.VMEM((GROUPS, WIDTH, 128), F32),
            pltpu.VMEM((GROUPS, QKV, WIDTH), BF16),
            pltpu.VMEM((GROUPS, UNITS, WIDTH), BF16),
            pltpu.VMEM((GROUPS, UNITS, WIDTH), BF16),
            pltpu.VMEM((D, D), BF16),
            pltpu.VMEM((GROUPS * LANE_COLS, WIDTH, 128), F32),
            pltpu.VMEM((GROUPS, 8, UNITS), F32),
            pltpu.VMEM((2, FWD_ROWS, SEQ_LEN), BF16),
            pltpu.VMEM((GROUPS, BWD_ROWS, SEQ_LEN), BF16),
            pltpu.VMEM((count * HEADS, 1, SEQ_LEN), F32),
            pltpu.VMEM((early * HEADS, 1, SEQ_LEN), F32),
            pltpu.VMEM((early, D, SEQ_LEN), BF16),
            pltpu.VMEM(token, F32),
            pltpu.VMEM((GROUPS, WIDTH + 16, SEQ_LEN), BF16),
            pltpu.VMEM((GROUPS, UNITS, SEQ_LEN), BF16),
            pltpu.VMEM((GROUPS, UNITS, SEQ_LEN), BF16),
            pltpu.VMEM(token, F32),
            pltpu.VMEM((UNITS, SEQ_LEN), BF16),
            pltpu.VMEM((D, SEQ_LEN), BF16),
            pltpu.VMEM(token, BF16),
            pltpu.VMEM((BLOCKS, GROUPS, WIDTH, UNITS), F32),
            pltpu.VMEM((GROUPS, WIDTH, QKV), F32),
            pltpu.VMEM((BLOCKS, 2, WIDTH, UNITS), BF16),
            pltpu.VMEM((BLOCKS, 2, WIDTH, UNITS), BF16),
            pltpu.VMEM((BLOCKS, 2, WIDTH // 2, UNITS), BF16),
            pltpu.VMEM((BLOCKS, 2, WIDTH // 2, UNITS), BF16),
            pltpu.VMEM((BLOCKS, owners) + piece, BF16),
            pltpu.VMEM((BLOCKS, depth) + piece, BF16),
            pltpu.VMEM((BLOCKS, WIDTH // 2, UNITS), BF16),
            pltpu.VMEM((BLOCKS, WIDTH // 2, UNITS), BF16),
            pltpu.VMEM((BLOCKS, owners) + piece, BF16),
            pltpu.VMEM((2, WIDTH, QKV), BF16),
            pltpu.VMEM((2, WIDTH, QKV), BF16),
            pltpu.VMEM((qowners,) + qpiece, BF16),
            pltpu.VMEM((size,) + qpiece, BF16),
            pltpu.VMEM(qpiece, BF16),
            pltpu.VMEM(qpiece, BF16),
            pltpu.VMEM((qowners,) + qpiece, BF16),
            pltpu.VMEM((size,) + qpiece, BF16),
            pltpu.VMEM((qowners,) + qpiece, BF16),
            pltpu.VMEM((GROUPS, TABLE, WIDTH), F32),
            pltpu.VMEM((GROUPS, TABLE, WIDTH), F32),
            pltpu.VMEM((TABLE, WIDTH), F32),
            pltpu.VMEM((size, TABLE, WIDTH), F32),
            pltpu.VMEM((GROUPS, 8, WIDTH), F32),
            pltpu.VMEM((GROUPS, 8, WIDTH), F32),
            pltpu.VMEM((8, WIDTH), F32),
            pltpu.VMEM((size, 8, WIDTH), F32),
        ]
        + [dma((count, GROUPS))] * 8
        + [dma((4, GROUPS))] * 2
        + [dma((34,))] * 2
        + [dma((11, size))] * 2
        + [dma((2,)), dma((GROUPS,))],
        compiler_params=pltpu.CompilerParams(
            vmem_limit_bytes=(64 << 20) - (1 << 17), collective_id=0, has_side_effects=True
        ),
    )(x, dy, *rest)


def local(
    size, layer_input, segment_ids, qkv_weight, qv_bias, out_weight, out_bias, gain_one, shift_one,
    up_weight, up_bias, down_weight, down_bias, gain_two, shift_two, out_grad,
):
    lo, dx, _, _, *grads = layer(
        size, layer_input, out_grad, segment_ids, qkv_weight, up_weight, down_weight, out_weight,
        qv_bias, up_bias, down_bias, gain_two, shift_two, out_bias, gain_one, shift_one,
    )
    lo, dx, g_qkv, g_up, g_down, g_out, qv, out_b, gain1, shift1, up_b, down_b, gain2, shift2 = widen(lo, dx, *grads)
    return lo, dx, g_qkv, qv, g_out, out_b, gain1, shift1, g_up, up_b, g_down, down_b, gain2, shift2


def widen_kernel(
    lo, dx, qkv, up, down, mix, sums, shared,
    lo_o, dx_o, qkv_o, up_o, down_o, mix_o, qv_o, out_o, gain1_o, shift1_o, up_b_o, down_b_o, gain2_o, shift2_o,
):
    for src, out in ((lo, lo_o), (dx, dx_o), (qkv, qkv_o), (up, up_o), (down, down_o), (mix, mix_o)):
        out[...] = src[...].astype(F32).reshape(out.shape)

    @pl.when(pl.program_id(0) == 0)
    def _():
        def own(first, n):
            return jnp.concatenate([sums[first + c : first + c + 1, :] for c in range(n)], axis=1)

        def joint(at):
            return jnp.concatenate([shared[g, at : at + 1, :] for g in range(GROUPS)], axis=1)

        qv_o[...] = own(Q_BIAS, 2)
        up_b_o[...] = own(UP_BIAS, PARTS)
        down_b_o[...] = own(DOWN_BIAS, 1)
        gain2_o[...] = own(GAIN_TWO, 1).reshape(WIDTH)
        shift2_o[...] = own(SHIFT_TWO, 1).reshape(WIDTH)
        for out, at in ((out_o, OUT_BIAS), (gain1_o, GAIN_ONE), (shift1_o, SHIFT_ONE)):
            out[...] = joint(at).reshape(D)


def widen(lo, dx, *grads):
    steps = 4
    part = WIDTH // steps
    data = pl.BlockSpec((lo.shape[0] // steps, WIDTH, SEQ_LEN), lambda i: (i, 0, 0))

    def slab(columns):
        return pl.BlockSpec((part, columns), lambda i: (i, 0)), pl.BlockSpec((1, part, columns), lambda i: (0, i, 0))

    def whole(shape):
        return pl.BlockSpec(shape, lambda i: (0,) * len(shape), pipeline_mode=pl.Buffered(1))

    qkv_in, qkv_out = slab(QKV)
    unit_in, unit_out = slab(UNITS)
    mix_in = pl.BlockSpec((1, D // steps, D), lambda i: (i, 0, 0))
    mix_out = pl.BlockSpec((D // steps, D), lambda i: (i, 0))
    wide = [(1, WIDTH, QKV), (1, WIDTH, UNITS), (1, WIDTH, UNITS), (D, D)]
    vectors = [(1, 2 * WIDTH), (D,), (D,), (D,), (1, UNITS), (1, WIDTH), (WIDTH,), (WIDTH,)]
    return pl.pallas_call(
        widen_kernel,
        grid=(steps,),
        out_shape=[jax.ShapeDtypeStruct(s, F32) for s in [lo.shape, dx.shape] + wide + vectors],
        in_specs=[data, data, qkv_in, unit_in, unit_in, mix_in] + [whole(a.shape) for a in grads[4:]],
        out_specs=[data, data, qkv_out, unit_out, unit_out, mix_out] + [whole(s) for s in vectors],
        compiler_params=pltpu.CompilerParams(vmem_limit_bytes=62 << 20),
    )(lo, dx, *grads)


def solution(mesh):
    group = P("grp", None, None)
    data = P("rows", "grp", None)
    in_specs = (
        data, P("rows", None), group, P("grp", None), P(), P(), P(), P(),
        group, P("grp", None), group, P("grp", None), P("grp"), P("grp"), data,
    )
    out_specs = (
        data, data, group, P("grp", None), P(), P(), P(), P(),
        group, P("grp", None), group, P("grp", None), P("grp"), P("grp"),
    )
    return jax.shard_map(functools.partial(local, mesh.shape["rows"]), mesh=mesh, in_specs=in_specs, out_specs=out_specs, check_vma=False)
```

```python
import functools

import jax
import jax.numpy as jnp
from jax import lax
from jax.experimental import pallas as pl
from jax.experimental.pallas import tpu as pltpu
from jax.sharding import PartitionSpec as P

D = 768
HEAD_DIM = 64
SEQ_LEN = 512
GROUPS = 4
WIDTH = D // GROUPS
HEADS_GROUP = WIDTH // HEAD_DIM
HEADS = D // HEAD_DIM
QKV = 3 * WIDTH
UNITS = 768
PARTS = UNITS // WIDTH
PAD = HEAD_DIM + 16
MASKED = -1e30
EPS = 1e-05
SCALE = HEAD_DIM ** (-0.5)
BLOCKS = 3
EARLY = 2
HALF = UNITS // 2

F32 = jnp.float32
BF16 = jnp.bfloat16
MESH = pl.DeviceIdType.MESH

Q_BIAS, V_BIAS, UP_BIAS, DOWN_BIAS, GAIN_TWO, SHIFT_TWO, OUT_BIAS, GAIN_ONE, SHIFT_ONE = 0, 1, 2, 6, 7, 8, 9, 10, 11
COLS = 12
LANE_COLS = COLS - PARTS
TABLE = 16

E_AT = 0
Q_AT = HEADS_GROUP * SEQ_LEN
K_AT = Q_AT + HEADS_GROUP * PAD
V_AT = K_AT + HEADS_GROUP * PAD
FWD_ROWS = V_AT + WIDTH
BWD_ROWS = 2 * WIDTH


def nn(a, b):
    return lax.dot_general(a, b, (((1,), (0,)), ((), ())), preferred_element_type=F32)


def nt(a, b):
    return lax.dot_general(a, b, (((1,), (1,)), ((), ())), preferred_element_type=F32)


def tn(a, b):
    return lax.dot_general(a, b, (((0,), (0,)), ((), ())), preferred_element_type=F32)


def lane_part(value):
    total = value[:, 0:128]
    for at in range(128, SEQ_LEN, 128):
        total = total + value[:, at : at + 128]
    return total


def channel_sum(value):
    return jnp.sum(value, axis=0, keepdims=True)


def fold(value):
    return jnp.sum(value.reshape(value.shape[0] // 8, 8, SEQ_LEN), axis=0)


def spread(column):
    return jnp.concatenate([column] * (SEQ_LEN // 128), axis=1)


def gelu_pair(u):
    half_erf = 0.5 * lax.erf(u * 0.7071067811865476) + 0.5
    density = jnp.exp(u * u * -0.5) * 0.3989422804014327
    return u * half_erf, half_erf + u * density


def flip(me, j):
    return (me + j) % 2 + 2 * ((me // 2 + j // 2) % 2)


def owners_of(rows, parts):
    return max(n for n in range(1, min(rows, parts) + 1) if parts % n == 0)


def layer_kernel(
    size, x_in, dy_in, seg, wqkv_in, wup_in, wdown_in, wout,
    qv_bias, up_bias, down_bias, gain_two, shift_two, out_bias, gain_one, shift_one,
    lo_out, dx_out, fwd_st, bwd_st, qkv_out, up_out, down_out, mix_out, sums_out, shared_out,
    x, dy, wqkv, wup, wdown, table, cols, wqkv_t, wup_t, wdown_t, wout_t, vec, up_sum,
    fwd, bwd, middle_s, linv_s, ctx_s, summed_s, hidden_s, act_s, slope_s, summed2_s,
    up_grad_s, hidden_grad_s, lo_s,
    acc, g_qkv, pair_t, pair_l, side_t, side_l, cut_t, cut_l, far_t, far_l, all_l,
    qpair_t, qpair_l, qfar_t, qfar_l, qpiece_t, qpiece_l, qcut_t, qcut_l, qall_l,
    sum_t, sum_l, sum_row_t, sum_row_l, end_t, end_l, end_row_t, end_row_l,
    s_x, r_x, s_dy, r_dy, s_lo, r_lo, s_dx, r_dx, s_w, r_w, s_one, r_one, s_row, r_row, s_fwd, s_bwd,
):
    count = x.shape[0]
    early = ctx_s.shape[0]
    me = lax.axis_index("grp")
    row = lax.axis_index("rows")
    zero = jnp.zeros((8, SEQ_LEN), F32)

    def over(n, body, init=0, unroll=False):
        return lax.fori_loop(0, n, body, init, unroll=unroll)

    def each(n, body):
        def run(at, carry):
            body(at)
            return carry

        lax.fori_loop(0, n, run, 0)

    def remote(src, dst, send, recv, to):
        return pltpu.make_async_remote_copy(
            src_ref=src, dst_ref=dst, send_sem=send, recv_sem=recv, device_id={"grp": to}, device_id_type=MESH
        )

    half = row % 2
    beside = row + 1 - 2 * half

    def half_rows(at):
        return pl.ds(pl.multiple_of(at * (WIDTH // 2), WIDTH // 2), WIDTH // 2)

    mine_half, other_half = half_rows(half), half_rows(1 - half)

    def across(at, src, dst, j):
        return remote(src, dst, s_one.at[at], r_one.at[at], flip(me, j))

    def aside(at, src, dst):
        return pltpu.make_async_remote_copy(
            src_ref=src, dst_ref=dst, send_sem=s_one.at[at], recv_sem=r_one.at[at],
            device_id={"rows": beside}, device_id_type=MESH,
        )

    barrier = pltpu.get_barrier_semaphore()
    for j in range(1, GROUPS):
        pl.semaphore_signal(barrier, inc=1, device_id={"grp": flip(me, j)}, device_id_type=MESH)

    def greet(k):
        pl.semaphore_signal(barrier, inc=1, device_id={"rows": (row + k + 1) % size}, device_id_type=MESH)

    each(size - 1, greet)
    pl.semaphore_wait(barrier, GROUPS - 1 + size - 1)

    def move_in(src, dst, send, recv, i, j):
        to = flip(me, j)
        return remote(src.at[to * count + i], dst.at[i, me], send.at[i, j], recv.at[i, j], to)

    def start_in(src, dst, send, recv, i):
        for j in (2, 3):
            move_in(src, dst, send, recv, i, j).start()

    def own_in(src, dst, send, i):
        return pltpu.make_async_copy(src.at[me * count + i], dst.at[i, me], send.at[i, 0])

    weights = (None, (wqkv_in.at[0], wqkv), (wup_in.at[0], wup), (wdown_in.at[0], wdown))

    def own_weight(k):
        src, dst = weights[k]
        return pltpu.make_async_copy(src, dst.at[me], s_w.at[k, 0])

    def send_table(j):
        return remote(table.at[me], table.at[me], s_w.at[0, j], r_w.at[0, j], flip(me, j))

    def send_weight(k, j):
        src, dst = weights[k]
        if j == 1:
            return remote(src, dst.at[me], s_w.at[k, 1], r_w.at[k, 1], flip(me, 1))
        if j == 2 and k == 1:
            return remote(src, dst.at[me], s_w.at[k, 2], r_w.at[k, 2], flip(me, 2))
        if j == 2:
            part = weights[k][0].at[mine_half]
            return remote(part, dst.at[me, mine_half], s_w.at[k, 2], r_w.at[k, 2], flip(me, 2))
        got = dst.at[flip(me, 2)]
        return remote(got, got, s_w.at[k, 3], r_w.at[k, 3], flip(me, 1))

    def pass_weight(k, rows):
        block = weights[k][1].at[flip(me, 2), rows]
        return aside(30 + k, block, block)

    def got_weight(k, j):
        dst = weights[k][1]
        block = dst.at[flip(me, j)] if j != 2 or k == 1 else dst.at[flip(me, j), mine_half]
        remote(block, block, s_w.at[k, j], r_w.at[k, j], flip(me, 1)).wait_recv()

    for c in range(2):
        table[me, c : c + 1, :] = qv_bias[:, c * WIDTH : (c + 1) * WIDTH]
    for c in range(PARTS):
        table[me, UP_BIAS + c : UP_BIAS + c + 1, :] = up_bias[:, c * WIDTH : (c + 1) * WIDTH]
    table[me, DOWN_BIAS : DOWN_BIAS + 1, :] = down_bias[...]
    table[me, GAIN_TWO : GAIN_TWO + 1, :] = gain_two[...].reshape(1, WIDTH)
    table[me, SHIFT_TWO : SHIFT_TWO + 1, :] = shift_two[...].reshape(1, WIDTH)
    table[me, OUT_BIAS:TABLE, :] = jnp.zeros((TABLE - OUT_BIAS, WIDTH), F32)
    for j in (2, 3, 1):
        send_table(j).start()
    own_weight(1).start()
    send_weight(1, 2).start()
    send_weight(1, 1).start()
    for k in range(2, 4):
        own_weight(k).start()
        send_weight(k, 2).start()

    def near_x(i):
        own_in(x_in, x, s_x, i).start()
        move_in(x_in, x, s_x, r_x, i, 1).start()

    def near_dy(i):
        own_in(dy_in, dy, s_dy, i).start()
        move_in(dy_in, dy, s_dy, r_dy, i, 1).start()

    each(count, near_x)
    for k in range(2, 4):
        send_weight(k, 1).start()
    each(count, near_dy)

    g_qkv[...] = jnp.zeros_like(g_qkv)
    acc[...] = jnp.zeros_like(acc)
    vec[...] = jnp.zeros_like(vec)
    up_sum[...] = jnp.zeros_like(up_sum)
    for g in range(GROUPS):
        hidden_s[g, WIDTH:, :] = jnp.ones((16, SEQ_LEN), BF16)
    wout_t[...] = wout[...].T

    for j in range(1, GROUPS):
        block = table.at[flip(me, j)]
        remote(block, block, s_w.at[0, j], r_w.at[0, j], flip(me, j)).wait_recv()
    for g in range(GROUPS):
        vectors = [a[...].reshape(1, D)[:, g * WIDTH : (g + 1) * WIDTH] for a in (out_bias, gain_one, shift_one)]
        rows = jnp.concatenate([table[g, 0:OUT_BIAS, :]] + vectors + [jnp.zeros((TABLE - COLS, WIDTH), F32)])
        cols[g, :, 0:TABLE] = rows.T

    def col(g, at):
        return cols[g, :, at : at + 1]

    def lane_col(g, at):
        return g * LANE_COLS + (at if at < UP_BIAS else at - PARTS)

    def add_sum(g, at, value):
        vec[lane_col(g, at)] += lane_part(value)

    def rows_of(g):
        return pl.ds(pl.multiple_of(g * WIDTH, WIDTH), WIDTH)

    def fwd_save(slot, i, g):
        return pltpu.make_async_copy(fwd.at[slot], fwd_st.at[i, g], s_fwd.at[slot])

    def bwd_save(slot, i, g):
        return pltpu.make_async_copy(bwd.at[slot], bwd_st.at[i, g], s_bwd.at[slot])

    def fwd_load(slot, i, g):
        return pltpu.make_async_copy(fwd_st.at[i, g], fwd.at[slot], s_fwd.at[slot])

    def bwd_load(slot, i, g):
        return pltpu.make_async_copy(bwd_st.at[i, g], bwd.at[slot], s_bwd.at[slot])

    def send_lo(i, j):
        to = flip(me, j)
        return remote(lo_s.at[to], lo_out.at[me * count + i], s_lo.at[i, j], r_lo.at[i, j], to)

    def own_lo(i):
        return pltpu.make_async_copy(lo_s.at[me], lo_out.at[me * count + i], s_lo.at[i, 0])

    def attend(i, j):
        first = i == 0
        label = seg[pl.ds(me * count + i, 1), :]
        ids = lax.broadcasted_iota(jnp.int32, (16, SEQ_LEN), 0)
        hot = (ids == label).astype(F32)
        hot_k = hot.astype(BF16)
        hot_q = jnp.where(ids < 4, (1.0 - hot) * MASKED, 0.0).astype(BF16)

        g = flip(me, j)
        slot = j % 2

        @pl.when(j == 0)
        def _():
            own_in(x_in, x, s_x, i).wait()

        @pl.when(j > 0)
        def _():
            block = x.at[i, g]
            remote(block, block, s_x.at[i, j], r_x.at[i, j], g).wait_recv()

        @pl.when(first & (j == 0))
        def _():
            own_weight(1).wait()

        @pl.when(first & (j == 1))
        def _():
            got_weight(1, 1)

        @pl.when(first & (j == 3))
        def _():
            got_weight(1, 3)

        @pl.when(first)
        def _():
            wqkv_t[g] = wqkv[g].T

        @pl.when(i * GROUPS + j >= 2)
        def _():
            fwd_save(slot, 0, 0).wait()

        xg = x[i, g]
        q = (nn(wqkv_t[g, 0:WIDTH, :], xg) + col(g, Q_BIAS)).astype(BF16) * jnp.asarray(SCALE, BF16)
        k = nn(wqkv_t[g, WIDTH : 2 * WIDTH, :], xg).astype(BF16)
        v = (nn(wqkv_t[g, 2 * WIDTH :, :], xg) + col(g, V_BIAS)).astype(BF16)
        fwd[slot, V_AT:FWD_ROWS, :] = v
        for h in range(HEADS_GROUP):
            part = slice(h * HEAD_DIM, (h + 1) * HEAD_DIM)
            qh = jnp.concatenate([q[part], hot_q])
            kh = jnp.concatenate([k[part], hot_k])
            fwd[slot, Q_AT + h * PAD : Q_AT + (h + 1) * PAD, :] = qh
            fwd[slot, K_AT + h * PAD : K_AT + (h + 1) * PAD, :] = kh
            scores = tn(kh, qh)
            largest = jnp.max(scores, axis=0, keepdims=True)
            powers = jnp.exp(scores - largest)
            inverse = 1.0 / channel_sum(powers)
            e = powers.astype(BF16)
            fwd[slot, E_AT + h * SEQ_LEN : E_AT + (h + 1) * SEQ_LEN, :] = e
            linv_s[i % early * HEADS + g * HEADS_GROUP + h] = inverse
            ctx_s[i % early, pl.ds(pl.multiple_of(g * WIDTH + h * HEAD_DIM, HEAD_DIM), HEAD_DIM), :] = (
                nn(v[part], e) * inverse
            ).astype(BF16)
        fwd_save(slot, i, g).start()

    def prepare(n):
        attend(n // 2, n % 2)

        @pl.when(n == 0)
        def _():
            start_in(x_in, x, s_x, r_x, 0)

        @pl.when(n == early)
        def _():
            got_weight(1, 2)
            send_weight(1, 3).start()
            for k in range(2, 4):
                got_weight(k, 2)
                pass_weight(k, mine_half).start()
            start_in(dy_in, dy, s_dy, r_dy, 0)

        @pl.when(n == 2 * early - 2)
        def _():
            for k in range(2, 4):
                pass_weight(k, other_half).wait_recv()
                send_weight(k, 3).start()

    def sequence(i):
        first = i == 0

        @pl.when(i + 1 < count)
        def _():
            start_in(x_in, x, s_x, r_x, i + 1)

        def attend_from(j, carry):
            attend(i, j)
            return carry

        lax.fori_loop(2 if early == count else jnp.where(i < early, 2, 0), GROUPS, attend_from, 0)

        @pl.when(i + 1 < count)
        def _():
            start_in(dy_in, dy, s_dy, r_dy, i + 1)

        def mix(g, carry):
            total, square = carry
            branch = (nn(wout_t[rows_of(g), :], ctx_s[i % early]) + col(g, OUT_BIAS)).astype(BF16)
            summed = branch.astype(F32) + x[i, g].astype(F32)
            summed_s[g] = summed
            return total + fold(summed), square + fold(summed * summed)

        total, square = over(GROUPS, mix, (zero, zero), 4)
        center1 = channel_sum(total) / D
        inverse1 = lax.rsqrt(channel_sum(square) / D - center1 * center1 + EPS)

        @pl.when(first)
        def _():
            for k in range(2, 4):
                own_weight(k).wait()
                got_weight(k, 1)
                got_weight(k, 3)

            def turn(g):
                wup_t[g] = wup[g].T
                wdown_t[g] = wdown[g].T

            each(GROUPS, turn)

        def feed(g, carry):
            total, square = carry
            normed = (summed_s[g] - center1) * inverse1
            hidden = (normed * col(g, GAIN_ONE) + col(g, SHIFT_ONE)).astype(BF16)
            hidden_s[g, 0:WIDTH, :] = hidden
            for part in range(PARTS):
                rows = slice(part * WIDTH, (part + 1) * WIDTH)
                u = nn(wup_t[g, rows, :], hidden) + col(g, UP_BIAS + part)
                act, slope = gelu_pair(u)
                act_s[g, rows, :] = act.astype(BF16)
                slope_s[g, rows, :] = slope.astype(BF16)
            summed2 = hidden.astype(F32) + nn(wdown[g], act_s[g]) + col(g, DOWN_BIAS)
            summed2_s[g] = summed2
            return total + fold(summed2), square + fold(summed2 * summed2)

        total, square = over(GROUPS, feed, (zero, zero), 4)
        center2 = channel_sum(total) / D
        inverse2 = lax.rsqrt(channel_sum(square) / D - center2 * center2 + EPS)

        @pl.when(i > 0)
        def _():
            own_lo(i - 1).wait()
            for j in range(1, GROUPS):
                send_lo(i - 1, j).wait_send()

        own_in(dy_in, dy, s_dy, i).wait()
        for j in range(1, GROUPS):
            block = dy.at[i, flip(me, j)]
            remote(block, block, s_dy.at[i, j], r_dy.at[i, j], flip(me, j)).wait_recv()

        def finish(g, carry):
            sum_e, sum_en = carry
            normed = (summed2_s[g] - center2) * inverse2
            gain = col(g, GAIN_TWO)
            lo_s[g] = (normed * gain + col(g, SHIFT_TWO)).astype(BF16)
            grad = dy[i, g].astype(F32)
            product = grad * normed
            add_sum(g, GAIN_TWO, product)
            add_sum(g, SHIFT_TWO, grad)
            summed2_s[g] = normed
            return sum_e + fold(grad * gain), sum_en + fold(product * gain)

        sum_e, sum_en = over(GROUPS, finish, (zero, zero), 4)
        mean_e = channel_sum(sum_e) / D
        mean_en = channel_sum(sum_en) / D

        own_lo(i).start()
        for j in range(1, GROUPS):
            send_lo(i, j).start()

        def feed_back(g, carry):
            sum_h, sum_hn = carry
            normed2 = summed2_s[g]
            scaled = dy[i, g].astype(F32) * col(g, GAIN_TWO)
            grad2 = (inverse2 * (scaled - mean_e - normed2 * mean_en)).astype(BF16)
            wide = grad2.astype(F32)
            add_sum(g, DOWN_BIAS, wide)
            for part in range(PARTS):
                rows = slice(part * WIDTH, (part + 1) * WIDTH)
                up_grad = (nn(wdown_t[g, rows, :], grad2) * slope_s[g, rows, :].astype(F32)).astype(BF16)
                up_grad_s[rows, :] = up_grad
            both = nt(hidden_s[g], up_grad_s[...])
            acc[0, g] += both[0:WIDTH]
            up_sum[g] += both[WIDTH : WIDTH + 8]
            acc[1, g] += nt(grad2, act_s[g])
            hidden_grad = (wide + nn(wup[g], up_grad_s[...])).astype(BF16)
            hidden_grad_s[rows_of(g), :] = hidden_grad
            grad1 = hidden_grad.astype(F32)
            normed1 = (summed_s[g] - center1) * inverse1
            product = grad1 * normed1
            gain = col(g, GAIN_ONE)
            add_sum(g, GAIN_ONE, product)
            add_sum(g, SHIFT_ONE, grad1)
            return sum_h + fold(grad1 * gain), sum_hn + fold(product * gain)

        sum_h, sum_hn = over(GROUPS, feed_back, (zero, zero), 4)
        mean_h = channel_sum(sum_h) / D
        mean_hn = channel_sum(sum_hn) / D

        def norm_back(g):
            normed1 = (summed_s[g] - center1) * inverse1
            scaled = hidden_grad_s[rows_of(g), :].astype(F32) * col(g, GAIN_ONE)
            summed_grad = (inverse1 * (scaled - mean_h - normed1 * mean_hn)).astype(BF16)
            hidden_grad_s[rows_of(g), :] = summed_grad
            add_sum(g, OUT_BIAS, summed_grad.astype(F32))

        for g in range(GROUPS):
            norm_back(g)

        def mix_back(g):
            slot = g
            ctx = ctx_s[i % early, rows_of(g), :]
            acc[2, g] += nt(ctx, hidden_grad_s[...])
            ctx_grad = nn(wout[rows_of(g), :], hidden_grad_s[...]).astype(BF16).astype(F32)
            for h in range(HEADS_GROUP):
                part = slice(h * HEAD_DIM, (h + 1) * HEAD_DIM)
                grad = (ctx_grad[part] * linv_s[i % early * HEADS + g * HEADS_GROUP + h]).astype(BF16)
                bwd[slot, h * HEAD_DIM : (h + 1) * HEAD_DIM, :] = grad
                middle_s[i * HEADS + g * HEADS_GROUP + h] = channel_sum(grad.astype(F32) * ctx[part].astype(F32))
            bwd[slot, WIDTH:BWD_ROWS, :] = hidden_grad_s[rows_of(g), :]
            bwd_save(slot, i, g).start()

        @pl.when(i > 0)
        def _():
            for g in range(GROUPS):
                bwd_save(g, 0, 0).wait()

        for g in range(GROUPS):
            mix_back(g)

    each(2 * early, prepare)
    each(count, sequence)
    for slot in range(2):
        fwd_save(slot, 0, 0).wait()
    for slot in range(GROUPS):
        bwd_save(slot, 0, 0).wait()

    def unit_of(u):
        return u % count, GROUPS - 1 - u // count

    def load(u):
        i, j = unit_of(u)
        g = flip(me, j)
        fwd_load(u % 2, i, g).start()
        bwd_load(u % 2, i, g).start()

    def send_dx(i, j):
        to = flip(me, j)
        return remote(x.at[i, to], dx_out.at[me * count + i], s_dx.at[i, j], r_dx.at[i, j], to)

    def own_dx(i):
        return pltpu.make_async_copy(x.at[i, me], dx_out.at[me * count + i], s_dx.at[i, 0])

    def when(condition, body):
        if condition is True:
            body()
        else:
            pl.when(condition)(body)

    depth = size // 2
    level = row // 2
    owners = all_l.shape[1]
    per_half = owners // 2
    cut = WIDTH // 2 // per_half
    pair_groups = (flip(me, 1), flip(me, 3))
    kept = (me, flip(me, 2))
    outs = (up_out, down_out, None)

    def peers(n, body):
        def run(k):
            body(k + 1)

        each(n - 1, run)

    def along(kind, src, dst, k, sided):
        to = (level + k) % depth * 2 + half if sided else (row + k) % size
        return pltpu.make_async_remote_copy(
            src_ref=src, dst_ref=dst, send_sem=s_row.at[kind, k], recv_sem=r_row.at[kind, k],
            device_id={"rows": to}, device_id_type=MESH,
        )

    def line(sided):
        return (depth, level) if sided else (size, row)

    def capped(at, n, length):
        return at if n == length else jnp.clip(at - (length - n) // 2, 0, n - 1)

    def owns(at, n, length):
        first = (length - n) // 2
        return True if n == length else (at >= first) & (at < first + n)

    def scatter(kind, parts, landing, sided, act):
        n = parts.shape[0]
        length, here = line(sided)

        def one(k):
            to = (here + k) % length
            piece = parts.at[capped(to, n, length)]
            when(owns(to, n, length), lambda: act(along(kind, piece, landing.at[k], k, sided)))

        peers(length, one)

    def scatter_got(kind, parts, landing, sided):
        peers(line(sided)[0], lambda k: along(kind, parts.at[0], landing.at[k], k, sided).wait_recv())

    def spread_out(kind, landing, sided, act):
        n = landing.shape[0]
        length, here = line(sided)
        own = landing.at[capped(here, n, length)]
        when(owns(here, n, length), lambda: peers(length, lambda k: act(along(kind, own, own, k, sided))))

    def spread_got(kind, landing, sided):
        n = landing.shape[0]
        length, here = line(sided)
        peers(
            length,
            lambda k: when(
                owns((here + length - k) % length, n, length),
                lambda: along(kind, landing.at[0], landing.at[0], k, sided).wait_recv(),
            ),
        )

    def start(copy):
        copy.start()

    def sent(copy):
        copy.wait_send()

    def pair_copy(b):
        return across(b, pair_t.at[b], pair_l.at[b], 1)

    def side_copy(b):
        return aside(3 + b, side_t.at[b], side_l.at[b])

    def far_copy(b):
        return across(6 + b, far_t.at[b], far_l.at[b], 2)

    def out_copy(b, rows):
        return aside(9 + b, outs[b].at[rows], outs[b].at[rows])

    def pair_send(b):
        for at in range(2):
            pair_t[b, at] = acc[b, pair_groups[at]].astype(BF16)
        pair_copy(b).start()

    def side_send(b):
        pair_copy(b).wait_recv()
        for at in range(2):
            acc[b, kept[at]] += pair_l[b, at].astype(F32)
            side_t[b, at] = acc[b, kept[at], other_half, :].astype(BF16)
        side_copy(b).start()

    def far_send(b):
        side_copy(b).wait_recv()
        acc[b, me, mine_half, :] += side_l[b, 0].astype(F32)
        far_t[b] = (acc[b, kept[1], mine_half, :] + side_l[b, 1].astype(F32)).astype(BF16)
        far_copy(b).start()

    def cut_send(b):
        far_copy(b).wait_recv()
        total = acc[b, me, mine_half, :] + far_l[b].astype(F32)
        for o in range(owners):
            rows = o % per_half * cut
            lanes = o // per_half * HALF
            cut_t[b, o] = total[rows : rows + cut, lanes : lanes + HALF].astype(BF16)
        scatter(b, cut_t.at[b], cut_l.at[b], True, start)

    def all_send(b):
        def close():
            scatter_got(b, cut_t.at[b], cut_l.at[b], True)
            own = capped(level, owners, depth)
            total = cut_t[b, own].astype(F32)
            for k in range(1, depth):
                total = total + cut_l[b, k].astype(F32)
            all_l[b, own] = total.astype(BF16)

        when(owns(level, owners, depth), close)
        spread_out(3 + b, all_l.at[b], True, start)

    def joined(b):
        spread_got(3 + b, all_l.at[b], True)
        sides = [
            jnp.concatenate([all_l[b, side * per_half + o] for o in range(per_half)]) for side in range(2)
        ]
        return jnp.concatenate(sides, axis=1)

    def out_send(b):
        outs[b][mine_half, :] = joined(b)
        out_copy(b, mine_half).start()

    def mix_part(g, rows):
        return mix_out.at[g, rows]

    def mix_far(g):
        return across(12, mix_part(g, mine_half), mix_part(g, mine_half), 2)

    def mix_beside(at, rows):
        return aside(13 + at, mix_part(kept[at], rows), mix_part(kept[at], rows))

    def mix_core(at, g):
        return across(15 + at, mix_out.at[g], mix_out.at[g], 1)

    def mix_far_send():
        mix_out[me, mine_half, :] = joined(2)
        mix_far(me).start()
        mix_beside(0, mine_half).start()

    def mix_beside_send():
        mix_far(flip(me, 2)).wait_recv()
        mix_beside(1, mine_half).start()

    def mix_core_send():
        for at in range(2):
            mix_beside(at, other_half).wait_recv()
            mix_core(at, kept[at]).start()

    def early_copy(j):
        return across(17 + j, sum_t.at[flip(me, j)], sum_l.at[j], j)

    def shared_copy(j):
        return across(20 + j, shared_out.at[me], shared_out.at[me], j)

    def end_copy(j):
        return across(23 + j, end_t.at[j], end_l.at[j], j)

    def lane_rows(g, columns):
        return [jnp.sum(vec[lane_col(g, c)].T, axis=0, keepdims=True) for c in columns]

    def early_send():
        for g in range(GROUPS):
            zeros = [jnp.zeros((1, WIDTH), F32)] * 2
            up = [up_sum[g, 0:1, c * WIDTH : (c + 1) * WIDTH] for c in range(PARTS)]
            rows = zeros + up + lane_rows(g, range(DOWN_BIAS, COLS)) + zeros * ((TABLE - COLS) // 2)
            sum_t[g] = jnp.concatenate(rows)
        for j in range(1, GROUPS):
            early_copy(j).start()

    def early_row_send():
        total = sum_t[me]
        for j in range(1, GROUPS):
            early_copy(j).wait_recv()
            total = total + sum_l[j]
        sum_row_t[...] = total
        peers(size, lambda k: along(8, sum_row_t, sum_row_l.at[k], k, False).start())

    def shared_send():
        total = sum_row_t[...]
        peers(size, lambda k: along(8, sum_row_t, sum_row_l.at[k], k, False).wait_recv())
        for k in range(1, size):
            total = total + sum_row_l[k]
        sums_out[...] = total
        shared_out[me] = total
        for j in range(1, GROUPS):
            shared_copy(j).start()

    qowners = qall_l.shape[0]
    qcut = WIDTH // qowners

    def qpair_copy(at):
        return across(27 + at, qpair_t.at[at], qpair_l.at[at], 1)

    def qpiece_copy():
        return across(29, qpiece_t, qpiece_l, 2)

    def qpair_send(at, j):
        qpair_t[at] = g_qkv[flip(me, j)].astype(BF16)
        qpair_copy(at).start()

    def qpieces(at, g, parts, landing, kind):
        qpair_copy(at).wait_recv()
        for o in range(qowners):
            rows = slice(o * qcut, (o + 1) * qcut)
            parts[o] = (g_qkv[g, rows, :] + qpair_l[at, rows, :].astype(F32)).astype(BF16)
        scatter(kind, parts, landing, False, start)

    def qtotal(parts, landing, kind):
        scatter_got(kind, parts, landing, False)
        total = parts[capped(row, qowners, size)].astype(F32)
        for k in range(1, size):
            total = total + landing[k].astype(F32)
        return total

    def qfar_send():
        qpieces(0, flip(me, 2), qfar_t, qfar_l, 6)

    def qpiece_send():
        def close():
            qpiece_t[...] = qtotal(qfar_t, qfar_l, 6).astype(BF16)
            qpiece_copy().start()

        when(owns(row, qowners, size), close)

    def end_sums(g):
        return jnp.concatenate(lane_rows(g, (Q_BIAS, V_BIAS)) + [jnp.zeros((6, WIDTH), F32)])

    def qcut_send():
        qpieces(1, me, qcut_t, qcut_l, 7)
        sums = end_sums(me)
        for j in range(1, GROUPS):
            end_copy(j).wait_recv()
            sums = sums + end_l[j]
        end_row_t[...] = sums
        peers(size, lambda k: along(9, end_row_t, end_row_l.at[k], k, False).start())

    def qall_send():
        def close():
            total = qtotal(qcut_t, qcut_l, 7)
            qpiece_copy().wait_recv()
            qall_l[capped(row, qowners, size)] = (total + qpiece_l[...].astype(F32)).astype(BF16)

        when(owns(row, qowners, size), close)
        spread_out(10, qall_l, False, start)

    def qclose():
        peers(size, lambda k: along(9, end_row_t, end_row_l.at[k], k, False).wait_recv())
        sums = end_row_t[...]
        for k in range(1, size):
            sums = sums + end_row_l[k]
        sums_out[0:2, :] = sums[0:2]
        spread_got(10, qall_l, False)
        for o in range(qowners):
            qkv_out[o * qcut : (o + 1) * qcut, :] = qall_l[o]

    UP, DOWN, MIX = 0, 1, 2
    plan = {
        1: [lambda: side_send(MIX), early_row_send],
        2: [lambda: side_send(UP)],
        4: [lambda: qpair_send(0, 3), lambda: side_send(DOWN)],
        5: [lambda: far_send(MIX), shared_send],
        6: [lambda: far_send(UP)],
        7: [lambda: cut_send(MIX)],
        8: [qfar_send],
        9: [lambda: cut_send(UP), lambda: far_send(DOWN)],
        10: [lambda: all_send(MIX)],
        11: [lambda: cut_send(DOWN)],
        12: [lambda: qpair_send(1, 1), lambda: all_send(UP), mix_far_send],
        13: [qpiece_send],
        14: [lambda: all_send(DOWN), lambda: out_send(UP)],
    }

    def follow(u):
        for at, steps in plan.items():

            @pl.when(u == count * GROUPS * at // 16 - 1)
            def _():
                for step in steps:
                    step()

    load(0)
    for b in (MIX, UP, DOWN):
        pair_send(b)
    early_send()

    def unit(u):
        i, j = unit_of(u)
        g = flip(me, j)
        slot = u % 2
        fwd_load(slot, i, g).wait()
        bwd_load(slot, i, g).wait()

        @pl.when(u + 1 < count * GROUPS)
        def _():
            load(u + 1)

        for h in range(HEADS_GROUP):
            e = fwd[slot, E_AT + h * SEQ_LEN : E_AT + (h + 1) * SEQ_LEN, :]
            q = fwd[slot, Q_AT + h * PAD : Q_AT + h * PAD + HEAD_DIM, :]
            k = fwd[slot, K_AT + h * PAD : K_AT + h * PAD + HEAD_DIM, :]
            v = fwd[slot, V_AT + h * HEAD_DIM : V_AT + (h + 1) * HEAD_DIM, :]
            grad = bwd[slot, h * HEAD_DIM : (h + 1) * HEAD_DIM, :]
            prob_grad = tn(v, grad)
            score_grad = (e.astype(F32) * (prob_grad - middle_s[i * HEADS + g * HEADS_GROUP + h])).astype(BF16)
            at = h * HEAD_DIM
            act_s[0, 2 * WIDTH + at : 2 * WIDTH + at + HEAD_DIM, :] = nt(grad, e).astype(BF16)
            act_s[0, at : at + HEAD_DIM, :] = (nn(k, score_grad) * SCALE).astype(BF16)
            act_s[0, WIDTH + at : WIDTH + at + HEAD_DIM, :] = nt(q, score_grad).astype(BF16)
        g_qkv[g] += nt(x[i, g], act_s[0, 0:QKV, :])
        add_sum(g, Q_BIAS, act_s[0, 0:WIDTH, :].astype(F32))
        add_sum(g, V_BIAS, act_s[0, 2 * WIDTH : QKV, :].astype(F32))
        into = bwd[slot, WIDTH:BWD_ROWS, :].astype(F32) + nn(wqkv[g], act_s[0, 0:QKV, :])
        x[i, g] = into.astype(BF16)

        @pl.when((j > 0) & (i == count - 1))
        def _():
            end_t[j] = end_sums(g)
            end_copy(j).start()

        @pl.when(j == 1)
        def _():
            send_dx(i, 1).start()

        @pl.when(u % 2 == 1)
        def _():
            late_i, late_j = unit_of(u // 2)
            send_dx(late_i, late_j).start()

        @pl.when(j == 0)
        def _():
            own_dx(i).start()

        follow(u)

    each(count * GROUPS, unit)
    qcut_send()
    mix_beside_send()
    qall_send()
    out_send(DOWN)
    mix_core_send()
    for j in range(1, GROUPS):
        block = shared_out.at[flip(me, j)]
        across(20 + j, block, block, j).wait_recv()
    for b in (UP, DOWN):
        out_copy(b, other_half).wait_recv()
    for at, j in enumerate((1, 3)):
        mix_core(at, flip(me, j)).wait_recv()
    qclose()

    for j in range(1, GROUPS):
        send_table(j).wait_send()
        for k in range(1, 4):
            send_weight(k, j).wait_send()
    for k in range(2, 4):
        pass_weight(k, mine_half).wait_send()
    own_lo(count - 1).wait()
    for j in range(1, GROUPS):
        send_lo(count - 1, j).wait_send()

    def drain(i):
        own_dx(i).wait()
        for j in range(1, GROUPS):
            move_in(x_in, x, s_x, r_x, i, j).wait_send()
            move_in(dy_in, dy, s_dy, r_dy, i, j).wait_send()
            send_lo(i, j).wait_recv()
            send_dx(i, j).wait_send()
            send_dx(i, j).wait_recv()

    each(count, drain)
    for b in range(BLOCKS):
        pair_copy(b).wait_send()
        side_copy(b).wait_send()
        scatter(b, cut_t.at[b], cut_l.at[b], True, sent)
        far_copy(b).wait_send()
        spread_out(3 + b, all_l.at[b], True, sent)
    for b in (UP, DOWN):
        out_copy(b, mine_half).wait_send()
    mix_far(me).wait_send()
    for at in range(2):
        mix_beside(at, mine_half).wait_send()
        mix_core(at, kept[at]).wait_send()
        qpair_copy(at).wait_send()
    when(owns(row, qowners, size), lambda: qpiece_copy().wait_send())
    for j in range(1, GROUPS):
        early_copy(j).wait_send()
        shared_copy(j).wait_send()
        end_copy(j).wait_send()
    scatter(6, qfar_t, qfar_l, False, sent)
    scatter(7, qcut_t, qcut_l, False, sent)
    spread_out(10, qall_l, False, sent)
    peers(size, lambda k: along(8, sum_row_t, sum_row_l.at[k], k, False).wait_send())
    peers(size, lambda k: along(9, end_row_t, end_row_l.at[k], k, False).wait_send())


def layer(size, x, dy, *rest):
    count = x.shape[0] // GROUPS
    here = pl.BlockSpec(memory_space=pl.ANY)
    vmem = pl.BlockSpec(memory_space=pltpu.VMEM)
    grads = [
        ((WIDTH, QKV), BF16),
        ((WIDTH, UNITS), BF16),
        ((WIDTH, UNITS), BF16),
        ((GROUPS, WIDTH, UNITS), BF16),
        ((TABLE, WIDTH), F32),
        ((GROUPS, TABLE, WIDTH), F32),
    ]
    early = min(count, EARLY)
    depth = size // 2
    owners = 2 * owners_of(depth // 2, WIDTH // 32)
    piece = (WIDTH // owners, HALF)
    qowners = owners_of(size, WIDTH // 16)
    qpiece = (WIDTH // qowners, QKV)
    token = (GROUPS, WIDTH, SEQ_LEN)
    dma = pltpu.SemaphoreType.DMA
    return pl.pallas_call(
        functools.partial(layer_kernel, size),
        out_shape=[jax.ShapeDtypeStruct(x.shape, BF16)] * 2
        + [
            jax.ShapeDtypeStruct((count, GROUPS, FWD_ROWS, SEQ_LEN), BF16),
            jax.ShapeDtypeStruct((count, GROUPS, BWD_ROWS, SEQ_LEN), BF16),
        ]
        + [jax.ShapeDtypeStruct(s, t) for s, t in grads],
        in_specs=[here, here, vmem, here, here, here] + [vmem] * 9,
        out_specs=[here] * 4 + [vmem] * len(grads),
        scratch_shapes=[
            pltpu.VMEM((count,) + token, BF16),
            pltpu.VMEM((count,) + token, BF16),
            pltpu.VMEM((GROUPS, WIDTH, QKV), BF16),
            pltpu.VMEM((GROUPS, WIDTH, UNITS), BF16),
            pltpu.VMEM((GROUPS, WIDTH, UNITS), BF16),
            pltpu.VMEM((GROUPS, TABLE, WIDTH), F32),
            pltpu.VMEM((GROUPS, WIDTH, 128), F32),
            pltpu.VMEM((GROUPS, QKV, WIDTH), BF16),
            pltpu.VMEM((GROUPS, UNITS, WIDTH), BF16),
            pltpu.VMEM((GROUPS, UNITS, WIDTH), BF16),
            pltpu.VMEM((D, D), BF16),
            pltpu.VMEM((GROUPS * LANE_COLS, WIDTH, 128), F32),
            pltpu.VMEM((GROUPS, 8, UNITS), F32),
            pltpu.VMEM((2, FWD_ROWS, SEQ_LEN), BF16),
            pltpu.VMEM((GROUPS, BWD_ROWS, SEQ_LEN), BF16),
            pltpu.VMEM((count * HEADS, 1, SEQ_LEN), F32),
            pltpu.VMEM((early * HEADS, 1, SEQ_LEN), F32),
            pltpu.VMEM((early, D, SEQ_LEN), BF16),
            pltpu.VMEM(token, F32),
            pltpu.VMEM((GROUPS, WIDTH + 16, SEQ_LEN), BF16),
            pltpu.VMEM((GROUPS, UNITS, SEQ_LEN), BF16),
            pltpu.VMEM((GROUPS, UNITS, SEQ_LEN), BF16),
            pltpu.VMEM(token, F32),
            pltpu.VMEM((UNITS, SEQ_LEN), BF16),
            pltpu.VMEM((D, SEQ_LEN), BF16),
            pltpu.VMEM(token, BF16),
            pltpu.VMEM((BLOCKS, GROUPS, WIDTH, UNITS), F32),
            pltpu.VMEM((GROUPS, WIDTH, QKV), F32),
            pltpu.VMEM((BLOCKS, 2, WIDTH, UNITS), BF16),
            pltpu.VMEM((BLOCKS, 2, WIDTH, UNITS), BF16),
            pltpu.VMEM((BLOCKS, 2, WIDTH // 2, UNITS), BF16),
            pltpu.VMEM((BLOCKS, 2, WIDTH // 2, UNITS), BF16),
            pltpu.VMEM((BLOCKS, owners) + piece, BF16),
            pltpu.VMEM((BLOCKS, depth) + piece, BF16),
            pltpu.VMEM((BLOCKS, WIDTH // 2, UNITS), BF16),
            pltpu.VMEM((BLOCKS, WIDTH // 2, UNITS), BF16),
            pltpu.VMEM((BLOCKS, owners) + piece, BF16),
            pltpu.VMEM((2, WIDTH, QKV), BF16),
            pltpu.VMEM((2, WIDTH, QKV), BF16),
            pltpu.VMEM((qowners,) + qpiece, BF16),
            pltpu.VMEM((size,) + qpiece, BF16),
            pltpu.VMEM(qpiece, BF16),
            pltpu.VMEM(qpiece, BF16),
            pltpu.VMEM((qowners,) + qpiece, BF16),
            pltpu.VMEM((size,) + qpiece, BF16),
            pltpu.VMEM((qowners,) + qpiece, BF16),
            pltpu.VMEM((GROUPS, TABLE, WIDTH), F32),
            pltpu.VMEM((GROUPS, TABLE, WIDTH), F32),
            pltpu.VMEM((TABLE, WIDTH), F32),
            pltpu.VMEM((size, TABLE, WIDTH), F32),
            pltpu.VMEM((GROUPS, 8, WIDTH), F32),
            pltpu.VMEM((GROUPS, 8, WIDTH), F32),
            pltpu.VMEM((8, WIDTH), F32),
            pltpu.VMEM((size, 8, WIDTH), F32),
        ]
        + [dma((count, GROUPS))] * 8
        + [dma((4, GROUPS))] * 2
        + [dma((34,))] * 2
        + [dma((11, size))] * 2
        + [dma((2,)), dma((GROUPS,))],
        compiler_params=pltpu.CompilerParams(
            vmem_limit_bytes=(64 << 20) - (1 << 17), collective_id=0, has_side_effects=True
        ),
    )(x, dy, *rest)


def local(
    size, layer_input, segment_ids, qkv_weight, qv_bias, out_weight, out_bias, gain_one, shift_one,
    up_weight, up_bias, down_weight, down_bias, gain_two, shift_two, out_grad,
):
    lo, dx, _, _, *grads = layer(
        size, layer_input, out_grad, segment_ids, qkv_weight, up_weight, down_weight, out_weight,
        qv_bias, up_bias, down_bias, gain_two, shift_two, out_bias, gain_one, shift_one,
    )
    lo, dx, g_qkv, g_up, g_down, g_out, qv, out_b, gain1, shift1, up_b, down_b, gain2, shift2 = widen(lo, dx, *grads)
    return lo, dx, g_qkv, qv, g_out, out_b, gain1, shift1, g_up, up_b, g_down, down_b, gain2, shift2


def widen_kernel(
    lo, dx, qkv, up, down, mix, sums, shared,
    lo_o, dx_o, qkv_o, up_o, down_o, mix_o, qv_o, out_o, gain1_o, shift1_o, up_b_o, down_b_o, gain2_o, shift2_o,
):
    for src, out in ((lo, lo_o), (dx, dx_o), (qkv, qkv_o), (up, up_o), (down, down_o), (mix, mix_o)):
        out[...] = src[...].astype(F32).reshape(out.shape)

    @pl.when(pl.program_id(0) == 0)
    def _():
        def own(first, n):
            return jnp.concatenate([sums[first + c : first + c + 1, :] for c in range(n)], axis=1)

        def joint(at):
            return jnp.concatenate([shared[g, at : at + 1, :] for g in range(GROUPS)], axis=1)

        qv_o[...] = own(Q_BIAS, 2)
        up_b_o[...] = own(UP_BIAS, PARTS)
        down_b_o[...] = own(DOWN_BIAS, 1)
        gain2_o[...] = own(GAIN_TWO, 1).reshape(WIDTH)
        shift2_o[...] = own(SHIFT_TWO, 1).reshape(WIDTH)
        for out, at in ((out_o, OUT_BIAS), (gain1_o, GAIN_ONE), (shift1_o, SHIFT_ONE)):
            out[...] = joint(at).reshape(D)


def widen(lo, dx, *grads):
    steps = 4
    part = WIDTH // steps
    data = pl.BlockSpec((lo.shape[0] // steps, WIDTH, SEQ_LEN), lambda i: (i, 0, 0))

    def slab(columns):
        return pl.BlockSpec((part, columns), lambda i: (i, 0)), pl.BlockSpec((1, part, columns), lambda i: (0, i, 0))

    def whole(shape):
        return pl.BlockSpec(shape, lambda i: (0,) * len(shape), pipeline_mode=pl.Buffered(1))

    qkv_in, qkv_out = slab(QKV)
    unit_in, unit_out = slab(UNITS)
    mix_in = pl.BlockSpec((1, D // steps, D), lambda i: (i, 0, 0))
    mix_out = pl.BlockSpec((D // steps, D), lambda i: (i, 0))
    wide = [(1, WIDTH, QKV), (1, WIDTH, UNITS), (1, WIDTH, UNITS), (D, D)]
    vectors = [(1, 2 * WIDTH), (D,), (D,), (D,), (1, UNITS), (1, WIDTH), (WIDTH,), (WIDTH,)]
    return pl.pallas_call(
        widen_kernel,
        grid=(steps,),
        out_shape=[jax.ShapeDtypeStruct(s, F32) for s in [lo.shape, dx.shape] + wide + vectors],
        in_specs=[data, data, qkv_in, unit_in, unit_in, mix_in] + [whole(a.shape) for a in grads[4:]],
        out_specs=[data, data, qkv_out, unit_out, unit_out, mix_out] + [whole(s) for s in vectors],
        compiler_params=pltpu.CompilerParams(vmem_limit_bytes=62 << 20),
    )(lo, dx, *grads)


def solution(mesh):
    group = P("grp", None, None)
    data = P("rows", "grp", None)
    in_specs = (
        data, P("rows", None), group, P("grp", None), P(), P(), P(), P(),
        group, P("grp", None), group, P("grp", None), P("grp"), P("grp"), data,
    )
    out_specs = (
        data, data, group, P("grp", None), P(), P(), P(), P(),
        group, P("grp", None), group, P("grp", None), P("grp"), P("grp"),
    )
    return jax.shard_map(functools.partial(local, mesh.shape["rows"]), mesh=mesh, in_specs=in_specs, out_specs=out_specs, check_vma=False)
```
